128 devices in a mesh: gx: 8 (over x, core), gy: 4 (over z), gz: 4 (over y).
Axes of the slice: x: 4, y: 4, z: 4, core: 2. Of those that a mesh axis runs over, the one named last changes fastest.
Arguments:
- velocity: float32 [3, 256, 256, 512], P(None, 'gx', 'gy', 'gz'), may hold values from -12 to 12
- inv_density: float32 [256, 256, 512], P('gx', 'gy', 'gz'), may hold values from 0.2 to 5
- factor_x: float32 [256, 64], P('gx'), may hold values from -0.5 to 0.5
- factor_y: float32 [256, 64], P('gy'), may hold values from -0.5 to 0.5
- factor_z: float32 [512, 64], P('gz'), may hold values from -0.375 to 0.375
Outputs:
- pressure: float32 [256, 256, 512], P('gx', 'gy', 'gz')
- corrected: float32 [3, 256, 256, 512], P(None, 'gx', 'gy', 'gz')
- core: float32 [64, 4, 64, 64], P('gx', None, 'gy', 'gz')
The draws below stay inside these ranges and needn't reach their ends.
All inputs are finite; a program needn't handle non-finite values.
Results may differ from the reference program's by a relative error of at most 0.00013.
Values sent between devices are 32-bit elements; how exact they have to be, the bound alone decides.
A program may use at most 128 MiB of HBM per device.

```python
import math
import jax
import jax.numpy as jnp
from jax import lax

RANK = 64
ITERS = 4
NX = 256
NY = 256
NZ = 512


def draw_velocity(key, part):
    position = jnp.arange(NX, dtype=jnp.float32) / NX
    ramp = (1.0 + 2.0 * position)[None, :, None, None]
    rough = jnp.clip(jax.random.normal(key, (3, NX, NY, NZ), jnp.float32), -4.0, 4.0)
    return ramp * rough


def strengthened(values, stream_key, source, target, shards_of, factor):
    def block_of(dim):
        return (jnp.arange(values.shape[dim]) // (values.shape[dim] // shards_of)).reshape((-1,) + (1,) * (values.ndim - 1 - dim))

    near = jax.random.permutation(stream_key, shards_of)[block_of(target)]
    second = (block_of(target) + shards_of // 2) % shards_of
    return jnp.where((block_of(source) == near) | (block_of(source) == second), factor * values, values)


def block_levels(stream_key, dims, cuts, low, largest):
    gain, own = 1.0, jax.random.fold_in(stream_key, 6)
    for dim, blocks in cuts:
        heights = jnp.exp(jax.random.uniform(jax.random.fold_in(own, dim), (blocks,), jnp.float32, low / len(cuts), largest / len(cuts)))
        gain = gain * jnp.repeat(heights, dims[dim] // blocks).reshape([-1 if axis == dim else 1 for axis in range(len(dims))])
    return gain


def bell_draw_with(own_key, extent, scale, bound, pieces, heavy, kind=jnp.bfloat16):
    values = scale * jax.random.normal(own_key, extent, jnp.float32)
    if pieces:
        values = values * block_levels(own_key, extent, pieces, -0.22, 0.18)
    return jnp.clip(strengthened(values, jax.random.fold_in(own_key, 3), *heavy), -bound, bound).astype(kind)


def setup_inputs(seed: int = 0) -> dict:
    keys = jax.random.split(jax.random.key(seed), 6)
    return {
        "velocity": draw_velocity(jax.random.fold_in(keys[5], 71), 0),
        "inv_density": jnp.clip(jnp.exp(math.log(5.0) - 3.218876 * jax.random.uniform(keys[1], (NX, NY, NZ), jnp.float32) ** block_levels(keys[1], (NX, NY, NZ), ((0, 8), (1, 4), (2, 4)), -0.2, 0.2)), 0.2, 5.0),
        "factor_x": bell_draw_with(keys[2], (NX, RANK), NX ** -0.5, 0.5, ((0, 8),), (0, 1, 8, 2.0), jnp.float32),
        "factor_y": bell_draw_with(keys[3], (NY, RANK), NY ** -0.5, 0.5, ((0, 4),), (0, 1, 4, 2.0), jnp.float32),
        "factor_z": bell_draw_with(keys[4], (NZ, RANK), NZ ** -0.5, 0.375, ((0, 4),), (0, 1, 4, 2.0), jnp.float32),
    }


SHIFT = 0.1
HIGHEST = lax.Precision.HIGHEST


def neighbours(padded):
    centre_cut = (slice(None),) + (slice(1, -1),) * 3
    result = []
    for dimension in range(1, 4):
        forward = list(centre_cut)
        forward[dimension] = slice(2, None)
        backward = list(centre_cut)
        backward[dimension] = slice(None, -2)
        result.append((padded[tuple(forward)], padded[tuple(backward)]))
    return result


def pad_cells(stack):
    return jnp.pad(stack, ((0, 0), (1, 1), (1, 1), (1, 1)))


def assemble(sides, inv_density):
    couplings = []
    diagonal = SHIFT + jnp.zeros_like(inv_density)
    divergence = jnp.zeros_like(inv_density)
    for dimension in range(3):
        forward, backward = sides[dimension]
        c_forward = 0.5 * (inv_density + forward[3])
        c_backward = 0.5 * (inv_density + backward[3])
        couplings.append((c_forward, c_backward))
        diagonal = diagonal + c_forward + c_backward
        divergence = divergence + 0.5 * (forward[dimension] - backward[dimension])
    return couplings, diagonal, -divergence


def apply_operator(sides, field, couplings, diagonal):
    result = diagonal * field
    for dimension in range(3):
        forward, backward = sides[dimension]
        result = result - couplings[dimension][0] * forward[0] - couplings[dimension][1] * backward[0]
    return result


def correct(sides, velocity, inv_density):
    parts = []
    for dimension in range(3):
        gradient = 0.5 * (sides[dimension][0][0] - sides[dimension][1][0])
        parts.append(velocity[dimension] - inv_density * gradient)
    return jnp.stack(parts, 0)


def reference(velocity, inv_density, factor_x, factor_y, factor_z):
    sides = neighbours(pad_cells(jnp.concatenate([velocity, inv_density[None]], 0)))
    couplings, diagonal, rhs = assemble(sides, inv_density)

    def operate(field):
        return apply_operator(neighbours(pad_cells(field[None])), field, couplings, diagonal)

    pressure = jnp.zeros_like(rhs)
    residual = rhs
    precond = residual / diagonal
    direction = precond
    product = jnp.sum(residual * precond)
    for iteration in range(ITERS):
        image = operate(direction)
        alpha = product / jnp.sum(direction * image)
        pressure = pressure + alpha * direction
        residual = residual - alpha * image
        precond = residual / diagonal
        fresh = jnp.sum(residual * precond)
        direction = precond + (fresh / product) * direction
        product = fresh
    corrected = correct(neighbours(pad_cells(pressure[None])), velocity, inv_density)
    fields = jnp.concatenate([corrected, pressure[None]], 0)
    first = jnp.einsum("fijk,ia->afjk", fields, factor_x, precision=HIGHEST)
    second = jnp.einsum("afjk,jb->afbk", first, factor_y, precision=HIGHEST)
    core = jnp.einsum("afbk,kc->afbc", second, factor_z, precision=HIGHEST)
    return pressure, corrected, core
```

```python
import jax
import jax.numpy as jnp
from jax import lax
from jax.experimental import pallas as pl
from jax.experimental.pallas import tpu as pltpu
from jax.sharding import PartitionSpec as P

ITERS = 4
SHIFT = 0.1
MESH = pl.DeviceIdType.MESH
F32 = jnp.float32
BF16 = jnp.bfloat16
NI, NJ, NK = 32, 64, 128
TOP = 8
AXES = ("gx", "gy", "gz")
SIZES = (8, 4, 4)
PLANE = [(dy, dz) for dy in range(4) for dz in range(4) if dy or dz]
ROUTES = {3: ("gz", 1), 1: ("gy", 1), 0: ("gz", -1), 2: ("gy", -1)}
ORDER = (3, 1, 0, 2)
TINY = 1e-11


def two_sum(a, b):
    s = a + b
    t = s - a
    return s, (a - (s - t)) + (b - t)


def quick(a, b):
    s = a + b
    return s, b - (s - a)


def df_add(x, y):
    s, e = two_sum(x[0], y[0])
    return quick(s, e + (x[1] + y[1]))


def df_neg(x):
    return -x[0], -x[1]


def halves(a):
    t = 4097.0 * a
    h = t - (t - a)
    return h, a - h


def df_mul(x, y):
    p = x[0] * y[0]
    ah, al = halves(x[0])
    bh, bl = halves(y[0])
    e = ((ah * bh - p) + ah * bl + al * bh) + al * bl
    return quick(p, e + (x[0] * y[1] + x[1] * y[0]))


def df_recip(x):
    r = 1.0 / x[0]
    one = (jnp.ones_like(r), jnp.zeros_like(r))
    two = (jnp.full_like(r, 2.0), jnp.zeros_like(r))
    y = (r, jnp.zeros_like(r))
    for _ in range(2):
        y = df_mul(y, df_add(two, df_neg(df_mul(x, y))))
    return y


def solve4(nu):
    n = ITERS
    g = [[None] * n for _ in range(n)]
    for i in range(n):
        for j in range(i + 1):
            g[i][j] = df_add(nu[i + j], df_neg(nu[i + j + 1]))
    y = list(nu[:n])
    low = [[None] * n for _ in range(n)]
    inv = []
    for k in range(n):
        pivot = g[k][k]
        start = nu[2 * k][0] - nu[2 * k + 1][0]
        ok = pivot[0] > TINY * start
        safe = (jnp.where(ok, pivot[0], 1.0), jnp.where(ok, pivot[1], 0.0))
        r = df_recip(safe)
        r = (jnp.where(ok, r[0], 0.0), jnp.where(ok, r[1], 0.0))
        inv.append(r)
        for i in range(k + 1, n):
            low[i][k] = df_mul(g[i][k], r)
        for i in range(k + 1, n):
            for j in range(k + 1, i + 1):
                g[i][j] = df_add(g[i][j], df_neg(df_mul(low[i][k], g[j][k])))
            y[i] = df_add(y[i], df_neg(df_mul(low[i][k], y[k])))
    c = [None] * n
    for i in reversed(range(n)):
        v = df_mul(y[i], inv[i])
        for j in range(i + 1, n):
            v = df_add(v, df_neg(df_mul(low[j][i], c[j])))
        c[i] = v
    return [v[0] for v in c]


def lanes(shape):
    return lax.broadcasted_iota(jnp.int32, shape, len(shape) - 1)


def rows(shape):
    return lax.broadcasted_iota(jnp.int32, shape, 0)


def split(x):
    hi = x.astype(BF16)
    return hi, (x - hi.astype(F32)).astype(BF16)


def dot(a, b):
    return lax.dot_general(a, b, (((1,), (0,)), ((), ())), preferred_element_type=F32)


def squeeze_face(face):
    lane = lanes((8, 128))
    halves_ = []
    for h in range(2):
        acc = face[32 * h : 32 * h + 8]
        for q in range(1, 4):
            part = face[32 * h + 8 * q : 32 * h + 8 * q + 8]
            acc = jnp.where(lane // 32 == q, pltpu.roll(part, 32 * q, 1), acc)
        halves_.append(acc)
    return jnp.concatenate(halves_, axis=0)


def spread_face(packed):
    parts = []
    for h in range(2):
        for q in range(4):
            part = packed[8 * h : 8 * h + 8]
            parts.append(part if q == 0 else pltpu.roll(part, 128 - 32 * q, 1))
    return jnp.concatenate(parts, axis=0)


def fold(x):
    t = [x[8 * q : 8 * q + 8] for q in range(8)]
    return ((t[0] + t[1]) + (t[2] + t[3])) + ((t[4] + t[5]) + (t[6] + t[7]))


def kernel(
    vel, inv, fx, fy, fz,
    out_p, out_c, out_core,
    vx, vy, vz, ip, w, cx, cy, cz, dinv, pp, pst, cst,
    ysend, yrecv, zsend, zrecv, ysend0, yrecv0, zsend0, zrecv0,
    a_send, a_recv0, a_recv1,
    wz_hi, wz_lo, fyt, k_hi, k_lo, xh, xl, u,
    za_in, za_acc, za_dir, za_out, ya_in, ya_acc, ya_dir, ya_out,
    b_src_z, b_src_y, b_in, b_acc, b_dir, b_out, ysc, v, v_recv,
    in_sem, out_sem, hs_sem, hr_sem, as_sem, ar_sem, rs_sem, rr_sem, xs_sem, xr_sem,
):
    me = [lax.axis_index(a) for a in AXES]
    has = []
    for a in range(3):
        has += [me[a] > 0, me[a] < SIZES[a] - 1]

    def neighbour(side):
        a = side // 2
        step = 1 if side % 2 else SIZES[a] - 1
        return {AXES[a]: lax.rem(me[a] + step, SIZES[a])}

    def remote(src, dst, ss, rs, dev):
        return pltpu.make_async_remote_copy(
            src_ref=src, dst_ref=dst, send_sem=ss, recv_sem=rs, device_id=dev, device_id_type=MESH
        )

    lane = lanes((NJ, NK))

    loads = [
        pltpu.make_async_copy(inv, ip.at[pl.ds(1, NI), pl.ds(TOP, NJ)], in_sem.at[0]),
        pltpu.make_async_copy(vel.at[2], vz, in_sem.at[1]),
        pltpu.make_async_copy(vel.at[1], vy.at[:, pl.ds(TOP, NJ)], in_sem.at[2]),
        pltpu.make_async_copy(vel.at[0], vx.at[pl.ds(1, NI)], in_sem.at[3]),
    ]
    for c in loads:
        c.start()

    barrier = pltpu.get_barrier_semaphore()
    for o in range(1, 8):
        pl.semaphore_signal(barrier, inc=1, device_id={"gx": lax.rem(me[0] + o, 8)}, device_id_type=MESH)
    for dy, dz in PLANE:
        pl.semaphore_signal(
            barrier, inc=1,
            device_id={"gy": lax.rem(me[1] + dy, 4), "gz": lax.rem(me[2] + dz, 4)},
            device_id_type=MESH,
        )

    zero_plane = jnp.zeros((NJ, NK), F32)
    for s in range(2):
        far = (0, NI + 1)[s]

        @pl.when(jnp.logical_not(has[s]))
        def _():
            vx[far] = zero_plane
            ip[far, pl.ds(TOP, NJ)] = zero_plane
            for k in range(ITERS):
                w[k, far, pl.ds(TOP, NJ)] = zero_plane

        @pl.when(jnp.logical_not(has[2 + s]))
        def _():
            yrecv0[s] = jnp.zeros((2, NI, NK), F32)
            for k in range(ITERS):
                yrecv[k, s] = jnp.zeros((NI, NK), F32)

        @pl.when(jnp.logical_not(has[4 + s]))
        def _():
            zrecv0[s] = jnp.zeros((2, 16, NK), F32)
            for k in range(ITERS):
                zrecv[k, s] = jnp.zeros((16, NK), F32)

    pl.semaphore_wait(barrier, 7 + len(PLANE))

    def halo(r, side, landing):
        near = (1, NI)[side % 2]
        far = (0, NI + 1)[landing % 2]
        s, t = side % 2, landing % 2
        ax = side // 2
        if r == 0:
            if ax == 0:
                edge = (0, NI - 1)[s]
                pairs = [
                    (vel.at[0, edge], vx.at[far]),
                    (inv.at[edge], ip.at[far, pl.ds(TOP, NJ)]),
                ]
            elif ax == 1:
                pairs = [(ysend0.at[s], yrecv0.at[t])]
            else:
                pairs = [(zsend0.at[s], zrecv0.at[t])]
        else:
            k = r - 1
            if ax == 0:
                pairs = [(w.at[k, near, pl.ds(TOP, NJ)], w.at[k, far, pl.ds(TOP, NJ)])]
            elif ax == 1:
                pairs = [(ysend.at[k, s], yrecv.at[k, t])]
            else:
                pairs = [(zsend.at[k, s], zrecv.at[k, t])]
        return [
            remote(a, b, hs_sem.at[r, side, n], hr_sem.at[r, landing, n], neighbour(side))
            for n, (a, b) in enumerate(pairs)
        ]

    def halo_start(r, sides):
        for side in sides:
            @pl.when(has[side])
            def _():
                for c in halo(r, side, side ^ 1):
                    c.start()

    def halo_wait(r, sides):
        for side in sides:
            @pl.when(has[side])
            def _():
                for c in halo(r, side, side):
                    c.wait_recv()

    def halo_sent(r, sides):
        for side in sides:
            @pl.when(has[side])
            def _():
                for c in halo(r, side, side ^ 1):
                    c.wait_send()

    halo_start(0, (0, 1))

    def take(acc, x, i, edge):
        moved = pltpu.roll(x, i if edge == 0 else i + 1, 1)
        return jnp.where(lane == i, moved, acc)

    for c in loads[:3]:
        c.wait()

    def face0(i, carry):
        u0, u1, n0, n1 = carry
        a = vz[i]
        b = ip[i + 1, pl.ds(TOP, NJ)]
        row = pl.ds(i, 1)
        ysend0[0, 0, row] = vy[i, pl.ds(TOP, 1)]
        ysend0[1, 0, row] = vy[i, pl.ds(TOP + NJ - 1, 1)]
        ysend0[0, 1, row] = b[0:1]
        ysend0[1, 1, row] = b[NJ - 1 : NJ]
        return take(u0, a, i, 0), take(u1, a, i, 1), take(n0, b, i, 0), take(n1, b, i, 1)

    u0, u1, n0, n1 = lax.fori_loop(0, NI, face0, (zero_plane,) * 4, unroll=2)
    zsend0[0, 0] = squeeze_face(u0)
    zsend0[1, 0] = squeeze_face(u1)
    zsend0[0, 1] = squeeze_face(n0)
    zsend0[1, 1] = squeeze_face(n1)
    halo_start(0, (2, 3, 4, 5))
    loads[3].wait()

    z64 = jnp.zeros((NK, 64), F32)
    fzp = jnp.concatenate([fz[...], z64], axis=1)
    lane_k = lanes((NK, 128))

    def build_z(i8, _):
        row = pl.ds(pl.multiple_of(i8 * 128, 128), 128)
        for r in range(4):
            moved = pltpu.roll(fzp, lax.rem(16 * i8 + 128 - 16 * r, 128), 1)
            hi, lo = split(jnp.where(lane_k // 16 == i8, moved, 0.0))
            wz_hi[row, pl.ds(128 * r, 128)] = hi
            wz_lo[row, pl.ds(128 * r, 128)] = lo
        return 0

    lax.fori_loop(0, 8, build_z, 0)
    fyp = jnp.concatenate([fy[...], jnp.zeros((NJ, 64), F32)], axis=1)
    hi, lo = split(fyp.T[:64])
    fyt[...] = jnp.concatenate([hi, lo, hi], axis=1)
    fx_hi, fx_lo = split(fx[...])
    rep = (rows((512, NI)) // 16 == lanes((512, NI))).astype(F32).astype(BF16)
    same = (rows((512, 128)) % 16) == (lanes((512, 128)) % 16)

    def build_x(m, _):
        pick = (rows((64, 128)) == 8 * m + lanes((64, 128)) // 16).astype(F32).astype(BF16)
        for part, dst in ((fx_hi, k_hi), (fx_lo, k_lo)):
            wide = dot(part, pick).astype(BF16)
            dst[m] = jnp.where(same, dot(rep, wide), 0.0).astype(BF16)
        return 0

    lax.fori_loop(0, 8, build_x, 0)

    halo_wait(0, range(6))

    def ahead(x, face, i):
        return pltpu.roll(jnp.where(lane == 0, pltpu.roll(face, lax.rem(NK - i, NK), 1), x), NK - 1, 1)

    def behind(x, face, i):
        return pltpu.roll(jnp.where(lane == NK - 1, pltpu.roll(face, NK - 1 - i, 1), x), 1, 1)

    um, up = spread_face(zrecv0[0, 0]), spread_face(zrecv0[1, 0])
    nm, np_ = spread_face(zrecv0[0, 1]), spread_face(zrecv0[1, 1])
    czb = 0.5 * (n0 + nm)
    zero_acc = jnp.zeros((8, NK), F32)

    def accumulate(acc, x):
        s, e = two_sum(acc[0], fold(x))
        return s, acc[1] + e

    def first(i, carry):
        z0, z1, acc = carry
        row = pl.ds(i, 1)
        ip[i + 1, pl.ds(TOP - 1, 1)] = yrecv0[0, 1, row]
        ip[i + 1, pl.ds(TOP + NJ, 1)] = yrecv0[1, 1, row]
        vy[i, pl.ds(TOP - 1, 1)] = yrecv0[0, 0, row]
        vy[i, pl.ds(TOP + NJ, 1)] = yrecv0[1, 0, row]
        n = ip[i + 1, pl.ds(TOP, NJ)]
        xb = 0.5 * (n + ip[i, pl.ds(TOP, NJ)])
        xf = 0.5 * (n + ip[i + 2, pl.ds(TOP, NJ)])
        yb = 0.5 * (n + ip[i + 1, pl.ds(TOP - 1, NJ)])
        yf = 0.5 * (n + ip[i + 1, pl.ds(TOP + 1, NJ)])
        zb = 0.5 * (n + behind(n, nm, i))
        zf = 0.5 * (n + ahead(n, np_, i))
        cx[i] = xb
        cx[i + 1] = xf
        cy[i, pl.ds(TOP, NJ)] = yf
        cy[i, pl.ds(TOP - 1, 1)] = yb[0:1]
        cz[i] = zf
        d = SHIFT + xf + xb + yf + yb + zf + zb
        a = vz[i]
        div = 0.5 * (vx[i + 2] - vx[i])
        div = div + 0.5 * (vy[i, pl.ds(TOP + 1, NJ)] - vy[i, pl.ds(TOP - 1, NJ)])
        div = div + 0.5 * (ahead(a, up, i) - behind(a, um, i))
        b = -div
        di = 1.0 / d
        dinv[i] = di
        w0 = b * di
        w[0, i + 1, pl.ds(TOP, NJ)] = w0
        ysend[0, 0, row] = w0[0:1]
        ysend[0, 1, row] = w0[NJ - 1 : NJ]
        return take(z0, w0, i, 0), take(z1, w0, i, 1), accumulate(acc, b * w0)

    z0, z1, acc = lax.fori_loop(0, NI, first, (zero_plane, zero_plane, (zero_acc, zero_acc)))
    moments = [acc]

    faces = []
    for k in range(ITERS):
        zsend[k, 0] = squeeze_face(z0)
        zsend[k, 1] = squeeze_face(z1)
        halo_start(k + 1, range(6))
        halo_wait(k + 1, range(6))
        wm, wp = spread_face(zrecv[k, 0]), spread_face(zrecv[k, 1])
        flux = czb * wm
        last = k == ITERS - 1

        def step(i, carry):
            z0, z1, odd, even = carry
            row = pl.ds(i, 1)
            w[k, i + 1, pl.ds(TOP - 1, 1)] = yrecv[k, 0, row]
            w[k, i + 1, pl.ds(TOP + NJ, 1)] = yrecv[k, 1, row]
            c = w[k, i + 1, pl.ds(TOP, NJ)]
            f = cz[i]
            bw = cx[i] * w[k, i, pl.ds(TOP, NJ)] + cx[i + 1] * w[k, i + 2, pl.ds(TOP, NJ)]
            bw = bw + cy[i, pl.ds(TOP - 1, NJ)] * w[k, i + 1, pl.ds(TOP - 1, NJ)]
            bw = bw + cy[i, pl.ds(TOP, NJ)] * w[k, i + 1, pl.ds(TOP + 1, NJ)]
            bw = bw + (f * ahead(c, wp, i) + behind(f * c, flux, i))
            odd = accumulate(odd, c * bw)
            if not last:
                nw = bw * dinv[i]
                even = accumulate(even, bw * nw)
                w[k + 1, i + 1, pl.ds(TOP, NJ)] = nw
                ysend[k + 1, 0, row] = nw[0:1]
                ysend[k + 1, 1, row] = nw[NJ - 1 : NJ]
                z0, z1 = take(z0, nw, i, 0), take(z1, nw, i, 1)
            return z0, z1, odd, even

        start = (zero_plane, zero_plane, (zero_acc, zero_acc), (zero_acc, zero_acc))
        z0, z1, odd, even = lax.fori_loop(0, NI, step, start)
        moments.append(odd)
        if not last:
            moments.append(even)

    row8 = rows((8, NK))
    lane8 = lanes((8, NK))
    hi = zero_acc
    lo = zero_acc
    for m, acc in enumerate(moments):
        for shift in (4, 2, 1):
            acc = df_add(acc, (pltpu.roll(acc[0], shift, 0), pltpu.roll(acc[1], shift, 0)))
        hi = jnp.where(row8 == m, acc[0], hi)
        lo = jnp.where(row8 == m, acc[1], lo)
    total = (hi, lo)
    for shift in (64, 32, 16, 8, 4, 2, 1):
        total = df_add(total, (pltpu.roll(total[0], shift, 1), pltpu.roll(total[1], shift, 1)))

    plane_to = [{"gy": lax.rem(me[1] + dy, 4), "gz": lax.rem(me[2] + dz, 4)} for dy, dz in PLANE]
    line_to = [{"gx": lax.rem(me[0] + o, 8)} for o in range(1, 8)]
    for stage, (peers, landing) in enumerate(((plane_to, a_recv0), (line_to, a_recv1))):
        a_send[stage] = jnp.where(lane8 < 64, total[0], total[1])
        copies = [
            remote(a_send.at[stage], landing.at[n], as_sem.at[stage, n], ar_sem.at[stage, n], dev)
            for n, dev in enumerate(peers)
        ]
        for c in copies:
            c.start()
        for c in copies:
            c.wait_recv()
        terms = [total]
        for n in range(len(peers)):
            x = landing[n]
            y = pltpu.roll(x, 64, 1)
            terms.append((jnp.where(lane8 < 64, x, y), jnp.where(lane8 < 64, y, x)))
        while len(terms) > 1:
            terms = [
                df_add(terms[t], terms[t + 1]) if t + 1 < len(terms) else terms[t]
                for t in range(0, len(terms), 2)
            ]
        total = terms[0]
        for c in copies:
            c.wait_send()

    nu = [(total[0][m : m + 1], total[1][m : m + 1]) for m in range(2 * ITERS)]
    coef = solve4(nu)

    def combine(parts):
        total = coef[0] * parts[0]
        for c, x in zip(coef[1:], parts[1:]):
            total = total + c * x
        return total

    pm = combine([spread_face(zrecv[k, 0]) for k in range(ITERS)])
    pf = combine([spread_face(zrecv[k, 1]) for k in range(ITERS)])
    for far in (0, NI + 1):
        pp[far, pl.ds(TOP, NJ)] = combine([w[k, far, pl.ds(TOP, NJ)] for k in range(ITERS)])

    def keep(f, i, x):
        hi, lo = split(x)
        rr = pl.ds(pl.multiple_of((i // 8) * NJ, NJ), NJ)
        cc = pl.ds(pl.multiple_of(lax.rem(i, 8) * NK, NK), NK)
        xh[f, rr, cc] = hi
        xl[f, rr, cc] = lo

    def press(i, _):
        for top, n in ((TOP - 1, 1), (TOP + NJ, 1)):
            pp[i + 1, pl.ds(top, n)] = combine([w[k, i + 1, pl.ds(top, n)] for k in range(ITERS)])
        x = combine([w[k, i + 1, pl.ds(TOP, NJ)] for k in range(ITERS)])
        pp[i + 1, pl.ds(TOP, NJ)] = x
        pst[i] = x
        keep(3, i, x)
        return 0

    lax.fori_loop(0, NI, press, 0)

    def fix(f):
        def body(i, _):
            n = ip[i + 1, pl.ds(TOP, NJ)]
            if f == 0:
                g = pp[i + 2, pl.ds(TOP, NJ)] - pp[i, pl.ds(TOP, NJ)]
                x = vx[i + 1]
            elif f == 1:
                g = pp[i + 1, pl.ds(TOP + 1, NJ)] - pp[i + 1, pl.ds(TOP - 1, NJ)]
                x = vy[i, pl.ds(TOP, NJ)]
            else:
                c = pp[i + 1, pl.ds(TOP, NJ)]
                g = ahead(c, pf, i) - behind(c, pm, i)
                x = vz[i]
            x = x - n * (0.5 * g)
            cst[f, i] = x
            keep(f, i, x)
            return 0

        lax.fori_loop(0, NI, body, 0)

    def ring(axis, way):
        a = AXES.index(axis)
        n = SIZES[a]
        to = lax.rem(me[a] + (n + way), n)
        back = lax.rem(me[a] + (n - way), n)
        opposite = lax.rem(me[a] + 2, n)
        return to, back, opposite

    def rows16(m):
        return pl.ds(pl.multiple_of(m * 16, 16), 16)

    def stage_refs(f, stage):
        axis, way = ROUTES[f]
        slot = 0 if way == 1 else 1
        if stage == 0:
            if axis == "gz":
                return axis, way, (lambda m: u.at[f, m]), za_in.at[slot], za_acc.at[slot], za_dir.at[slot], za_out.at[slot]
            return axis, way, (lambda m: u.at[f, :, :, rows16(m)]), ya_in.at[slot], ya_acc.at[slot], ya_dir.at[slot], ya_out.at[slot]
        other = "gy" if axis == "gz" else "gz"
        if axis == "gz":
            chunk = lambda m: b_src_z.at[slot, :, rows16(m)]
        else:
            chunk = lambda m: b_src_y.at[slot, m]
        return other, way, chunk, b_in.at[f], b_acc.at[f], b_dir.at[f], b_out.at[f]

    def stage_copies(f, stage):
        axis, way, chunk, r_in, r_acc, r_dir, r_out = stage_refs(f, stage)
        to, back, opposite = ring(axis, way)
        sems = lambda n: (rs_sem.at[f, stage, n], rr_sem.at[f, stage, n])
        return (
            remote(chunk(opposite), r_in, *sems(0), {axis: to}),
            remote(chunk(back), r_dir, *sems(1), {axis: back}),
            remote(r_out, r_acc, *sems(2), {axis: to}),
        )

    def stage_open(f, stage):
        far, near, _ = stage_copies(f, stage)
        far.start()
        near.start()

    def stage_relay(f, stage):
        axis, way, chunk, r_in, r_acc, r_dir, r_out = stage_refs(f, stage)
        to, back, opposite = ring(axis, way)
        far, near, relay = stage_copies(f, stage)
        far.wait_recv()
        r_out[...] = r_in[...] + chunk(to)[...]
        relay.start()

    def stage_close(f, stage):
        axis, way, chunk, r_in, r_acc, r_dir, r_out = stage_refs(f, stage)
        far, near, relay = stage_copies(f, stage)
        near.wait_recv()
        relay.wait_recv()
        return chunk(me[AXES.index(axis)])[...] + r_acc[...] + r_dir[...]

    def contract(f):
        wh, wl = wz_hi[...], wz_lo[...]
        a, b = xh[f], xl[f]
        for half in range(2):
            cols = slice(256 * half, 256 * half + 256)
            z = dot(a, wh[:, cols]) + dot(b, wh[:, cols]) + dot(a, wl[:, cols])
            for g in range(4):
                hi, lo = split(z[NJ * g : NJ * g + NJ])
                y = dot(fyt[...], jnp.concatenate([hi, hi, lo], axis=0))
                u[f, 2 * half, g] = y[:, :128]
                u[f, 2 * half + 1, g] = y[:, 128:]

    stores = [pltpu.make_async_copy(pst, out_p, out_sem.at[3])]
    stores[0].start()
    for f in ORDER:
        if f != 3:
            fix(f)
            stores.append(pltpu.make_async_copy(cst.at[f], out_c.at[f], out_sem.at[f]))
            stores[-1].start()
        contract(f)
        stage_open(f, 0)
    for f in ORDER:
        stage_relay(f, 0)
    for f in ORDER:
        whole = stage_close(f, 0)
        slot = 0 if ROUTES[f][1] == 1 else 1
        if ROUTES[f][0] == "gz":
            b_src_z[slot] = whole
        else:
            b_src_y[slot] = whole
        stage_open(f, 1)
    for f in ORDER:
        stage_relay(f, 1)
    for f in ORDER:
        whole = stage_close(f, 1)
        for g in range(4):
            ysc[16 * f : 16 * f + 16, 128 * g : 128 * g + 128] = whole[g]

    hi, lo = split(ysc[...])

    def last_dot(m, _):
        v[m] = dot(hi, k_hi[m]) + dot(lo, k_hi[m]) + dot(hi, k_lo[m])
        return 0

    lax.fori_loop(0, 8, last_dot, 0)
    copies = [
        remote(v.at[lax.rem(me[0] + o, 8)], v_recv.at[o - 1], xs_sem.at[o - 1], xr_sem.at[o - 1], line_to[o - 1])
        for o in range(1, 8)
    ]
    for c in copies:
        c.start()
    total = v[me[0]]
    for o in range(1, 8):
        copies[o - 1].wait_recv()
        total = total + v_recv[o - 1]
    for a in range(8):
        moved = total if a == 0 else pltpu.roll(total, 128 - 16 * a, 1)
        for f in range(4):
            out_core[a, f] = moved[16 * f : 16 * f + 16, :16]

    for c in copies:
        c.wait_send()
    for r in range(5):
        halo_sent(r, range(6))
    for f in ORDER:
        for stage in range(2):
            for c in stage_copies(f, stage):
                c.wait_send()
    for c in stores:
        c.wait()


def per_device(velocity, inv_density, factor_x, factor_y, factor_z):
    vmem = pl.BlockSpec(memory_space=pltpu.VMEM)
    hbm = pl.BlockSpec(memory_space=pl.ANY)
    tall = TOP + NJ + 8
    dma = pltpu.SemaphoreType.DMA
    scratch = [
        pltpu.VMEM((NI + 2, NJ, NK), F32),
        pltpu.VMEM((NI, tall, NK), F32),
        pltpu.VMEM((NI, NJ, NK), F32),
        pltpu.VMEM((NI + 2, tall, NK), F32),
        pltpu.VMEM((ITERS, NI + 2, tall, NK), F32),
        pltpu.VMEM((NI + 1, NJ, NK), F32),
        pltpu.VMEM((NI, tall, NK), F32),
        pltpu.VMEM((NI, NJ, NK), F32),
        pltpu.VMEM((NI, NJ, NK), F32),
        pltpu.VMEM((NI + 2, tall, NK), F32),
        pltpu.VMEM((NI, NJ, NK), F32),
        pltpu.VMEM((3, NI, NJ, NK), F32),
        pltpu.VMEM((ITERS, 2, NI, NK), F32),
        pltpu.VMEM((ITERS, 2, NI, NK), F32),
        pltpu.VMEM((ITERS, 2, 16, NK), F32),
        pltpu.VMEM((ITERS, 2, 16, NK), F32),
        pltpu.VMEM((2, 2, NI, NK), F32),
        pltpu.VMEM((2, 2, NI, NK), F32),
        pltpu.VMEM((2, 2, 16, NK), F32),
        pltpu.VMEM((2, 2, 16, NK), F32),
        pltpu.VMEM((2, 8, NK), F32),
        pltpu.VMEM((len(PLANE), 8, NK), F32),
        pltpu.VMEM((7, 8, NK), F32),
        pltpu.VMEM((1024, 512), BF16),
        pltpu.VMEM((1024, 512), BF16),
        pltpu.VMEM((64, 192), BF16),
        pltpu.VMEM((8, 512, 128), BF16),
        pltpu.VMEM((8, 512, 128), BF16),
        pltpu.VMEM((4, 256, 1024), BF16),
        pltpu.VMEM((4, 256, 1024), BF16),
        pltpu.VMEM((4, 4, 4, 64, 128), F32),
    ]
    scratch += [pltpu.VMEM((2, 4, 64, 128), F32)] * 4
    scratch += [pltpu.VMEM((2, 4, 4, 16, 128), F32)] * 4
    scratch += [pltpu.VMEM((2, 4, 64, 128), F32), pltpu.VMEM((2, 4, 4, 16, 128), F32)]
    scratch += [pltpu.VMEM((4, 4, 16, 128), F32)] * 4
    scratch += [
        pltpu.VMEM((64, 512), F32),
        pltpu.VMEM((8, 64, 128), F32),
        pltpu.VMEM((7, 64, 128), F32),
        dma((4,)),
        dma((4,)),
        dma((5, 6, 2)),
        dma((5, 6, 2)),
        dma((2, len(PLANE))),
        dma((2, len(PLANE))),
        dma((4, 2, 3)),
        dma((4, 2, 3)),
        dma((7,)),
        dma((7,)),
    ]
    return pl.pallas_call(
        kernel,
        out_shape=(
            jax.ShapeDtypeStruct(inv_density.shape, F32),
            jax.ShapeDtypeStruct(velocity.shape, F32),
            jax.ShapeDtypeStruct((8, 4, 16, 16), F32),
        ),
        in_specs=[hbm, hbm, vmem, vmem, vmem],
        out_specs=(hbm, hbm, vmem),
        scratch_shapes=scratch,
        compiler_params=pltpu.CompilerParams(
            collective_id=0, has_side_effects=True, vmem_limit_bytes=60 * 1024 * 1024
        ),
    )(velocity, inv_density, factor_x, factor_y, factor_z)


def solution(mesh):
    placed = (
        P(None, "gx", "gy", "gz"),
        P("gx", "gy", "gz"),
        P("gx", None),
        P("gy", None),
        P("gz", None),
    )
    return jax.shard_map(
        per_device,
        mesh=mesh,
        in_specs=placed,
        out_specs=(P("gx", "gy", "gz"), P(None, "gx", "gy", "gz"), P("gx", None, "gy", "gz")),
        check_vma=False,
    )
```

```python
import jax
import jax.numpy as jnp
from jax import lax
from jax.experimental import pallas as pl
from jax.experimental.pallas import tpu as pltpu
from jax.sharding import PartitionSpec as P

ITERS = 4
SHIFT = 0.1
MESH = pl.DeviceIdType.MESH
F32 = jnp.float32
BF16 = jnp.bfloat16
NI, NJ, NK = 32, 64, 128
TOP = 8
AXES = ("gx", "gy", "gz")
SIZES = (8, 4, 4)
PLANE = [(dy, dz) for dy in range(4) for dz in range(4) if dy or dz]
ROUTES = {3: ("gz", 1), 1: ("gy", 1), 0: ("gz", -1), 2: ("gy", -1)}
ORDER = (3, 1, 0, 2)
TINY = 1e-11


def two_sum(a, b):
    s = a + b
    t = s - a
    return s, (a - (s - t)) + (b - t)


def quick(a, b):
    s = a + b
    return s, b - (s - a)


def df_add(x, y):
    s, e = two_sum(x[0], y[0])
    return quick(s, e + (x[1] + y[1]))


def df_neg(x):
    return -x[0], -x[1]


def halves(a):
    t = 4097.0 * a
    h = t - (t - a)
    return h, a - h


def df_mul(x, y):
    p = x[0] * y[0]
    ah, al = halves(x[0])
    bh, bl = halves(y[0])
    e = ((ah * bh - p) + ah * bl + al * bh) + al * bl
    return quick(p, e + (x[0] * y[1] + x[1] * y[0]))


def df_recip(x):
    r = 1.0 / x[0]
    one = (jnp.ones_like(r), jnp.zeros_like(r))
    two = (jnp.full_like(r, 2.0), jnp.zeros_like(r))
    y = (r, jnp.zeros_like(r))
    for _ in range(2):
        y = df_mul(y, df_add(two, df_neg(df_mul(x, y))))
    return y


def solve4(nu):
    n = ITERS
    g = [[None] * n for _ in range(n)]
    for i in range(n):
        for j in range(i + 1):
            g[i][j] = df_add(nu[i + j], df_neg(nu[i + j + 1]))
    y = list(nu[:n])
    low = [[None] * n for _ in range(n)]
    inv = []
    for k in range(n):
        pivot = g[k][k]
        start = nu[2 * k][0] - nu[2 * k + 1][0]
        ok = pivot[0] > TINY * start
        safe = (jnp.where(ok, pivot[0], 1.0), jnp.where(ok, pivot[1], 0.0))
        r = df_recip(safe)
        r = (jnp.where(ok, r[0], 0.0), jnp.where(ok, r[1], 0.0))
        inv.append(r)
        for i in range(k + 1, n):
            low[i][k] = df_mul(g[i][k], r)
        for i in range(k + 1, n):
            for j in range(k + 1, i + 1):
                g[i][j] = df_add(g[i][j], df_neg(df_mul(low[i][k], g[j][k])))
            y[i] = df_add(y[i], df_neg(df_mul(low[i][k], y[k])))
    c = [None] * n
    for i in reversed(range(n)):
        v = df_mul(y[i], inv[i])
        for j in range(i + 1, n):
            v = df_add(v, df_neg(df_mul(low[j][i], c[j])))
        c[i] = v
    return [v[0] for v in c]


def lanes(shape):
    return lax.broadcasted_iota(jnp.int32, shape, len(shape) - 1)


def rows(shape):
    return lax.broadcasted_iota(jnp.int32, shape, 0)


def split(x):
    hi = x.astype(BF16)
    return hi, (x - hi.astype(F32)).astype(BF16)


def dot(a, b):
    return lax.dot_general(a, b, (((1,), (0,)), ((), ())), preferred_element_type=F32)


def kernel(
    vel, inv, fx, fy, fz,
    out_p, out_c, out_core,
    vx, vy, vz, ip, w0, w1, w2, w3, cx, cy, cz, dinv, pp, pst, cst,
    zsend, zrecv, zsend0, zrecv0,
    a_send, a_recv0, a_recv1,
    wz_hi, wz_lo, fyt, k_hi, k_lo, xh, xl, u,
    za_in, za_acc, za_dir, za_out, ya_in, ya_acc, ya_dir, ya_out,
    b_src_z, b_src_y, b_in, b_acc, b_dir, b_out, ysc, v, v_recv,
    in_sem, out_sem, hs_sem, hr_sem, as_sem, ar_sem, rs_sem, rr_sem, xs_sem, xr_sem,
):
    w = (w0, w1, w2, w3)
    me = [lax.axis_index(a) for a in AXES]
    has = []
    for a in range(3):
        has += [me[a] > 0, me[a] < SIZES[a] - 1]

    def neighbour(side):
        a = side // 2
        step = 1 if side % 2 else SIZES[a] - 1
        return {AXES[a]: lax.rem(me[a] + step, SIZES[a])}

    def remote(src, dst, ss, rs, dev):
        return pltpu.make_async_remote_copy(
            src_ref=src, dst_ref=dst, send_sem=ss, recv_sem=rs, device_id=dev, device_id_type=MESH
        )

    lane = lanes((8, NK))
    pending = []

    loads = [
        pltpu.make_async_copy(inv, ip.at[pl.ds(1, NI), pl.ds(TOP, NJ)], in_sem.at[0]),
        pltpu.make_async_copy(vel.at[2], vz, in_sem.at[1]),
        pltpu.make_async_copy(vel.at[1], vy.at[:, pl.ds(TOP, NJ)], in_sem.at[2]),
        pltpu.make_async_copy(vel.at[0], vx.at[pl.ds(1, NI)], in_sem.at[3]),
    ]
    for c in loads:
        c.start()

    barrier = pltpu.get_barrier_semaphore()
    for side in range(6):
        pl.semaphore_signal(barrier, inc=1, device_id=neighbour(side), device_id_type=MESH)

    zero_plane = jnp.zeros((NJ, NK), F32)
    zero_row = jnp.zeros((1, NK), F32)
    for s in range(2):
        far = (0, NI + 1)[s]
        edge = (TOP - 1, TOP + NJ)[s]

        @pl.when(jnp.logical_not(has[s]))
        def _():
            vx[far] = zero_plane
            for ref in (ip,) + w:
                ref[far, pl.ds(TOP, NJ)] = zero_plane

        @pl.when(jnp.logical_not(has[2 + s]))
        def _():
            for i in range(NI):
                vy[i, pl.ds(edge, 1)] = zero_row
                for ref in (ip,) + w:
                    ref[i + 1, pl.ds(edge, 1)] = zero_row

        @pl.when(jnp.logical_not(has[4 + s]))
        def _():
            zrecv0[s] = jnp.zeros((2, 32, NK), F32)
            for k in range(ITERS):
                zrecv[k, s] = jnp.zeros((32, NK), F32)

    pl.semaphore_wait(barrier, 6)

    def halo(r, side, landing):
        s, t = side % 2, landing % 2
        ax = side // 2
        planes = pl.ds(1, NI)
        if ax == 0:
            near, far = (1, NI)[s], (0, NI + 1)[t]
            if r == 0:
                edge = (0, NI - 1)[s]
                pairs = [
                    (vel.at[0, edge], vx.at[far]),
                    (inv.at[edge], ip.at[far, pl.ds(TOP, NJ)]),
                ]
            else:
                ref = w[r - 1]
                pairs = [(ref.at[near, pl.ds(TOP, NJ)], ref.at[far, pl.ds(TOP, NJ)])]
        elif ax == 1:
            near, far = (TOP, TOP + NJ - 1)[s], (TOP - 1, TOP + NJ)[t]
            if r == 0:
                edge = (0, NJ - 1)[s]
                pairs = [(vel.at[1, :, edge], vy.at[:, far]), (inv.at[:, edge], ip.at[planes, far])]
            else:
                ref = w[r - 1]
                pairs = [(ref.at[planes, near], ref.at[planes, far])]
        elif r == 0:
            pairs = [(zsend0, zrecv0.at[t])]
        else:
            pairs = [(zsend.at[r - 1], zrecv.at[r - 1, t])]
        return [
            remote(a, b, hs_sem.at[r, side, n], hr_sem.at[r, landing, n], neighbour(side))
            for n, (a, b) in enumerate(pairs)
        ]

    def halo_start(r, sides):
        pending.append(lambda: halo_sent(r, sides))
        for side in sides:
            @pl.when(has[side])
            def _():
                for c in halo(r, side, side ^ 1):
                    c.start()

    def halo_wait(r, sides):
        for side in sides:
            @pl.when(has[side])
            def _():
                for c in halo(r, side, side):
                    c.wait_recv()

    def halo_sent(r, sides):
        for side in sides:
            @pl.when(has[side])
            def _():
                for c in halo(r, side, side ^ 1):
                    c.wait_send()

    halo_start(0, range(4))

    def tiles(x):
        return [x[8 * q : 8 * q + 8] for q in range(x.shape[0] // 8)]

    def pack(acc, x, i):
        out = list(acc)
        for q, part in enumerate(x):
            moved = pltpu.roll(part, 2 * i + 1 + 64 * (q // 4), 1)
            out[q % 4] = jnp.where(lane // 2 == i + 32 * (q // 4), moved, out[q % 4])
        return out

    def unpack(faces, i):
        return [pltpu.roll(faces[q % 4], lax.rem(255 - 2 * i - 64 * (q // 4), 128), 1) for q in range(8)]

    def ahead(x, ends):
        return [pltpu.roll(jnp.where(lane == 0, e, a), NK - 1, 1) for a, e in zip(x, ends)]

    def behind(x, ends):
        return [pltpu.roll(jnp.where(lane == NK - 1, e, a), 1, 1) for a, e in zip(x, ends)]

    first_half = lax.broadcasted_iota(jnp.int32, (8, NK), 1) % 2 == 1

    def merge(plus, minus):
        return [jnp.where(first_half, a, b) for a, b in zip(plus, minus)]

    GROUP = 4
    no_faces = [jnp.zeros((8, NK), F32)] * 4
    zero_acc = jnp.zeros((8, NK), F32)

    for c in loads[:2]:
        c.wait()

    def face0(t, carry):
        a, b = carry
        for g in range(GROUP):
            i = t * GROUP + g
            a = pack(a, tiles(vz[i]), i)
            b = pack(b, tiles(ip[i + 1, pl.ds(TOP, NJ)]), i)
        return a, b

    fu, fn = lax.fori_loop(0, NI // GROUP, face0, (no_faces, no_faces))
    zsend0[0] = jnp.concatenate(fu, axis=0)
    zsend0[1] = jnp.concatenate(fn, axis=0)
    halo_start(0, (4, 5))
    for c in loads[2:]:
        c.wait()

    fzp = jnp.concatenate([fz[...], jnp.zeros((64, NK), F32)], axis=0).T
    lane_k = lanes((NK, 128))

    def build_z(i8, _):
        row = pl.ds(pl.multiple_of(i8 * 128, 128), 128)
        for r in range(4):
            moved = pltpu.roll(fzp, lax.rem(16 * i8 + 128 - 16 * r, 128), 1)
            hi, lo = split(jnp.where(lane_k // 16 == i8, moved, 0.0))
            wz_hi[row, pl.ds(128 * r, 128)] = hi
            wz_lo[row, pl.ds(128 * r, 128)] = lo
        return 0

    lax.fori_loop(0, 8, build_z, 0)
    fyp = jnp.concatenate([fy[...], jnp.zeros((NJ, 64), F32)], axis=1)
    hi, lo = split(fyp.T[:64])
    fyt[...] = jnp.concatenate([hi, lo, hi], axis=1)
    fx_hi, fx_lo = split(fx[...])
    rep = (rows((512, NI)) // 16 == lanes((512, NI))).astype(F32).astype(BF16)
    same = (rows((512, 128)) % 16) == (lanes((512, 128)) % 16)

    def build_x(m, _):
        pick = (rows((64, 128)) == 8 * m + lanes((64, 128)) // 16).astype(F32).astype(BF16)
        for part, dst in ((fx_hi, k_hi), (fx_lo, k_lo)):
            wide = dot(part, pick).astype(BF16)
            dst[m] = jnp.where(same, dot(rep, wide), 0.0).astype(BF16)
        return 0

    lax.fori_loop(0, 8, build_x, 0)

    halo_wait(0, range(6))

    fu = merge(tiles(zrecv0[1, 0]), tiles(zrecv0[0, 0]))
    nminus = tiles(zrecv0[0, 1])
    czb = [0.5 * (a + pltpu.roll(b, NK - 1, 1)) for a, b in zip(nminus, fn)]
    fn = merge(tiles(zrecv0[1, 1]), nminus)

    def accumulate(acc, parts):
        while len(parts) > 1:
            parts = [parts[n] + parts[n + 1] for n in range(0, len(parts), 2)]
        s, e = two_sum(acc[0], parts[0])
        return s, acc[1] + e

    def mul(a, b):
        return [x * y for x, y in zip(a, b)]

    def join(x):
        return jnp.concatenate(x, axis=0)

    def first(t, carry):
        faces, acc = carry
        terms = []
        for g in range(GROUP):
            i = t * GROUP + g
            n = ip[i + 1, pl.ds(TOP, NJ)]
            xf = ip[i + 2, pl.ds(TOP, NJ)]
            yf = ip[i + 1, pl.ds(TOP + 1, NJ)]
            xb = ip[i, pl.ds(TOP, NJ)]
            yb = ip[i + 1, pl.ds(TOP - 1, NJ)]
            nt = tiles(n)
            ends = unpack(fn, i)
            zb = join(behind(nt, ends))
            zf = join(ahead(nt, ends))
            cx[i + 1] = 0.5 * (n + xf)
            cy[i, pl.ds(TOP, NJ)] = 0.5 * (n + yf)
            cy[i, pl.ds(TOP - 1, 1)] = 0.5 * (n + yb)[0:1]
            cz[i] = 0.5 * (n + zf)
            d = (SHIFT + 3.0 * n) + 0.5 * (((xf + xb) + (yf + yb)) + (zf + zb))
            at = tiles(vz[i])
            ends = unpack(fu, i)
            div = (vx[i + 2] - vx[i]) + (vy[i, pl.ds(TOP + 1, NJ)] - vy[i, pl.ds(TOP - 1, NJ)])
            div = div + (join(ahead(at, ends)) - join(behind(at, ends)))
            b = -0.5 * div
            di = 1.0 / d
            dinv[i] = di
            new = b * di
            w0[i + 1, pl.ds(TOP, NJ)] = new
            faces = pack(faces, tiles(new), i)
            terms += tiles(b * new)
        return faces, accumulate(acc, terms)

    cx[0] = 0.5 * (ip[0, pl.ds(TOP, NJ)] + ip[1, pl.ds(TOP, NJ)])
    faces, acc = lax.fori_loop(0, NI // GROUP, first, (no_faces, (zero_acc, zero_acc)))
    moments = [acc]

    for k in range(ITERS):
        zsend[k] = join(faces)
        halo_start(k + 1, range(6))
        halo_wait(k + 1, range(6))
        after = tiles(zrecv[k, 1])
        flux = merge(after, mul(czb, tiles(zrecv[k, 0])))
        last = k == ITERS - 1
        here = w[k]
        there = None if last else w[k + 1]

        def step(t, carry):
            faces, odd, even = carry
            t_odd, t_even = [], []
            for g in range(GROUP):
                i = t * GROUP + g
                c = here[i + 1, pl.ds(TOP, NJ)]
                f = cz[i]
                bw = cx[i] * here[i, pl.ds(TOP, NJ)] + cx[i + 1] * here[i + 2, pl.ds(TOP, NJ)]
                bw = bw + cy[i, pl.ds(TOP - 1, NJ)] * here[i + 1, pl.ds(TOP - 1, NJ)]
                bw = bw + cy[i, pl.ds(TOP, NJ)] * here[i + 1, pl.ds(TOP + 1, NJ)]
                ends = unpack(flux, i)
                bw = bw + (f * join(ahead(tiles(c), ends)) + join(behind(tiles(f * c), ends)))
                t_odd += tiles(c * bw)
                if not last:
                    new = bw * dinv[i]
                    t_even += tiles(bw * new)
                    there[i + 1, pl.ds(TOP, NJ)] = new
                    faces = pack(faces, tiles(new), i)
            odd = accumulate(odd, t_odd)
            if not last:
                even = accumulate(even, t_even)
            return faces, odd, even

        start = (no_faces, (zero_acc, zero_acc), (zero_acc, zero_acc))
        faces, odd, even = lax.fori_loop(0, NI // GROUP, step, start)
        moments.append(odd)
        if not last:
            moments.append(even)

    row8 = rows((8, NK))
    lane8 = lanes((8, NK))
    hi = zero_acc
    lo = zero_acc
    for m, acc in enumerate(moments):
        for shift in (4, 2, 1):
            acc = df_add(acc, (pltpu.roll(acc[0], shift, 0), pltpu.roll(acc[1], shift, 0)))
        hi = jnp.where(row8 == m, acc[0], hi)
        lo = jnp.where(row8 == m, acc[1], lo)
    total = (hi, lo)
    for shift in (64, 32, 16, 8, 4, 2, 1):
        total = df_add(total, (pltpu.roll(total[0], shift, 1), pltpu.roll(total[1], shift, 1)))

    plane_to = [{"gy": lax.rem(me[1] + dy, 4), "gz": lax.rem(me[2] + dz, 4)} for dy, dz in PLANE]
    line_to = [{"gx": lax.rem(me[0] + o, 8)} for o in range(1, 8)]
    for stage, (peers, landing) in enumerate(((plane_to, a_recv0), (line_to, a_recv1))):
        a_send[stage] = jnp.where(lane8 < 64, total[0], total[1])
        copies = [
            remote(a_send.at[stage], landing.at[n], as_sem.at[stage, n], ar_sem.at[stage, n], dev)
            for n, dev in enumerate(peers)
        ]
        for c in copies:
            c.start()
        for c in copies:
            c.wait_recv()
        terms = [total]
        for n in range(len(peers)):
            x = landing[n]
            y = pltpu.roll(x, 64, 1)
            terms.append((jnp.where(lane8 < 64, x, y), jnp.where(lane8 < 64, y, x)))
        while len(terms) > 1:
            terms = [
                df_add(terms[t], terms[t + 1]) if t + 1 < len(terms) else terms[t]
                for t in range(0, len(terms), 2)
            ]
        total = terms[0]
        for c in copies:
            c.wait_send()

    nu = [(total[0][m : m + 1], total[1][m : m + 1]) for m in range(2 * ITERS)]
    coef = solve4(nu)

    def combine(parts):
        total = coef[0] * parts[0]
        for c, x in zip(coef[1:], parts[1:]):
            total = total + c * x
        return total

    pe = combine([join(merge(tiles(zrecv[k, 1]), tiles(zrecv[k, 0]))) for k in range(ITERS)])
    pe = tiles(pe)
    for far in (0, NI + 1):
        pp[far, pl.ds(TOP, NJ)] = combine([ref[far, pl.ds(TOP, NJ)] for ref in w])

    def keep(f, i, x):
        hi, lo = split(x)
        rr = pl.ds(pl.multiple_of((i // 8) * NJ, NJ), NJ)
        cc = pl.ds(pl.multiple_of(lax.rem(i, 8) * NK, NK), NK)
        xh[f, rr, cc] = hi
        xl[f, rr, cc] = lo

    def press(t, _):
        for g in range(GROUP):
            i = t * GROUP + g
            for top, n in ((TOP - 1, 1), (TOP + NJ, 1)):
                pp[i + 1, pl.ds(top, n)] = combine([ref[i + 1, pl.ds(top, n)] for ref in w])
            x = combine([ref[i + 1, pl.ds(TOP, NJ)] for ref in w])
            pp[i + 1, pl.ds(TOP, NJ)] = x
            pst[i] = x
            keep(3, i, x)
        return 0

    lax.fori_loop(0, NI // GROUP, press, 0)

    def fix(f):
        def body(t, _):
            for g in range(GROUP):
                i = t * GROUP + g
                n = ip[i + 1, pl.ds(TOP, NJ)]
                if f == 0:
                    g_ = pp[i + 2, pl.ds(TOP, NJ)] - pp[i, pl.ds(TOP, NJ)]
                    x = vx[i + 1]
                elif f == 1:
                    g_ = pp[i + 1, pl.ds(TOP + 1, NJ)] - pp[i + 1, pl.ds(TOP - 1, NJ)]
                    x = vy[i, pl.ds(TOP, NJ)]
                else:
                    c = tiles(pp[i + 1, pl.ds(TOP, NJ)])
                    ends = unpack(pe, i)
                    g_ = join(ahead(c, ends)) - join(behind(c, ends))
                    x = vz[i]
                x = x - n * (0.5 * g_)
                cst[f, i] = x
                keep(f, i, x)
            return 0

        lax.fori_loop(0, NI // GROUP, body, 0)

    def ring(axis, way):
        a = AXES.index(axis)
        n = SIZES[a]
        to = lax.rem(me[a] + (n + way), n)
        back = lax.rem(me[a] + (n - way), n)
        opposite = lax.rem(me[a] + 2, n)
        return to, back, opposite

    def rows16(m):
        return pl.ds(pl.multiple_of(m * 16, 16), 16)

    def stage_refs(f, stage):
        axis, way = ROUTES[f]
        slot = 0 if way == 1 else 1
        if stage == 0:
            if axis == "gz":
                return axis, way, (lambda m: u.at[f, m]), za_in.at[slot], za_acc.at[slot], za_dir.at[slot], za_out.at[slot]
            return axis, way, (lambda m: u.at[f, :, :, rows16(m)]), ya_in.at[slot], ya_acc.at[slot], ya_dir.at[slot], ya_out.at[slot]
        other = "gy" if axis == "gz" else "gz"
        if axis == "gz":
            chunk = lambda m: b_src_z.at[slot, :, rows16(m)]
        else:
            chunk = lambda m: b_src_y.at[slot, m]
        return other, way, chunk, b_in.at[f], b_acc.at[f], b_dir.at[f], b_out.at[f]

    def stage_copies(f, stage):
        axis, way, chunk, r_in, r_acc, r_dir, r_out = stage_refs(f, stage)
        to, back, opposite = ring(axis, way)
        sems = lambda n: (rs_sem.at[f, stage, n], rr_sem.at[f, stage, n])
        return (
            remote(chunk(opposite), r_in, *sems(0), {axis: to}),
            remote(chunk(back), r_dir, *sems(1), {axis: back}),
            remote(r_out, r_acc, *sems(2), {axis: to}),
        )

    def stage_open(f, stage):
        far, near, _ = stage_copies(f, stage)
        far.start()
        near.start()
        pending.append(far.wait_send)
        pending.append(near.wait_send)

    def stage_relay(f, stage):
        axis, way, chunk, r_in, r_acc, r_dir, r_out = stage_refs(f, stage)
        to, back, opposite = ring(axis, way)
        far, near, relay = stage_copies(f, stage)
        far.wait_recv()
        r_out[...] = r_in[...] + chunk(to)[...]
        relay.start()
        pending.append(relay.wait_send)

    def stage_close(f, stage):
        axis, way, chunk, r_in, r_acc, r_dir, r_out = stage_refs(f, stage)
        far, near, relay = stage_copies(f, stage)
        near.wait_recv()
        relay.wait_recv()
        return chunk(me[AXES.index(axis)])[...] + r_acc[...] + r_dir[...]

    def contract(f):
        wh, wl = wz_hi[...], wz_lo[...]
        a, b = xh[f], xl[f]
        for half in range(2):
            cols = slice(256 * half, 256 * half + 256)
            z = dot(a, wh[:, cols]) + dot(b, wh[:, cols]) + dot(a, wl[:, cols])
            for g in range(4):
                hi, lo = split(z[NJ * g : NJ * g + NJ])
                y = dot(fyt[...], jnp.concatenate([hi, hi, lo], axis=0))
                u[f, 2 * half, g] = y[:, :128]
                u[f, 2 * half + 1, g] = y[:, 128:]

    stores = [pltpu.make_async_copy(pst, out_p, out_sem.at[3])]
    stores[0].start()
    pending.append(stores[0].wait)
    for f in ORDER:
        if f != 3:
            fix(f)
            stores.append(pltpu.make_async_copy(cst.at[f], out_c.at[f], out_sem.at[f]))
            stores[-1].start()
            pending.append(stores[-1].wait)
        contract(f)
        stage_open(f, 0)
    for f in ORDER:
        stage_relay(f, 0)
    for f in ORDER:
        whole = stage_close(f, 0)
        slot = 0 if ROUTES[f][1] == 1 else 1
        if ROUTES[f][0] == "gz":
            b_src_z[slot] = whole
        else:
            b_src_y[slot] = whole
        stage_open(f, 1)
    for f in ORDER:
        stage_relay(f, 1)
    for f in ORDER:
        whole = stage_close(f, 1)
        for g in range(4):
            ysc[16 * f : 16 * f + 16, 128 * g : 128 * g + 128] = whole[g]

    hi, lo = split(ysc[...])

    def last_dot(m, _):
        v[m] = dot(hi, k_hi[m]) + dot(lo, k_hi[m]) + dot(hi, k_lo[m])
        return 0

    lax.fori_loop(0, 8, last_dot, 0)
    copies = [
        remote(v.at[lax.rem(me[0] + o, 8)], v_recv.at[o - 1], xs_sem.at[o - 1], xr_sem.at[o - 1], line_to[o - 1])
        for o in range(1, 8)
    ]
    for c in copies:
        c.start()
        pending.append(c.wait_send)
    total = v[me[0]]
    for o in range(1, 8):
        copies[o - 1].wait_recv()
        total = total + v_recv[o - 1]
    for a in range(8):
        moved = total if a == 0 else pltpu.roll(total, 128 - 16 * a, 1)
        for f in range(4):
            out_core[a, f] = moved[16 * f : 16 * f + 16, :16]

    for wait in pending:
        wait()


def per_device(velocity, inv_density, factor_x, factor_y, factor_z):
    vmem = pl.BlockSpec(memory_space=pltpu.VMEM)
    hbm = pl.BlockSpec(memory_space=pl.ANY)
    tall = TOP + NJ + 8
    dma = pltpu.SemaphoreType.DMA
    scratch = [
        pltpu.VMEM((NI + 2, NJ, NK), F32),
        pltpu.VMEM((NI, tall, NK), F32),
        pltpu.VMEM((NI, NJ, NK), F32),
        pltpu.VMEM((NI + 2, tall, NK), F32),
        pltpu.VMEM((NI + 2, tall, NK), F32),
        pltpu.VMEM((NI + 2, tall, NK), F32),
        pltpu.VMEM((NI + 2, tall, NK), F32),
        pltpu.VMEM((NI + 2, tall, NK), F32),
        pltpu.VMEM((NI + 1, NJ, NK), F32),
        pltpu.VMEM((NI, tall, NK), F32),
        pltpu.VMEM((NI, NJ, NK), F32),
        pltpu.VMEM((NI, NJ, NK), F32),
        pltpu.VMEM((NI + 2, tall, NK), F32),
        pltpu.VMEM((NI, NJ, NK), F32),
        pltpu.VMEM((3, NI, NJ, NK), F32),
        pltpu.VMEM((ITERS, 32, NK), F32),
        pltpu.VMEM((ITERS, 2, 32, NK), F32),
        pltpu.VMEM((2, 32, NK), F32),
        pltpu.VMEM((2, 2, 32, NK), F32),
        pltpu.VMEM((2, 8, NK), F32),
        pltpu.VMEM((len(PLANE), 8, NK), F32),
        pltpu.VMEM((7, 8, NK), F32),
        pltpu.VMEM((1024, 512), BF16),
        pltpu.VMEM((1024, 512), BF16),
        pltpu.VMEM((64, 192), BF16),
        pltpu.VMEM((8, 512, 128), BF16),
        pltpu.VMEM((8, 512, 128), BF16),
        pltpu.VMEM((4, 256, 1024), BF16),
        pltpu.VMEM((4, 256, 1024), BF16),
        pltpu.VMEM((4, 4, 4, 64, 128), F32),
    ]
    scratch += [pltpu.VMEM((2, 4, 64, 128), F32)] * 4
    scratch += [pltpu.VMEM((2, 4, 4, 16, 128), F32)] * 4
    scratch += [pltpu.VMEM((2, 4, 64, 128), F32), pltpu.VMEM((2, 4, 4, 16, 128), F32)]
    scratch += [pltpu.VMEM((4, 4, 16, 128), F32)] * 4
    scratch += [
        pltpu.VMEM((64, 512), F32),
        pltpu.VMEM((8, 64, 128), F32),
        pltpu.VMEM((7, 64, 128), F32),
        dma((4,)),
        dma((4,)),
        dma((5, 6, 2)),
        dma((5, 6, 2)),
        dma((2, len(PLANE))),
        dma((2, len(PLANE))),
        dma((4, 2, 3)),
        dma((4, 2, 3)),
        dma((7,)),
        dma((7,)),
    ]
    return pl.pallas_call(
        kernel,
        out_shape=(
            jax.ShapeDtypeStruct(inv_density.shape, F32),
            jax.ShapeDtypeStruct(velocity.shape, F32),
            jax.ShapeDtypeStruct((8, 4, 16, 16), F32),
        ),
        in_specs=[hbm, hbm, vmem, vmem, vmem],
        out_specs=(hbm, hbm, vmem),
        scratch_shapes=scratch,
        compiler_params=pltpu.CompilerParams(
            collective_id=0, has_side_effects=True, vmem_limit_bytes=60 * 1024 * 1024
        ),
    )(velocity, inv_density, factor_x, factor_y, factor_z.T)


def solution(mesh):
    placed = (
        P(None, "gx", "gy", "gz"),
        P("gx", "gy", "gz"),
        P("gx", None),
        P("gy", None),
        P("gz", None),
    )
    return jax.shard_map(
        per_device,
        mesh=mesh,
        in_specs=placed,
        out_specs=(P("gx", "gy", "gz"), P(None, "gx", "gy", "gz"), P("gx", None, "gy", "gz")),
        check_vma=False,
    )
```

```python
import jax
import jax.numpy as jnp
from jax import lax
from jax.experimental import pallas as pl
from jax.experimental.pallas import tpu as pltpu
from jax.sharding import PartitionSpec as P

ITERS = 4
SHIFT = 0.1
MESH = pl.DeviceIdType.MESH
F32 = jnp.float32
BF16 = jnp.bfloat16
NI, NJ, NK = 32, 64, 128
TOP = 8
AXES = ("gx", "gy", "gz")
SIZES = (8, 4, 4)
PLANE = [(dy, dz) for dy in range(4) for dz in range(4) if dy or dz]
ROUTES = {3: ("gz", 1), 1: ("gy", 1), 0: ("gz", -1), 2: ("gy", -1)}
ORDER = (3, 1, 0, 2)
TINY = 1e-11


def two_sum(a, b):
    s = a + b
    t = s - a
    return s, (a - (s - t)) + (b - t)


def quick(a, b):
    s = a + b
    return s, b - (s - a)


def df_add(x, y):
    s, e = two_sum(x[0], y[0])
    return quick(s, e + (x[1] + y[1]))


def df_neg(x):
    return -x[0], -x[1]


def halves(a):
    t = 4097.0 * a
    h = t - (t - a)
    return h, a - h


def df_mul(x, y):
    p = x[0] * y[0]
    ah, al = halves(x[0])
    bh, bl = halves(y[0])
    e = ((ah * bh - p) + ah * bl + al * bh) + al * bl
    return quick(p, e + (x[0] * y[1] + x[1] * y[0]))


def df_recip(x):
    r = 1.0 / x[0]
    one = (jnp.ones_like(r), jnp.zeros_like(r))
    two = (jnp.full_like(r, 2.0), jnp.zeros_like(r))
    y = (r, jnp.zeros_like(r))
    for _ in range(2):
        y = df_mul(y, df_add(two, df_neg(df_mul(x, y))))
    return y


def solve4(nu):
    n = ITERS
    g = [[None] * n for _ in range(n)]
    for i in range(n):
        for j in range(i + 1):
            g[i][j] = df_add(nu[i + j], df_neg(nu[i + j + 1]))
    y = list(nu[:n])
    low = [[None] * n for _ in range(n)]
    inv = []
    for k in range(n):
        pivot = g[k][k]
        start = nu[2 * k][0] - nu[2 * k + 1][0]
        ok = pivot[0] > TINY * start
        safe = (jnp.where(ok, pivot[0], 1.0), jnp.where(ok, pivot[1], 0.0))
        r = df_recip(safe)
        r = (jnp.where(ok, r[0], 0.0), jnp.where(ok, r[1], 0.0))
        inv.append(r)
        for i in range(k + 1, n):
            low[i][k] = df_mul(g[i][k], r)
        for i in range(k + 1, n):
            for j in range(k + 1, i + 1):
                g[i][j] = df_add(g[i][j], df_neg(df_mul(low[i][k], g[j][k])))
            y[i] = df_add(y[i], df_neg(df_mul(low[i][k], y[k])))
    c = [None] * n
    for i in reversed(range(n)):
        v = df_mul(y[i], inv[i])
        for j in range(i + 1, n):
            v = df_add(v, df_neg(df_mul(low[j][i], c[j])))
        c[i] = v
    return [v[0] for v in c]


def lanes(shape):
    return lax.broadcasted_iota(jnp.int32, shape, len(shape) - 1)


def rows(shape):
    return lax.broadcasted_iota(jnp.int32, shape, 0)


def split(x):
    hi = x.astype(BF16)
    return hi, (x - hi.astype(F32)).astype(BF16)


def dot(a, b):
    return lax.dot_general(a, b, (((1,), (0,)), ((), ())), preferred_element_type=F32)


def kernel(
    vel, inv, fx, fy, fz,
    out_p, out_c, out_core,
    vx, vy, vz, ip, w0, w1, w2, w3, cx, cy, cz, dinv, pp, pst, cst,
    part, xrecv, xrecv0, xcoef, ysend, yrecv, yrecv0, yown, ycoef, yf, yd,
    zsend, zrecv, zsend0, zrecv0,
    a_send, a_recv0, a_recv1,
    wz_hi, wz_lo, fyt, k_hi, k_lo, xh, xl, u,
    za_in, za_acc, za_dir, za_out, ya_in, ya_acc, ya_dir, ya_out,
    b_src_z, b_src_y, b_in, b_acc, b_dir, b_out, ysc, v, v_recv,
    in_sem, out_sem, hs_sem, hr_sem, as_sem, ar_sem, rs_sem, rr_sem, xs_sem, xr_sem,
):
    w = (w0, w1, w2, w3)
    me = [lax.axis_index(a) for a in AXES]
    has = []
    for a in range(3):
        has += [me[a] > 0, me[a] < SIZES[a] - 1]

    def neighbour(side):
        a = side // 2
        step = 1 if side % 2 else SIZES[a] - 1
        return {AXES[a]: lax.rem(me[a] + step, SIZES[a])}

    def remote(src, dst, ss, rs, dev):
        return pltpu.make_async_remote_copy(
            src_ref=src, dst_ref=dst, send_sem=ss, recv_sem=rs, device_id=dev, device_id_type=MESH
        )

    lane = lanes((8, NK))
    pending = []

    loads = [
        pltpu.make_async_copy(inv, ip.at[pl.ds(1, NI), pl.ds(TOP, NJ)], in_sem.at[0]),
        pltpu.make_async_copy(vel.at[2], vz, in_sem.at[1]),
        pltpu.make_async_copy(vel.at[1], vy.at[:, pl.ds(TOP, NJ)], in_sem.at[2]),
        pltpu.make_async_copy(vel.at[0], vx.at[pl.ds(1, NI)], in_sem.at[3]),
        pltpu.make_async_copy(inv.at[:, 0], yown.at[0], in_sem.at[4]),
        pltpu.make_async_copy(inv.at[:, NJ - 1], yown.at[1], in_sem.at[5]),
    ]
    for c in loads:
        c.start()

    barrier = pltpu.get_barrier_semaphore()
    for side in range(6):
        pl.semaphore_signal(barrier, inc=1, device_id=neighbour(side), device_id_type=MESH)

    zero_plane = jnp.zeros((NJ, NK), F32)
    zero_row = jnp.zeros((1, NK), F32)
    for ref in (vx, ip) + w:
        top = 0 if ref is vx else TOP
        for far in (0, NI + 1):
            ref[far, pl.ds(top, NJ)] = zero_plane
    for ref in (vy, ip) + w:
        for i in range(NI):
            for far in (TOP - 1, TOP + NJ):
                ref[i if ref is vy else i + 1, pl.ds(far, 1)] = zero_row
    for s in range(2):
        @pl.when(jnp.logical_not(has[s]))
        def _():
            xrecv0[s] = jnp.zeros((2, NJ, NK), F32)
            for k in range(ITERS):
                xrecv[k, s] = zero_plane

        @pl.when(jnp.logical_not(has[2 + s]))
        def _():
            yrecv0[s] = jnp.zeros((2, NI, NK), F32)
            for k in range(ITERS):
                yrecv[k, s] = jnp.zeros((NI, NK), F32)

        @pl.when(jnp.logical_not(has[4 + s]))
        def _():
            zrecv0[s] = jnp.zeros((2, 32, NK), F32)
            for k in range(ITERS):
                zrecv[k, s] = jnp.zeros((32, NK), F32)

    pl.semaphore_wait(barrier, 6)

    def halo(r, side, landing):
        s, t = side % 2, landing % 2
        ax = side // 2
        if ax == 0:
            if r == 0:
                edge = (0, NI - 1)[s]
                pairs = [(vel.at[0, edge], xrecv0.at[t, 0]), (inv.at[edge], xrecv0.at[t, 1])]
            else:
                pairs = [(w[r - 1].at[(1, NI)[s], pl.ds(TOP, NJ)], xrecv.at[r - 1, t])]
        elif ax == 1:
            if r == 0:
                edge = (0, NJ - 1)[s]
                pairs = [(vel.at[1, :, edge], yrecv0.at[t, 0]), (inv.at[:, edge], yrecv0.at[t, 1])]
            else:
                pairs = [(ysend.at[r - 1, s], yrecv.at[r - 1, t])]
        elif r == 0:
            pairs = [(zsend0, zrecv0.at[t])]
        else:
            pairs = [(zsend.at[r - 1], zrecv.at[r - 1, t])]
        return [
            remote(a, b, hs_sem.at[r, side, n], hr_sem.at[r, landing, n], neighbour(side))
            for n, (a, b) in enumerate(pairs)
        ]

    def halo_start(r, sides):
        pending.append(lambda: halo_sent(r, sides))
        for side in sides:
            @pl.when(has[side])
            def _():
                for c in halo(r, side, side ^ 1):
                    c.start()

    def halo_wait(r, sides):
        for side in sides:
            @pl.when(has[side])
            def _():
                for c in halo(r, side, side):
                    c.wait_recv()

    def halo_sent(r, sides):
        for side in sides:
            @pl.when(has[side])
            def _():
                for c in halo(r, side, side ^ 1):
                    c.wait_send()

    halo_start(0, range(4))

    def tiles(x):
        return [x[8 * q : 8 * q + 8] for q in range(x.shape[0] // 8)]

    def pack(acc, x, i):
        out = list(acc)
        for q, part in enumerate(x):
            moved = pltpu.roll(part, 2 * i + 1 + 64 * (q // 4), 1)
            out[q % 4] = jnp.where(lane // 2 == i + 32 * (q // 4), moved, out[q % 4])
        return out

    def unpack(faces, i):
        return [pltpu.roll(faces[q % 4], lax.rem(255 - 2 * i - 64 * (q // 4), 128), 1) for q in range(8)]

    odd_lane = lane % 2 == 1
    end_lane = (lane == 0) | (lane == NK - 1)
    sub = rows((8, NK))

    def ahead(x):
        return [jnp.where(lane == NK - 1, 0.0, pltpu.roll(a, NK - 1, 1)) for a in x]

    def behind(x):
        return [jnp.where(lane == 0, 0.0, pltpu.roll(a, 1, 1)) for a in x]

    def opposite_faces(plus, minus):
        return [
            jnp.where(odd_lane, pltpu.roll(b, 1, 1), pltpu.roll(a, NK - 1, 1))
            for a, b in zip(tiles(plus), tiles(minus))
        ]

    def at_ends(faces, i):
        return [jnp.where(end_lane, e, 0.0) for e in unpack(faces, i)]

    def add_rows(x, ref, i):
        low = jnp.where(sub == 0, ref[0, pl.ds(i, 1)], 0.0)
        high = jnp.where(sub == 7, ref[1, pl.ds(i, 1)], 0.0)
        return [x[0] + low] + x[1:7] + [x[7] + high]

    GROUP = 4
    no_faces = [jnp.zeros((8, NK), F32)] * 4
    zero_acc = jnp.zeros((8, NK), F32)

    for c in loads[:2]:
        c.wait()

    def face0(t, carry):
        a, b = carry
        for g in range(GROUP):
            i = t * GROUP + g
            a = pack(a, tiles(vz[i]), i)
            b = pack(b, tiles(ip[i + 1, pl.ds(TOP, NJ)]), i)
        return a, b

    fu, fn = lax.fori_loop(0, NI // GROUP, face0, (no_faces, no_faces))
    zsend0[0] = jnp.concatenate(fu, axis=0)
    zsend0[1] = jnp.concatenate(fn, axis=0)
    halo_start(0, (4, 5))
    for c in loads[2:]:
        c.wait()

    fzp = jnp.concatenate([fz[...], jnp.zeros((64, NK), F32)], axis=0).T
    lane_k = lanes((NK, 128))

    def build_z(i8, _):
        row = pl.ds(pl.multiple_of(i8 * 128, 128), 128)
        for r in range(4):
            moved = pltpu.roll(fzp, lax.rem(16 * i8 + 128 - 16 * r, 128), 1)
            hi, lo = split(jnp.where(lane_k // 16 == i8, moved, 0.0))
            wz_hi[row, pl.ds(128 * r, 128)] = hi
            wz_lo[row, pl.ds(128 * r, 128)] = lo
        return 0

    lax.fori_loop(0, 8, build_z, 0)
    fyp = jnp.concatenate([fy[...], jnp.zeros((NJ, 64), F32)], axis=1)
    hi, lo = split(fyp.T[:64])
    fyt[...] = jnp.concatenate([hi, lo, hi], axis=1)
    fx_hi, fx_lo = split(fx[...])
    rep = (rows((512, NI)) // 16 == lanes((512, NI))).astype(F32).astype(BF16)
    same = (rows((512, 128)) % 16) == (lanes((512, 128)) % 16)

    def build_x(m, _):
        pick = (rows((64, 128)) == 8 * m + lanes((64, 128)) // 16).astype(F32).astype(BF16)
        for part, dst in ((fx_hi, k_hi), (fx_lo, k_lo)):
            wide = dot(part, pick).astype(BF16)
            dst[m] = jnp.where(same, dot(rep, wide), 0.0).astype(BF16)
        return 0

    lax.fori_loop(0, 8, build_x, 0)

    def accumulate(acc, parts):
        while len(parts) > 1:
            parts = [parts[n] + parts[n + 1] for n in range(0, len(parts), 2)]
        s, e = two_sum(acc[0], parts[0])
        return s, acc[1] + e

    def mul(a, b):
        return [x * y for x, y in zip(a, b)]

    def join(x):
        return jnp.concatenate(x, axis=0)

    def join_edges(ref):
        return jnp.stack([ref[1, pl.ds(TOP, NJ)], ref[NI, pl.ds(TOP, NJ)]])

    cx[0] = zero_plane

    def inner0(t, _):
        for g in range(GROUP):
            i = t * GROUP + g
            n = ip[i + 1, pl.ds(TOP, NJ)]
            xf = ip[i + 2, pl.ds(TOP, NJ)]
            yn = ip[i + 1, pl.ds(TOP + 1, NJ)]
            nt = tiles(n)
            zn = ahead(nt)
            cx[i + 1] = 0.5 * (n + xf)
            cy[i, pl.ds(TOP, NJ)] = 0.5 * (n + yn)
            cy[i, pl.ds(TOP - 1, 1)] = zero_row
            cz[i] = join([jnp.where(lane == NK - 1, 0.0, 0.5 * (a + b)) for a, b in zip(nt, zn)])
            around = (xf + ip[i, pl.ds(TOP, NJ)]) + (yn + ip[i + 1, pl.ds(TOP - 1, NJ)])
            around = around + (join(zn) + join(behind(nt)))
            dinv[i] = (SHIFT + 3.0 * n) + 0.5 * around
            at = tiles(vz[i])
            div = (vx[i + 2] - vx[i]) + (vy[i, pl.ds(TOP + 1, NJ)] - vy[i, pl.ds(TOP - 1, NJ)])
            part[i] = div + (join(ahead(at)) - join(behind(at)))
        return 0

    lax.fori_loop(0, NI // GROUP, inner0, 0)

    halo_wait(0, range(6))

    xcoef[...] = 0.5 * (xrecv0[:, 1] + join_edges(ip))
    ycoef[...] = 0.5 * (yrecv0[:, 1] + yown[...])
    hn = opposite_faces(zrecv0[1, 1], zrecv0[0, 1])
    hu = opposite_faces(zrecv0[1, 0], zrecv0[0, 0])
    hu = [jnp.where(odd_lane, -a, a) for a in hu]
    zcoef = [0.5 * (a + b) for a, b in zip(hn, fn)]
    yd[...] = 0.5 * yrecv0[:, 1]
    yf[0] = -yrecv0[0, 0]
    yf[1] = yrecv0[1, 0]
    hn = [0.5 * a for a in hn]
    dinv[0] = dinv[0] + 0.5 * xrecv0[0, 1]
    dinv[NI - 1] = dinv[NI - 1] + 0.5 * xrecv0[1, 1]
    part[0] = part[0] - xrecv0[0, 0]
    part[NI - 1] = part[NI - 1] + xrecv0[1, 0]

    def first(t, carry):
        faces, acc = carry
        terms = []
        for g in range(GROUP):
            i = t * GROUP + g
            row = pl.ds(i, 1)
            d = add_rows(tiles(dinv[i]), yd, i)
            d = [a + b for a, b in zip(d, at_ends(hn, i))]
            b = add_rows(tiles(part[i]), yf, i)
            b = [-0.5 * (x + y) for x, y in zip(b, at_ends(hu, i))]
            di = [1.0 / x for x in d]
            new = mul(b, di)
            dinv[i] = join(di)
            w0[i + 1, pl.ds(TOP, NJ)] = join(new)
            ysend[0, 0, row] = new[0][0:1]
            ysend[0, 1, row] = new[7][7:8]
            faces = pack(faces, new, i)
            terms += mul(b, new)
        return faces, accumulate(acc, terms)

    faces, acc = lax.fori_loop(0, NI // GROUP, first, (no_faces, (zero_acc, zero_acc)))
    moments = [acc]

    for k in range(ITERS):
        zsend[k] = join(faces)
        halo_start(k + 1, range(6))
        last = k == ITERS - 1
        here = w[k]

        def inner(t, odd):
            terms = []
            for g in range(GROUP):
                i = t * GROUP + g
                c = here[i + 1, pl.ds(TOP, NJ)]
                f = cz[i]
                bw = cx[i] * here[i, pl.ds(TOP, NJ)] + cx[i + 1] * here[i + 2, pl.ds(TOP, NJ)]
                bw = bw + cy[i, pl.ds(TOP - 1, NJ)] * here[i + 1, pl.ds(TOP - 1, NJ)]
                bw = bw + cy[i, pl.ds(TOP, NJ)] * here[i + 1, pl.ds(TOP + 1, NJ)]
                nxt = join([pltpu.roll(a, NK - 1, 1) for a in tiles(c)])
                prv = join([pltpu.roll(a, 1, 1) for a in tiles(f * c)])
                bw = bw + (f * nxt + prv)
                part[i] = bw
                terms += tiles(c * bw)
            return accumulate(odd, terms)

        odd = lax.fori_loop(0, NI // GROUP, inner, (zero_acc, zero_acc))

        halo_wait(k + 1, range(6))
        flux = mul(zcoef, opposite_faces(zrecv[k, 1], zrecv[k, 0]))
        terms = mul(flux, faces)
        for s in range(2):
            side = ycoef[s] * yrecv[k, s]
            yf[s] = side
            terms += tiles(side * ysend[k, s])
            side = xcoef[s] * xrecv[k, s]
            edge = (0, NI - 1)[s]
            terms += tiles(side * here[edge + 1, pl.ds(TOP, NJ)])
            if not last:
                part[edge] = part[edge] + side
        while len(terms) & (len(terms) - 1):
            terms.append(zero_acc)
        moments.append(accumulate(odd, terms))
        if last:
            break
        there = w[k + 1]

        def outer(t, carry):
            faces, even = carry
            terms = []
            for g in range(GROUP):
                i = t * GROUP + g
                row = pl.ds(i, 1)
                bw = add_rows(tiles(part[i]), yf, i)
                bw = [a + b for a, b in zip(bw, at_ends(flux, i))]
                new = mul(bw, tiles(dinv[i]))
                there[i + 1, pl.ds(TOP, NJ)] = join(new)
                ysend[k + 1, 0, row] = new[0][0:1]
                ysend[k + 1, 1, row] = new[7][7:8]
                faces = pack(faces, new, i)
                terms += mul(bw, new)
            return faces, accumulate(even, terms)

        faces, even = lax.fori_loop(0, NI // GROUP, outer, (no_faces, (zero_acc, zero_acc)))
        moments.append(even)

    row8 = rows((8, NK))
    lane8 = lanes((8, NK))
    hi = zero_acc
    lo = zero_acc
    for m, acc in enumerate(moments):
        for shift in (4, 2, 1):
            acc = df_add(acc, (pltpu.roll(acc[0], shift, 0), pltpu.roll(acc[1], shift, 0)))
        hi = jnp.where(row8 == m, acc[0], hi)
        lo = jnp.where(row8 == m, acc[1], lo)
    total = (hi, lo)
    for shift in (64, 32, 16, 8, 4, 2, 1):
        total = df_add(total, (pltpu.roll(total[0], shift, 1), pltpu.roll(total[1], shift, 1)))

    plane_to = [{"gy": lax.rem(me[1] + dy, 4), "gz": lax.rem(me[2] + dz, 4)} for dy, dz in PLANE]
    line_to = [{"gx": lax.rem(me[0] + o, 8)} for o in range(1, 8)]
    for stage, (peers, landing) in enumerate(((plane_to, a_recv0), (line_to, a_recv1))):
        a_send[stage] = jnp.where(lane8 < 64, total[0], total[1])
        copies = [
            remote(a_send.at[stage], landing.at[n], as_sem.at[stage, n], ar_sem.at[stage, n], dev)
            for n, dev in enumerate(peers)
        ]
        for c in copies:
            c.start()
        for c in copies:
            c.wait_recv()
        terms = [total]
        for n in range(len(peers)):
            x = landing[n]
            y = pltpu.roll(x, 64, 1)
            terms.append((jnp.where(lane8 < 64, x, y), jnp.where(lane8 < 64, y, x)))
        while len(terms) > 1:
            terms = [
                df_add(terms[t], terms[t + 1]) if t + 1 < len(terms) else terms[t]
                for t in range(0, len(terms), 2)
            ]
        total = terms[0]
        for c in copies:
            c.wait_send()

    nu = [(total[0][m : m + 1], total[1][m : m + 1]) for m in range(2 * ITERS)]
    coef = solve4(nu)

    def combine(parts):
        total = coef[0] * parts[0]
        for c, x in zip(coef[1:], parts[1:]):
            total = total + c * x
        return total

    pe = [opposite_faces(zrecv[k, 1], zrecv[k, 0]) for k in range(ITERS)]
    pe = [combine(list(parts)) for parts in zip(*pe)]
    pe = [jnp.where(odd_lane, -a, a) for a in pe]
    for s in range(2):
        pp[(0, NI + 1)[s], pl.ds(TOP, NJ)] = combine([xrecv[k, s] for k in range(ITERS)])
        yf[s] = combine([yrecv[k, s] for k in range(ITERS)])

    def keep(f, i, x):
        hi, lo = split(x)
        rr = pl.ds(pl.multiple_of((i // 8) * NJ, NJ), NJ)
        cc = pl.ds(pl.multiple_of(lax.rem(i, 8) * NK, NK), NK)
        xh[f, rr, cc] = hi
        xl[f, rr, cc] = lo

    def press(t, _):
        for g in range(GROUP):
            i = t * GROUP + g
            pp[i + 1, pl.ds(TOP - 1, 1)] = yf[0, pl.ds(i, 1)]
            pp[i + 1, pl.ds(TOP + NJ, 1)] = yf[1, pl.ds(i, 1)]
            x = combine([ref[i + 1, pl.ds(TOP, NJ)] for ref in w])
            pp[i + 1, pl.ds(TOP, NJ)] = x
            pst[i] = x
            keep(3, i, x)
        return 0

    lax.fori_loop(0, NI // GROUP, press, 0)

    def fix(f):
        def body(t, _):
            for g in range(GROUP):
                i = t * GROUP + g
                n = ip[i + 1, pl.ds(TOP, NJ)]
                if f == 0:
                    g_ = pp[i + 2, pl.ds(TOP, NJ)] - pp[i, pl.ds(TOP, NJ)]
                    x = vx[i + 1]
                elif f == 1:
                    g_ = pp[i + 1, pl.ds(TOP + 1, NJ)] - pp[i + 1, pl.ds(TOP - 1, NJ)]
                    x = vy[i, pl.ds(TOP, NJ)]
                else:
                    c = tiles(pp[i + 1, pl.ds(TOP, NJ)])
                    g_ = join(ahead(c)) - join(behind(c)) + join(at_ends(pe, i))
                    x = vz[i]
                x = x - n * (0.5 * g_)
                cst[f, i] = x
                keep(f, i, x)
            return 0

        lax.fori_loop(0, NI // GROUP, body, 0)

    def ring(axis, way):
        a = AXES.index(axis)
        n = SIZES[a]
        to = lax.rem(me[a] + (n + way), n)
        back = lax.rem(me[a] + (n - way), n)
        opposite = lax.rem(me[a] + 2, n)
        return to, back, opposite

    def rows16(m):
        return pl.ds(pl.multiple_of(m * 16, 16), 16)

    def stage_refs(f, stage):
        axis, way = ROUTES[f]
        slot = 0 if way == 1 else 1
        if stage == 0:
            if axis == "gz":
                return axis, way, (lambda m: u.at[f, m]), za_in.at[slot], za_acc.at[slot], za_dir.at[slot], za_out.at[slot]
            return axis, way, (lambda m: u.at[f, :, :, rows16(m)]), ya_in.at[slot], ya_acc.at[slot], ya_dir.at[slot], ya_out.at[slot]
        other = "gy" if axis == "gz" else "gz"
        if axis == "gz":
            chunk = lambda m: b_src_z.at[slot, :, rows16(m)]
        else:
            chunk = lambda m: b_src_y.at[slot, m]
        return other, way, chunk, b_in.at[f], b_acc.at[f], b_dir.at[f], b_out.at[f]

    def stage_copies(f, stage):
        axis, way, chunk, r_in, r_acc, r_dir, r_out = stage_refs(f, stage)
        to, back, opposite = ring(axis, way)
        sems = lambda n: (rs_sem.at[f, stage, n], rr_sem.at[f, stage, n])
        return (
            remote(chunk(opposite), r_in, *sems(0), {axis: to}),
            remote(chunk(back), r_dir, *sems(1), {axis: back}),
            remote(r_out, r_acc, *sems(2), {axis: to}),
        )

    def stage_open(f, stage):
        far, near, _ = stage_copies(f, stage)
        far.start()
        near.start()
        pending.append(far.wait_send)
        pending.append(near.wait_send)

    def stage_relay(f, stage):
        axis, way, chunk, r_in, r_acc, r_dir, r_out = stage_refs(f, stage)
        to, back, opposite = ring(axis, way)
        far, near, relay = stage_copies(f, stage)
        far.wait_recv()
        r_out[...] = r_in[...] + chunk(to)[...]
        relay.start()
        pending.append(relay.wait_send)

    def stage_close(f, stage):
        axis, way, chunk, r_in, r_acc, r_dir, r_out = stage_refs(f, stage)
        far, near, relay = stage_copies(f, stage)
        near.wait_recv()
        relay.wait_recv()
        return chunk(me[AXES.index(axis)])[...] + r_acc[...] + r_dir[...]

    def contract(f):
        wh, wl = wz_hi[...], wz_lo[...]
        a, b = xh[f], xl[f]
        for half in range(2):
            cols = slice(256 * half, 256 * half + 256)
            z = dot(a, wh[:, cols]) + dot(b, wh[:, cols]) + dot(a, wl[:, cols])
            for g in range(4):
                hi, lo = split(z[NJ * g : NJ * g + NJ])
                y = dot(fyt[...], jnp.concatenate([hi, hi, lo], axis=0))
                u[f, 2 * half, g] = y[:, :128]
                u[f, 2 * half + 1, g] = y[:, 128:]

    stores = [pltpu.make_async_copy(pst, out_p, out_sem.at[3])]
    stores[0].start()
    pending.append(stores[0].wait)
    for f in ORDER:
        if f != 3:
            fix(f)
            stores.append(pltpu.make_async_copy(cst.at[f], out_c.at[f], out_sem.at[f]))
            stores[-1].start()
            pending.append(stores[-1].wait)
        contract(f)
        stage_open(f, 0)
    for f in ORDER:
        stage_relay(f, 0)
    for f in ORDER:
        whole = stage_close(f, 0)
        slot = 0 if ROUTES[f][1] == 1 else 1
        if ROUTES[f][0] == "gz":
            b_src_z[slot] = whole
        else:
            b_src_y[slot] = whole
        stage_open(f, 1)
    for f in ORDER:
        stage_relay(f, 1)
    for f in ORDER:
        whole = stage_close(f, 1)
        for g in range(4):
            ysc[16 * f : 16 * f + 16, 128 * g : 128 * g + 128] = whole[g]

    hi, lo = split(ysc[...])

    def last_dot(m, _):
        v[m] = dot(hi, k_hi[m]) + dot(lo, k_hi[m]) + dot(hi, k_lo[m])
        return 0

    lax.fori_loop(0, 8, last_dot, 0)
    copies = [
        remote(v.at[lax.rem(me[0] + o, 8)], v_recv.at[o - 1], xs_sem.at[o - 1], xr_sem.at[o - 1], line_to[o - 1])
        for o in range(1, 8)
    ]
    for c in copies:
        c.start()
        pending.append(c.wait_send)
    total = v[me[0]]
    for o in range(1, 8):
        copies[o - 1].wait_recv()
        total = total + v_recv[o - 1]
    for a in range(8):
        moved = total if a == 0 else pltpu.roll(total, 128 - 16 * a, 1)
        for f in range(4):
            out_core[a, f] = moved[16 * f : 16 * f + 16, :16]

    for wait in pending:
        wait()


def per_device(velocity, inv_density, factor_x, factor_y, factor_z):
    vmem = pl.BlockSpec(memory_space=pltpu.VMEM)
    hbm = pl.BlockSpec(memory_space=pl.ANY)
    tall = TOP + NJ + 8
    dma = pltpu.SemaphoreType.DMA
    scratch = [
        pltpu.VMEM((NI + 2, NJ, NK), F32),
        pltpu.VMEM((NI, tall, NK), F32),
        pltpu.VMEM((NI, NJ, NK), F32),
        pltpu.VMEM((NI + 2, tall, NK), F32),
        pltpu.VMEM((NI + 2, tall, NK), F32),
        pltpu.VMEM((NI + 2, tall, NK), F32),
        pltpu.VMEM((NI + 2, tall, NK), F32),
        pltpu.VMEM((NI + 2, tall, NK), F32),
        pltpu.VMEM((NI + 1, NJ, NK), F32),
        pltpu.VMEM((NI, tall, NK), F32),
        pltpu.VMEM((NI, NJ, NK), F32),
        pltpu.VMEM((NI, NJ, NK), F32),
        pltpu.VMEM((NI + 2, tall, NK), F32),
        pltpu.VMEM((NI, NJ, NK), F32),
        pltpu.VMEM((3, NI, NJ, NK), F32),
        pltpu.VMEM((NI, NJ, NK), F32),
        pltpu.VMEM((ITERS, 2, NJ, NK), F32),
        pltpu.VMEM((2, 2, NJ, NK), F32),
        pltpu.VMEM((2, NJ, NK), F32),
        pltpu.VMEM((ITERS, 2, NI, NK), F32),
        pltpu.VMEM((ITERS, 2, NI, NK), F32),
        pltpu.VMEM((2, 2, NI, NK), F32),
        pltpu.VMEM((2, NI, NK), F32),
        pltpu.VMEM((2, NI, NK), F32),
        pltpu.VMEM((2, NI, NK), F32),
        pltpu.VMEM((2, NI, NK), F32),
        pltpu.VMEM((ITERS, 32, NK), F32),
        pltpu.VMEM((ITERS, 2, 32, NK), F32),
        pltpu.VMEM((2, 32, NK), F32),
        pltpu.VMEM((2, 2, 32, NK), F32),
        pltpu.VMEM((2, 8, NK), F32),
        pltpu.VMEM((len(PLANE), 8, NK), F32),
        pltpu.VMEM((7, 8, NK), F32),
        pltpu.VMEM((1024, 512), BF16),
        pltpu.VMEM((1024, 512), BF16),
        pltpu.VMEM((64, 192), BF16),
        pltpu.VMEM((8, 512, 128), BF16),
        pltpu.VMEM((8, 512, 128), BF16),
        pltpu.VMEM((4, 256, 1024), BF16),
        pltpu.VMEM((4, 256, 1024), BF16),
        pltpu.VMEM((4, 4, 4, 64, 128), F32),
    ]
    scratch += [pltpu.VMEM((2, 4, 64, 128), F32)] * 4
    scratch += [pltpu.VMEM((2, 4, 4, 16, 128), F32)] * 4
    scratch += [pltpu.VMEM((2, 4, 64, 128), F32), pltpu.VMEM((2, 4, 4, 16, 128), F32)]
    scratch += [pltpu.VMEM((4, 4, 16, 128), F32)] * 4
    scratch += [
        pltpu.VMEM((64, 512), F32),
        pltpu.VMEM((8, 64, 128), F32),
        pltpu.VMEM((7, 64, 128), F32),
        dma((6,)),
        dma((4,)),
        dma((5, 6, 2)),
        dma((5, 6, 2)),
        dma((2, len(PLANE))),
        dma((2, len(PLANE))),
        dma((4, 2, 3)),
        dma((4, 2, 3)),
        dma((7,)),
        dma((7,)),
    ]
    return pl.pallas_call(
        kernel,
        out_shape=(
            jax.ShapeDtypeStruct(inv_density.shape, F32),
            jax.ShapeDtypeStruct(velocity.shape, F32),
            jax.ShapeDtypeStruct((8, 4, 16, 16), F32),
        ),
        in_specs=[hbm, hbm, vmem, vmem, vmem],
        out_specs=(hbm, hbm, vmem),
        scratch_shapes=scratch,
        compiler_params=pltpu.CompilerParams(
            collective_id=0, has_side_effects=True, vmem_limit_bytes=60 * 1024 * 1024
        ),
    )(velocity, inv_density, factor_x, factor_y, factor_z.T)


def solution(mesh):
    placed = (
        P(None, "gx", "gy", "gz"),
        P("gx", "gy", "gz"),
        P("gx", None),
        P("gy", None),
        P("gz", None),
    )
    return jax.shard_map(
        per_device,
        mesh=mesh,
        in_specs=placed,
        out_specs=(P("gx", "gy", "gz"), P(None, "gx", "gy", "gz"), P("gx", None, "gy", "gz")),
        check_vma=False,
    )
```

```python
import jax
import jax.numpy as jnp
from jax import lax
from jax.experimental import pallas as pl
from jax.experimental.pallas import tpu as pltpu
from jax.sharding import PartitionSpec as P

ITERS = 4
SHIFT = 0.1
MESH = pl.DeviceIdType.MESH
F32 = jnp.float32
BF16 = jnp.bfloat16
NI, NJ, NK = 32, 64, 128
TOP = 8
AXES = ("gx", "gy", "gz")
SIZES = (8, 4, 4)
PLANE = [(dy, dz) for dy in range(4) for dz in range(4) if dy or dz]
ROUTES = {3: ("gz", 1), 1: ("gy", 1), 0: ("gz", -1), 2: ("gy", -1)}
ORDER = (3, 1, 0, 2)
TINY = 1e-11


def two_sum(a, b):
    s = a + b
    t = s - a
    return s, (a - (s - t)) + (b - t)


def quick(a, b):
    s = a + b
    return s, b - (s - a)


def df_add(x, y):
    s, e = two_sum(x[0], y[0])
    return quick(s, e + (x[1] + y[1]))


def exact_sum(x):
    def total(a):
        return jnp.sum(jnp.sum(a, axis=0, keepdims=True), axis=1, keepdims=True)

    big = 4.0 * total(jnp.abs(x[0]))
    coarse = (x[0] + big) - big
    return quick(total(coarse), total((x[0] - coarse) + x[1]))


def df_neg(x):
    return -x[0], -x[1]


def halves(a):
    t = 4097.0 * a
    h = t - (t - a)
    return h, a - h


def df_mul(x, y):
    p = x[0] * y[0]
    ah, al = halves(x[0])
    bh, bl = halves(y[0])
    e = ((ah * bh - p) + ah * bl + al * bh) + al * bl
    return quick(p, e + (x[0] * y[1] + x[1] * y[0]))


def df_recip(x):
    r = 1.0 / x[0]
    one = (jnp.ones_like(r), jnp.zeros_like(r))
    two = (jnp.full_like(r, 2.0), jnp.zeros_like(r))
    y = (r, jnp.zeros_like(r))
    for _ in range(2):
        y = df_mul(y, df_add(two, df_neg(df_mul(x, y))))
    return y


def solve4(nu):
    n = ITERS
    g = [[None] * n for _ in range(n)]
    for i in range(n):
        for j in range(i + 1):
            g[i][j] = df_add(nu[i + j], df_neg(nu[i + j + 1]))
    y = list(nu[:n])
    low = [[None] * n for _ in range(n)]
    inv = []
    for k in range(n):
        pivot = g[k][k]
        start = nu[2 * k][0] - nu[2 * k + 1][0]
        ok = pivot[0] > TINY * start
        safe = (jnp.where(ok, pivot[0], 1.0), jnp.where(ok, pivot[1], 0.0))
        r = df_recip(safe)
        r = (jnp.where(ok, r[0], 0.0), jnp.where(ok, r[1], 0.0))
        inv.append(r)
        for i in range(k + 1, n):
            low[i][k] = df_mul(g[i][k], r)
        for i in range(k + 1, n):
            for j in range(k + 1, i + 1):
                g[i][j] = df_add(g[i][j], df_neg(df_mul(low[i][k], g[j][k])))
            y[i] = df_add(y[i], df_neg(df_mul(low[i][k], y[k])))
    c = [None] * n
    for i in reversed(range(n)):
        v = df_mul(y[i], inv[i])
        for j in range(i + 1, n):
            v = df_add(v, df_neg(df_mul(low[j][i], c[j])))
        c[i] = v
    return [v[0] for v in c]


def lanes(shape):
    return lax.broadcasted_iota(jnp.int32, shape, len(shape) - 1)


def rows(shape):
    return lax.broadcasted_iota(jnp.int32, shape, 0)


def split(x):
    hi = x.astype(BF16)
    return hi, (x - hi.astype(F32)).astype(BF16)


def dot(a, b):
    return lax.dot_general(a, b, (((1,), (0,)), ((), ())), preferred_element_type=F32)


def kernel(
    vel, inv, fx, fy, fz,
    pst, cst, out_core,
    vx, vy, vz, ip, w0, w1, w2, w3, cx, cy, cz, dinv, pp,
    part, xrecv, xrecv0, xcoef, ysend, yrecv, yrecv0, yown, ycoef, yf, yd,
    zsend, zrecv, zsend0, zrecv0,
    a_send, a_recv0, a_recv1,
    wz, fyt, k_hi, k_lo, xh, xl, u,
    za_in, za_acc, za_dir, za_out, ya_in, ya_acc, ya_dir, ya_out,
    b_src_z, b_src_y, b_in, b_acc, b_dir, b_out, ysc, v, v_recv,
    in_sem, hs_sem, hr_sem, as_sem, ar_sem, rs_sem, rr_sem, xs_sem, xr_sem,
):
    w = (w0, w1, w2, w3)
    me = [lax.axis_index(a) for a in AXES]
    has = []
    for a in range(3):
        has += [me[a] > 0, me[a] < SIZES[a] - 1]

    def neighbour(side):
        a = side // 2
        step = 1 if side % 2 else SIZES[a] - 1
        return {AXES[a]: lax.rem(me[a] + step, SIZES[a])}

    def remote(src, dst, ss, rs, dev):
        return pltpu.make_async_remote_copy(
            src_ref=src, dst_ref=dst, send_sem=ss, recv_sem=rs, device_id=dev, device_id_type=MESH
        )

    lane = lanes((8, NK))
    pending = []

    loads = [
        pltpu.make_async_copy(inv, ip.at[pl.ds(1, NI), pl.ds(TOP, NJ)], in_sem.at[0]),
        pltpu.make_async_copy(vel.at[2], vz, in_sem.at[1]),
        pltpu.make_async_copy(vel.at[1], vy.at[:, pl.ds(TOP, NJ)], in_sem.at[2]),
        pltpu.make_async_copy(vel.at[0], vx.at[pl.ds(1, NI)], in_sem.at[3]),
        pltpu.make_async_copy(inv.at[:, 0], yown.at[0], in_sem.at[4]),
        pltpu.make_async_copy(inv.at[:, NJ - 1], yown.at[1], in_sem.at[5]),
    ]
    for c in loads:
        c.start()

    barrier = pltpu.get_barrier_semaphore()
    for side in range(6):
        pl.semaphore_signal(barrier, inc=1, device_id=neighbour(side), device_id_type=MESH)

    def tiles(x):
        return [x[8 * q : 8 * q + 8] for q in range(x.shape[0] // 8)]

    def pack(acc, x, i):
        out = list(acc)
        for q, part in enumerate(x):
            moved = pltpu.roll(part, 2 * i + 1 + 64 * (q // 4), 1)
            out[q % 4] = jnp.where(lane // 2 == i + 32 * (q // 4), moved, out[q % 4])
        return out

    def unpack(faces, i):
        return [pltpu.roll(faces[q % 4], lax.rem(255 - 2 * i - 64 * (q // 4), 128), 1) for q in range(8)]

    odd_lane = lane % 2 == 1
    end_lane = (lane == 0) | (lane == NK - 1)
    sub = rows((8, NK))

    def ahead(x):
        return [jnp.where(lane == NK - 1, 0.0, pltpu.roll(a, NK - 1, 1)) for a in x]

    def behind(x):
        return [jnp.where(lane == 0, 0.0, pltpu.roll(a, 1, 1)) for a in x]

    def opposite_faces(plus, minus):
        return [
            jnp.where(odd_lane, pltpu.roll(b, 1, 1), pltpu.roll(a, NK - 1, 1))
            for a, b in zip(tiles(plus), tiles(minus))
        ]

    def at_ends(faces, i):
        return [jnp.where(end_lane, e, 0.0) for e in unpack(faces, i)]

    def add_rows(x, ref, i):
        low = jnp.where(sub == 0, ref[0, pl.ds(i, 1)], 0.0)
        high = jnp.where(sub == 7, ref[1, pl.ds(i, 1)], 0.0)
        return [x[0] + low] + x[1:7] + [x[7] + high]

    GROUP = 4
    no_faces = [jnp.zeros((8, NK), F32)] * 4
    zero_acc = jnp.zeros((8, NK), F32)

    zero_plane = jnp.zeros((NJ, NK), F32)
    zero_row = jnp.zeros((1, NK), F32)
    for ref in (vx, ip) + w:
        top = 0 if ref is vx else TOP
        for far in (0, NI + 1):
            ref[far, pl.ds(top, NJ)] = zero_plane
    for ref in (vy, ip) + w:
        for i in range(NI):
            for far in (TOP - 1, TOP + NJ):
                ref[i if ref is vy else i + 1, pl.ds(far, 1)] = zero_row
    for s in range(2):
        @pl.when(jnp.logical_not(has[s]))
        def _():
            xrecv0[s] = jnp.zeros((2, NJ, NK), F32)
            for k in range(ITERS):
                xrecv[k, s] = zero_plane

        @pl.when(jnp.logical_not(has[2 + s]))
        def _():
            yrecv0[s] = jnp.zeros((2, NI, NK), F32)
            for k in range(ITERS):
                yrecv[k, s] = jnp.zeros((NI, NK), F32)

        @pl.when(jnp.logical_not(has[4 + s]))
        def _():
            zrecv0[s] = jnp.zeros((2, 32, NK), F32)
            for k in range(ITERS):
                zrecv[k, s] = jnp.zeros((32, NK), F32)

    for c in loads[:2]:
        c.wait()

    def face0(t, carry):
        a, b = carry
        for g in range(GROUP):
            i = t * GROUP + g
            a = pack(a, tiles(vz[i]), i)
            b = pack(b, tiles(ip[i + 1, pl.ds(TOP, NJ)]), i)
        return a, b

    fu, fn = lax.fori_loop(0, NI // GROUP, face0, (no_faces, no_faces))
    zsend0[0] = jnp.concatenate(fu, axis=0)
    zsend0[1] = jnp.concatenate(fn, axis=0)
    pl.semaphore_wait(barrier, 6)

    def halo(r, side, landing):
        s, t = side % 2, landing % 2
        ax = side // 2
        if ax == 0:
            if r == 0:
                edge = (0, NI - 1)[s]
                pairs = [(vel.at[0, edge], xrecv0.at[t, 0]), (inv.at[edge], xrecv0.at[t, 1])]
            else:
                pairs = [(w[r - 1].at[(1, NI)[s], pl.ds(TOP, NJ)], xrecv.at[r - 1, t])]
        elif ax == 1:
            if r == 0:
                edge = (0, NJ - 1)[s]
                pairs = [(vel.at[1, :, edge], yrecv0.at[t, 0]), (inv.at[:, edge], yrecv0.at[t, 1])]
            else:
                pairs = [(ysend.at[r - 1, s], yrecv.at[r - 1, t])]
        elif r == 0:
            pairs = [(zsend0, zrecv0.at[t])]
        else:
            pairs = [(zsend.at[r - 1], zrecv.at[r - 1, t])]
        return [
            remote(a, b, hs_sem.at[r, side, n], hr_sem.at[r, landing, n], neighbour(side))
            for n, (a, b) in enumerate(pairs)
        ]

    def halo_start(r, sides):
        pending.append(lambda: halo_sent(r, sides))
        for side in sides:
            @pl.when(has[side])
            def _():
                for c in halo(r, side, side ^ 1):
                    c.start()

    def halo_wait(r, sides):
        for side in sides:
            @pl.when(has[side])
            def _():
                for c in halo(r, side, side):
                    c.wait_recv()

    def halo_sent(r, sides):
        for side in sides:
            @pl.when(has[side])
            def _():
                for c in halo(r, side, side ^ 1):
                    c.wait_send()

    halo_start(0, range(6))

    for c in loads[2:]:
        c.wait()

    def accumulate(acc, parts):
        while len(parts) > 1:
            parts = [parts[n] + parts[n + 1] for n in range(0, len(parts), 2)]
        s, e = two_sum(acc[0], parts[0])
        return s, acc[1] + e

    def mul(a, b):
        return [x * y for x, y in zip(a, b)]

    def join(x):
        return jnp.concatenate(x, axis=0)

    def join_edges(ref):
        return jnp.stack([ref[1, pl.ds(TOP, NJ)], ref[NI, pl.ds(TOP, NJ)]])

    cx[0] = zero_plane

    def inner0(t, _):
        for g in range(GROUP):
            i = t * GROUP + g
            n = ip[i + 1, pl.ds(TOP, NJ)]
            xf = ip[i + 2, pl.ds(TOP, NJ)]
            yn = ip[i + 1, pl.ds(TOP + 1, NJ)]
            nt = tiles(n)
            zn = ahead(nt)
            cx[i + 1] = 0.5 * (n + xf)
            cy[i, pl.ds(TOP, NJ)] = 0.5 * (n + yn)
            cy[i, pl.ds(TOP - 1, 1)] = zero_row
            cz[i] = join([jnp.where(lane == NK - 1, 0.0, 0.5 * (a + b)) for a, b in zip(nt, zn)])
            around = (xf + ip[i, pl.ds(TOP, NJ)]) + (yn + ip[i + 1, pl.ds(TOP - 1, NJ)])
            around = around + (join(zn) + join(behind(nt)))
            dinv[i] = (SHIFT + 3.0 * n) + 0.5 * around
            at = tiles(vz[i])
            div = (vx[i + 2] - vx[i]) + (vy[i, pl.ds(TOP + 1, NJ)] - vy[i, pl.ds(TOP - 1, NJ)])
            part[i] = div + (join(ahead(at)) - join(behind(at)))
        return 0

    lax.fori_loop(0, NI // GROUP, inner0, 0)

    halo_wait(0, range(6))

    xcoef[...] = 0.5 * (xrecv0[:, 1] + join_edges(ip))
    ycoef[...] = 0.5 * (yrecv0[:, 1] + yown[...])
    hn = opposite_faces(zrecv0[1, 1], zrecv0[0, 1])
    hu = opposite_faces(zrecv0[1, 0], zrecv0[0, 0])
    hu = [jnp.where(odd_lane, -a, a) for a in hu]
    zcoef = [0.5 * (a + b) for a, b in zip(hn, fn)]
    yd[...] = 0.5 * yrecv0[:, 1]
    yf[0] = -yrecv0[0, 0]
    yf[1] = yrecv0[1, 0]
    hn = [0.5 * a for a in hn]
    dinv[0] = dinv[0] + 0.5 * xrecv0[0, 1]
    dinv[NI - 1] = dinv[NI - 1] + 0.5 * xrecv0[1, 1]
    part[0] = part[0] - xrecv0[0, 0]
    part[NI - 1] = part[NI - 1] + xrecv0[1, 0]

    def first(t, carry):
        faces, acc = carry
        terms = []
        for g in range(GROUP):
            i = t * GROUP + g
            row = pl.ds(i, 1)
            d = add_rows(tiles(dinv[i]), yd, i)
            d = [a + b for a, b in zip(d, at_ends(hn, i))]
            b = add_rows(tiles(part[i]), yf, i)
            b = [-0.5 * (x + y) for x, y in zip(b, at_ends(hu, i))]
            di = [1.0 / x for x in d]
            new = mul(b, di)
            dinv[i] = join(di)
            w0[i + 1, pl.ds(TOP, NJ)] = join(new)
            ysend[0, 0, row] = new[0][0:1]
            ysend[0, 1, row] = new[7][7:8]
            faces = pack(faces, new, i)
            terms += mul(b, new)
        return faces, accumulate(acc, terms)

    faces, acc = lax.fori_loop(0, NI // GROUP, first, (no_faces, (zero_acc, zero_acc)))
    moments = [acc]

    for k in range(ITERS):
        zsend[k] = join(faces)
        halo_start(k + 1, range(6))
        last = k == ITERS - 1
        here = w[k]

        def inner(t, odd):
            terms = []
            for g in range(GROUP):
                i = t * GROUP + g
                c = here[i + 1, pl.ds(TOP, NJ)]
                f = cz[i]
                bw = cx[i] * here[i, pl.ds(TOP, NJ)] + cx[i + 1] * here[i + 2, pl.ds(TOP, NJ)]
                bw = bw + cy[i, pl.ds(TOP - 1, NJ)] * here[i + 1, pl.ds(TOP - 1, NJ)]
                bw = bw + cy[i, pl.ds(TOP, NJ)] * here[i + 1, pl.ds(TOP + 1, NJ)]
                nxt = join([pltpu.roll(a, NK - 1, 1) for a in tiles(c)])
                prv = join([pltpu.roll(a, 1, 1) for a in tiles(f * c)])
                bw = bw + (f * nxt + prv)
                part[i] = bw
                terms += tiles(c * bw)
            return accumulate(odd, terms)

        odd = lax.fori_loop(0, NI // GROUP, inner, (zero_acc, zero_acc))

        halo_wait(k + 1, range(6))
        flux = mul(zcoef, opposite_faces(zrecv[k, 1], zrecv[k, 0]))
        terms = mul(flux, faces)
        for s in range(2):
            side = ycoef[s] * yrecv[k, s]
            yf[s] = side
            terms += tiles(side * ysend[k, s])
            side = xcoef[s] * xrecv[k, s]
            edge = (0, NI - 1)[s]
            terms += tiles(side * here[edge + 1, pl.ds(TOP, NJ)])
            if not last:
                part[edge] = part[edge] + side
        while len(terms) & (len(terms) - 1):
            terms.append(zero_acc)
        moments.append(accumulate(odd, terms))
        if last:
            break
        there = w[k + 1]

        def outer(t, carry):
            faces, even = carry
            terms = []
            for g in range(GROUP):
                i = t * GROUP + g
                row = pl.ds(i, 1)
                bw = add_rows(tiles(part[i]), yf, i)
                bw = [a + b for a, b in zip(bw, at_ends(flux, i))]
                new = mul(bw, tiles(dinv[i]))
                there[i + 1, pl.ds(TOP, NJ)] = join(new)
                ysend[k + 1, 0, row] = new[0][0:1]
                ysend[k + 1, 1, row] = new[7][7:8]
                faces = pack(faces, new, i)
                terms += mul(bw, new)
            return faces, accumulate(even, terms)

        faces, even = lax.fori_loop(0, NI // GROUP, outer, (no_faces, (zero_acc, zero_acc)))
        moments.append(even)

    def build_operands():
        fzp = jnp.concatenate([fz[...], jnp.zeros((64, NK), F32)], axis=0).T
        hi, lo = split(jnp.concatenate([fzp, pltpu.roll(fzp, 64, 1)], axis=0))
        wz[...] = jnp.concatenate([hi, lo], axis=1)
        fyp = jnp.concatenate([fy[...], jnp.zeros((NJ, 64), F32)], axis=1)
        hi, lo = split(fyp.T[:64])
        fyt[...] = jnp.concatenate([hi, lo, hi], axis=1)
        fx_hi, fx_lo = split(fx[...])
        row = rows((512, NI))
        plane = (row // 128) * 8 + ((row % 64) // 16) * 2 + (row % 128) // 64
        rep = (plane == lanes((512, NI))).astype(F32).astype(BF16)
        same = (rows((512, 128)) % 16) == (lanes((512, 128)) % 16)

        def build_x(m, _):
            pick = (rows((64, 128)) == 8 * m + lanes((64, 128)) // 16).astype(F32).astype(BF16)
            for part_, dst in ((fx_hi, k_hi), (fx_lo, k_lo)):
                wide = dot(part_, pick).astype(BF16)
                dst[m] = jnp.where(same, dot(rep, wide), 0.0).astype(BF16)
            return 0

        lax.fori_loop(0, 8, build_x, 0)

    row8 = rows((8, NK))
    lane8 = lanes((8, NK))
    hi = zero_acc
    lo = zero_acc
    for m, acc in enumerate(moments):
        acc = exact_sum(acc)
        hi = jnp.where(row8 == m, acc[0], hi)
        lo = jnp.where(row8 == m, acc[1], lo)
    total = (hi, lo)

    plane_to = [{"gy": lax.rem(me[1] + dy, 4), "gz": lax.rem(me[2] + dz, 4)} for dy, dz in PLANE]
    line_to = [{"gx": lax.rem(me[0] + o, 8)} for o in range(1, 8)]
    for stage, (peers, landing) in enumerate(((plane_to, a_recv0), (line_to, a_recv1))):
        a_send[stage] = jnp.where(lane8 < 64, total[0], total[1])
        copies = [
            remote(a_send.at[stage], landing.at[n], as_sem.at[stage, n], ar_sem.at[stage, n], dev)
            for n, dev in enumerate(peers)
        ]
        for c in copies:
            c.start()
        if stage == 0:
            build_operands()
        for c in copies:
            c.wait_recv()
        terms = [total]
        for n in range(len(peers)):
            x = landing[n]
            y = pltpu.roll(x, 64, 1)
            terms.append((jnp.where(lane8 < 64, x, y), jnp.where(lane8 < 64, y, x)))
        while len(terms) > 1:
            terms = [
                df_add(terms[t], terms[t + 1]) if t + 1 < len(terms) else terms[t]
                for t in range(0, len(terms), 2)
            ]
        total = terms[0]
        for c in copies:
            c.wait_send()

    nu = [(total[0][m : m + 1], total[1][m : m + 1]) for m in range(2 * ITERS)]
    coef = solve4(nu)

    def combine(parts):
        total = coef[0] * parts[0]
        for c, x in zip(coef[1:], parts[1:]):
            total = total + c * x
        return total

    pe = [opposite_faces(zrecv[k, 1], zrecv[k, 0]) for k in range(ITERS)]
    pe = [combine(list(parts)) for parts in zip(*pe)]
    pe = [jnp.where(odd_lane, -a, a) for a in pe]
    for s in range(2):
        pp[(0, NI + 1)[s], pl.ds(TOP, NJ)] = combine([xrecv[k, s] for k in range(ITERS)])
        yf[s] = combine([yrecv[k, s] for k in range(ITERS)])

    def keep(f, i, x, odd_plane):
        hi, lo = split(x)
        rr = pl.ds(pl.multiple_of((i // 2) * NJ, NJ), NJ)
        cc = slice(NK * odd_plane, NK * odd_plane + NK)
        xh[f, rr, cc] = hi
        xl[f, rr, cc] = lo

    def press(t, _):
        for g in range(GROUP):
            i = t * GROUP + g
            pp[i + 1, pl.ds(TOP - 1, 1)] = yf[0, pl.ds(i, 1)]
            pp[i + 1, pl.ds(TOP + NJ, 1)] = yf[1, pl.ds(i, 1)]
            x = combine([ref[i + 1, pl.ds(TOP, NJ)] for ref in w])
            pp[i + 1, pl.ds(TOP, NJ)] = x
            pst[i] = x
            keep(3, i, x, g % 2)
        return 0

    lax.fori_loop(0, NI // GROUP, press, 0)

    def fix(f):
        def body(t, _):
            for g in range(GROUP):
                i = t * GROUP + g
                n = ip[i + 1, pl.ds(TOP, NJ)]
                if f == 0:
                    g_ = pp[i + 2, pl.ds(TOP, NJ)] - pp[i, pl.ds(TOP, NJ)]
                    x = vx[i + 1]
                elif f == 1:
                    g_ = pp[i + 1, pl.ds(TOP + 1, NJ)] - pp[i + 1, pl.ds(TOP - 1, NJ)]
                    x = vy[i, pl.ds(TOP, NJ)]
                else:
                    c = tiles(pp[i + 1, pl.ds(TOP, NJ)])
                    g_ = join(ahead(c)) - join(behind(c)) + join(at_ends(pe, i))
                    x = vz[i]
                x = x - n * (0.5 * g_)
                cst[f, i] = x
                keep(f, i, x, g % 2)
            return 0

        lax.fori_loop(0, NI // GROUP, body, 0)

    def ring(axis, way):
        a = AXES.index(axis)
        n = SIZES[a]
        to = lax.rem(me[a] + (n + way), n)
        back = lax.rem(me[a] + (n - way), n)
        opposite = lax.rem(me[a] + 2, n)
        return to, back, opposite

    def rows16(m):
        return pl.ds(pl.multiple_of(m * 16, 16), 16)

    def stage_refs(f, stage):
        axis, way = ROUTES[f]
        slot = 0 if way == 1 else 1
        if stage == 0:
            if axis == "gz":
                return axis, way, (lambda m: u.at[f, m]), za_in.at[slot], za_acc.at[slot], za_dir.at[slot], za_out.at[slot]
            return axis, way, (lambda m: u.at[f, :, :, rows16(m)]), ya_in.at[slot], ya_acc.at[slot], ya_dir.at[slot], ya_out.at[slot]
        other = "gy" if axis == "gz" else "gz"
        if axis == "gz":
            chunk = lambda m: b_src_z.at[slot, :, rows16(m)]
        else:
            chunk = lambda m: b_src_y.at[slot, m]
        return other, way, chunk, b_in.at[f], b_acc.at[f], b_dir.at[f], b_out.at[f]

    def stage_copies(f, stage):
        axis, way, chunk, r_in, r_acc, r_dir, r_out = stage_refs(f, stage)
        to, back, opposite = ring(axis, way)
        sems = lambda n: (rs_sem.at[f, stage, n], rr_sem.at[f, stage, n])
        return (
            remote(chunk(opposite), r_in, *sems(0), {axis: to}),
            remote(chunk(back), r_dir, *sems(1), {axis: back}),
            remote(r_out, r_acc, *sems(2), {axis: to}),
        )

    def stage_open(f, stage):
        far, near, _ = stage_copies(f, stage)
        far.start()
        near.start()
        pending.append(far.wait_send)
        pending.append(near.wait_send)

    def stage_relay(f, stage):
        axis, way, chunk, r_in, r_acc, r_dir, r_out = stage_refs(f, stage)
        to, back, opposite = ring(axis, way)
        far, near, relay = stage_copies(f, stage)
        far.wait_recv()
        r_out[...] = r_in[...] + chunk(to)[...]
        relay.start()
        pending.append(relay.wait_send)

    def stage_close(f, stage):
        axis, way, chunk, r_in, r_acc, r_dir, r_out = stage_refs(f, stage)
        far, near, relay = stage_copies(f, stage)
        near.wait_recv()
        relay.wait_recv()
        return chunk(me[AXES.index(axis)])[...] + r_acc[...] + r_dir[...]

    block = (lane % 64) // 16

    def contract(f):
        operand = wz[...]
        for g in range(4):
            cut = slice(256 * g, 256 * g + 256)
            both = dot(xh[f, cut], operand)
            z = (both[:, :128] + both[:, 128:]) + dot(xl[f, cut], operand[:, :128])
            done = []
            for h in range(2):
                pair = [z[NJ * n : NJ * n + NJ] for n in (2 * h, 2 * h + 1)]
                hi, lo = split(jnp.concatenate(pair, axis=1))
                y = dot(fyt[...], jnp.concatenate([hi, hi, lo], axis=0))
                done += [tiles(y[:, :128]), tiles(y[:, 128:])]
            for r in range(4):
                out = []
                for q in range(8):
                    acc = done[r][q]
                    for n in range(4):
                        if n != r:
                            moved = pltpu.roll(done[n][q], (16 * (n - r)) % 128, 1)
                            acc = jnp.where(block == n, moved, acc)
                    out.append(acc)
                u[f, r, g] = join(out)

    for f in ORDER:
        if f != 3:
            fix(f)
        contract(f)
        stage_open(f, 0)
    for f in ORDER:
        stage_relay(f, 0)
    for f in ORDER:
        whole = stage_close(f, 0)
        slot = 0 if ROUTES[f][1] == 1 else 1
        if ROUTES[f][0] == "gz":
            b_src_z[slot] = whole
        else:
            b_src_y[slot] = whole
        stage_open(f, 1)
    for f in ORDER:
        stage_relay(f, 1)
    for f in ORDER:
        whole = stage_close(f, 1)
        for g in range(4):
            ysc[16 * f : 16 * f + 16, 128 * g : 128 * g + 128] = whole[g]

    hi, lo = split(ysc[...])

    def last_dot(m, _):
        v[m] = dot(hi, k_hi[m]) + dot(lo, k_hi[m]) + dot(hi, k_lo[m])
        return 0

    lax.fori_loop(0, 8, last_dot, 0)
    copies = [
        remote(v.at[lax.rem(me[0] + o, 8)], v_recv.at[o - 1], xs_sem.at[o - 1], xr_sem.at[o - 1], line_to[o - 1])
        for o in range(1, 8)
    ]
    for c in copies:
        c.start()
        pending.append(c.wait_send)
    total = v[me[0]]
    for o in range(1, 8):
        copies[o - 1].wait_recv()
        total = total + v_recv[o - 1]
    for a in range(8):
        moved = total if a == 0 else pltpu.roll(total, 128 - 16 * a, 1)
        for f in range(4):
            out_core[a, f] = moved[16 * f : 16 * f + 16, :16]

    for wait in pending:
        wait()


def per_device(velocity, inv_density, factor_x, factor_y, factor_z):
    vmem = pl.BlockSpec(memory_space=pltpu.VMEM)
    hbm = pl.BlockSpec(memory_space=pl.ANY)
    tall = TOP + NJ + 8
    dma = pltpu.SemaphoreType.DMA
    scratch = [
        pltpu.VMEM((NI + 2, NJ, NK), F32),
        pltpu.VMEM((NI, tall, NK), F32),
        pltpu.VMEM((NI, NJ, NK), F32),
        pltpu.VMEM((NI + 2, tall, NK), F32),
        pltpu.VMEM((NI + 2, tall, NK), F32),
        pltpu.VMEM((NI + 2, tall, NK), F32),
        pltpu.VMEM((NI + 2, tall, NK), F32),
        pltpu.VMEM((NI + 2, tall, NK), F32),
        pltpu.VMEM((NI + 1, NJ, NK), F32),
        pltpu.VMEM((NI, tall, NK), F32),
        pltpu.VMEM((NI, NJ, NK), F32),
        pltpu.VMEM((NI, NJ, NK), F32),
        pltpu.VMEM((NI + 2, tall, NK), F32),
        pltpu.VMEM((NI, NJ, NK), F32),
        pltpu.VMEM((ITERS, 2, NJ, NK), F32),
        pltpu.VMEM((2, 2, NJ, NK), F32),
        pltpu.VMEM((2, NJ, NK), F32),
        pltpu.VMEM((ITERS, 2, NI, NK), F32),
        pltpu.VMEM((ITERS, 2, NI, NK), F32),
        pltpu.VMEM((2, 2, NI, NK), F32),
        pltpu.VMEM((2, NI, NK), F32),
        pltpu.VMEM((2, NI, NK), F32),
        pltpu.VMEM((2, NI, NK), F32),
        pltpu.VMEM((2, NI, NK), F32),
        pltpu.VMEM((ITERS, 32, NK), F32),
        pltpu.VMEM((ITERS, 2, 32, NK), F32),
        pltpu.VMEM((2, 32, NK), F32),
        pltpu.VMEM((2, 2, 32, NK), F32),
        pltpu.VMEM((2, 8, NK), F32),
        pltpu.VMEM((len(PLANE), 8, NK), F32),
        pltpu.VMEM((7, 8, NK), F32),
        pltpu.VMEM((256, 256), BF16),
        pltpu.VMEM((64, 192), BF16),
        pltpu.VMEM((8, 512, 128), BF16),
        pltpu.VMEM((8, 512, 128), BF16),
        pltpu.VMEM((4, 1024, 256), BF16),
        pltpu.VMEM((4, 1024, 256), BF16),
        pltpu.VMEM((4, 4, 4, 64, 128), F32),
    ]
    scratch += [pltpu.VMEM((2, 4, 64, 128), F32)] * 4
    scratch += [pltpu.VMEM((2, 4, 4, 16, 128), F32)] * 4
    scratch += [pltpu.VMEM((2, 4, 64, 128), F32), pltpu.VMEM((2, 4, 4, 16, 128), F32)]
    scratch += [pltpu.VMEM((4, 4, 16, 128), F32)] * 4
    scratch += [
        pltpu.VMEM((64, 512), F32),
        pltpu.VMEM((8, 64, 128), F32),
        pltpu.VMEM((7, 64, 128), F32),
        dma((6,)),
        dma((5, 6, 2)),
        dma((5, 6, 2)),
        dma((2, len(PLANE))),
        dma((2, len(PLANE))),
        dma((4, 2, 3)),
        dma((4, 2, 3)),
        dma((7,)),
        dma((7,)),
    ]
    pressure, corrected, core = pl.pallas_call(
        kernel,
        out_shape=(
            pltpu.VMEM(inv_density.shape, F32),
            pltpu.VMEM(velocity.shape, F32),
            pltpu.VMEM((8, 4, 16, 16), F32),
        ),
        in_specs=[hbm, hbm, vmem, vmem, vmem],
        out_specs=(vmem, vmem, vmem),
        scratch_shapes=scratch,
        compiler_params=pltpu.CompilerParams(
            collective_id=0, has_side_effects=True, vmem_limit_bytes=52 * 1024 * 1024
        ),
    )(velocity, inv_density, factor_x, factor_y, factor_z.T)
    return pressure, corrected, core


def solution(mesh):
    placed = (
        P(None, "gx", "gy", "gz"),
        P("gx", "gy", "gz"),
        P("gx", None),
        P("gy", None),
        P("gz", None),
    )
    return jax.shard_map(
        per_device,
        mesh=mesh,
        in_specs=placed,
        out_specs=(P("gx", "gy", "gz"), P(None, "gx", "gy", "gz"), P("gx", None, "gy", "gz")),
        check_vma=False,
    )
```

```python
import jax
import jax.numpy as jnp
from jax import lax
from jax.experimental import pallas as pl
from jax.experimental.pallas import tpu as pltpu
from jax.sharding import PartitionSpec as P

ITERS = 4
SHIFT = 0.1
MESH = pl.DeviceIdType.MESH
F32 = jnp.float32
BF16 = jnp.bfloat16
NI, NJ, NK = 32, 64, 128
TOP = 8
AXES = ("gx", "gy", "gz")
SIZES = (8, 4, 4)
PLANE = [(dy, dz) for dy in range(4) for dz in range(4) if dy or dz]
ROUTES = {3: ("gz", 1), 1: ("gy", 1), 0: ("gz", -1), 2: ("gy", -1)}
ORDER = (3, 1, 0, 2)
TINY = 1e-11


def two_sum(a, b):
    s = a + b
    t = s - a
    return s, (a - (s - t)) + (b - t)


def quick(a, b):
    s = a + b
    return s, b - (s - a)


def df_add(x, y):
    s, e = two_sum(x[0], y[0])
    return quick(s, e + (x[1] + y[1]))


def exact_sum(x):
    def total(a):
        return jnp.sum(jnp.sum(a, axis=0, keepdims=True), axis=1, keepdims=True)

    big = 4.0 * total(jnp.abs(x[0]))
    coarse = (x[0] + big) - big
    return quick(total(coarse), total((x[0] - coarse) + x[1]))


def df_neg(x):
    return -x[0], -x[1]


def halves(a):
    t = 4097.0 * a
    h = t - (t - a)
    return h, a - h


def df_mul(x, y):
    p = x[0] * y[0]
    ah, al = halves(x[0])
    bh, bl = halves(y[0])
    e = ((ah * bh - p) + ah * bl + al * bh) + al * bl
    return quick(p, e + (x[0] * y[1] + x[1] * y[0]))


def df_recip(x):
    r = 1.0 / x[0]
    one = (jnp.ones_like(r), jnp.zeros_like(r))
    two = (jnp.full_like(r, 2.0), jnp.zeros_like(r))
    y = (r, jnp.zeros_like(r))
    for _ in range(2):
        y = df_mul(y, df_add(two, df_neg(df_mul(x, y))))
    return y


def solve4(nu):
    n = ITERS
    g = [[None] * n for _ in range(n)]
    for i in range(n):
        for j in range(i + 1):
            g[i][j] = df_add(nu[i + j], df_neg(nu[i + j + 1]))
    y = list(nu[:n])
    low = [[None] * n for _ in range(n)]
    inv = []
    for k in range(n):
        pivot = g[k][k]
        start = nu[2 * k][0] - nu[2 * k + 1][0]
        ok = pivot[0] > TINY * start
        safe = (jnp.where(ok, pivot[0], 1.0), jnp.where(ok, pivot[1], 0.0))
        r = df_recip(safe)
        r = (jnp.where(ok, r[0], 0.0), jnp.where(ok, r[1], 0.0))
        inv.append(r)
        for i in range(k + 1, n):
            low[i][k] = df_mul(g[i][k], r)
        for i in range(k + 1, n):
            for j in range(k + 1, i + 1):
                g[i][j] = df_add(g[i][j], df_neg(df_mul(low[i][k], g[j][k])))
            y[i] = df_add(y[i], df_neg(df_mul(low[i][k], y[k])))
    c = [None] * n
    for i in reversed(range(n)):
        v = df_mul(y[i], inv[i])
        for j in range(i + 1, n):
            v = df_add(v, df_neg(df_mul(low[j][i], c[j])))
        c[i] = v
    return [v[0] for v in c]


def lanes(shape):
    return lax.broadcasted_iota(jnp.int32, shape, len(shape) - 1)


def rows(shape):
    return lax.broadcasted_iota(jnp.int32, shape, 0)


def split(x):
    hi = x.astype(BF16)
    return hi, (x - hi.astype(F32)).astype(BF16)


def dot(a, b):
    return lax.dot_general(a, b, (((1,), (0,)), ((), ())), preferred_element_type=F32)


def kernel(
    vel, inv, fx, fy, fz,
    pst, cst, out_core,
    vx, vy, vz, ip, w0, w1, w2, w3, cx, cy, cz, dinv, pp,
    part, xrecv, xrecv0, xcoef, ysend, yrecv, yrecv0, yown, ycoef, yf, yd,
    zsend, zrecv, zsend0, zrecv0,
    a_send, a_recv0, a_recv1,
    wz, zb, fyt, k_hi, k_lo, xh, xl, u,
    za_in, za_acc, za_dir, za_out, ya_in, ya_acc, ya_dir, ya_out,
    b_src_z, b_src_y, b_in, b_acc, b_dir, b_out, ysc, v, v_recv,
    in_sem, hs_sem, hr_sem, as_sem, ar_sem, rs_sem, rr_sem, xs_sem, xr_sem,
):
    w = (w0, w1, w2, w3)
    me = [lax.axis_index(a) for a in AXES]
    has = []
    for a in range(3):
        has += [me[a] > 0, me[a] < SIZES[a] - 1]

    def neighbour(side):
        a = side // 2
        step = 1 if side % 2 else SIZES[a] - 1
        return {AXES[a]: lax.rem(me[a] + step, SIZES[a])}

    def remote(src, dst, ss, rs, dev):
        return pltpu.make_async_remote_copy(
            src_ref=src, dst_ref=dst, send_sem=ss, recv_sem=rs, device_id=dev, device_id_type=MESH
        )

    lane = lanes((8, NK))
    pending = []

    loads = [
        pltpu.make_async_copy(inv, ip.at[pl.ds(1, NI), pl.ds(TOP, NJ)], in_sem.at[0]),
        pltpu.make_async_copy(vel.at[2], vz, in_sem.at[1]),
        pltpu.make_async_copy(vel.at[1], vy.at[:, pl.ds(TOP, NJ)], in_sem.at[2]),
        pltpu.make_async_copy(vel.at[0], vx.at[pl.ds(1, NI)], in_sem.at[3]),
        pltpu.make_async_copy(inv.at[:, 0], yown.at[0], in_sem.at[4]),
        pltpu.make_async_copy(inv.at[:, NJ - 1], yown.at[1], in_sem.at[5]),
    ]
    for c in loads:
        c.start()

    barrier = pltpu.get_barrier_semaphore()
    for side in range(6):
        pl.semaphore_signal(barrier, inc=1, device_id=neighbour(side), device_id_type=MESH)

    def tiles(x):
        return [x[8 * q : 8 * q + 8] for q in range(x.shape[0] // 8)]

    def pack(acc, x, i):
        out = list(acc)
        for q, part in enumerate(x):
            moved = pltpu.roll(part, 2 * i + 1 + 64 * (q // 4), 1)
            out[q % 4] = jnp.where(lane // 2 == i + 32 * (q // 4), moved, out[q % 4])
        return out

    def unpack(faces, i):
        return [pltpu.roll(faces[q % 4], lax.rem(255 - 2 * i - 64 * (q // 4), 128), 1) for q in range(8)]

    odd_lane = lane % 2 == 1
    end_lane = (lane == 0) | (lane == NK - 1)
    sub = rows((8, NK))

    def ahead(x):
        return [jnp.where(lane == NK - 1, 0.0, pltpu.roll(a, NK - 1, 1)) for a in x]

    def behind(x):
        return [jnp.where(lane == 0, 0.0, pltpu.roll(a, 1, 1)) for a in x]

    def opposite_faces(plus, minus):
        return [
            jnp.where(odd_lane, pltpu.roll(b, 1, 1), pltpu.roll(a, NK - 1, 1))
            for a, b in zip(tiles(plus), tiles(minus))
        ]

    def at_ends(faces, i):
        return [jnp.where(end_lane, e, 0.0) for e in unpack(faces, i)]

    def add_rows(x, ref, i):
        low = jnp.where(sub == 0, ref[0, pl.ds(i, 1)], 0.0)
        high = jnp.where(sub == 7, ref[1, pl.ds(i, 1)], 0.0)
        return [x[0] + low] + x[1:7] + [x[7] + high]

    GROUP = 4
    no_faces = [jnp.zeros((8, NK), F32)] * 4
    zero_acc = jnp.zeros((8, NK), F32)

    zero_plane = jnp.zeros((NJ, NK), F32)
    zero_row = jnp.zeros((1, NK), F32)
    for ref in (vx, ip) + w:
        top = 0 if ref is vx else TOP
        for far in (0, NI + 1):
            ref[far, pl.ds(top, NJ)] = zero_plane
    for ref in (vy, ip) + w:
        for i in range(NI):
            for far in (TOP - 1, TOP + NJ):
                ref[i if ref is vy else i + 1, pl.ds(far, 1)] = zero_row
    for s in range(2):
        @pl.when(jnp.logical_not(has[s]))
        def _():
            xrecv0[s] = jnp.zeros((2, NJ, NK), F32)
            for k in range(ITERS):
                xrecv[k, s] = zero_plane

        @pl.when(jnp.logical_not(has[2 + s]))
        def _():
            yrecv0[s] = jnp.zeros((2, NI, NK), F32)
            for k in range(ITERS):
                yrecv[k, s] = jnp.zeros((NI, NK), F32)

        @pl.when(jnp.logical_not(has[4 + s]))
        def _():
            zrecv0[s] = jnp.zeros((2, 32, NK), F32)
            for k in range(ITERS):
                zrecv[k, s] = jnp.zeros((32, NK), F32)

    for c in loads[:2]:
        c.wait()

    def face0(t, carry):
        a, b = carry
        for g in range(GROUP):
            i = t * GROUP + g
            a = pack(a, tiles(vz[i]), i)
            b = pack(b, tiles(ip[i + 1, pl.ds(TOP, NJ)]), i)
        return a, b

    fu, fn = lax.fori_loop(0, NI // GROUP, face0, (no_faces, no_faces))
    zsend0[0] = jnp.concatenate(fu, axis=0)
    zsend0[1] = jnp.concatenate(fn, axis=0)
    pl.semaphore_wait(barrier, 6)

    def halo(r, side, landing):
        s, t = side % 2, landing % 2
        ax = side // 2
        if ax == 0:
            if r == 0:
                edge = (0, NI - 1)[s]
                pairs = [(vel.at[0, edge], xrecv0.at[t, 0]), (inv.at[edge], xrecv0.at[t, 1])]
            else:
                pairs = [(w[r - 1].at[(1, NI)[s], pl.ds(TOP, NJ)], xrecv.at[r - 1, t])]
        elif ax == 1:
            if r == 0:
                edge = (0, NJ - 1)[s]
                pairs = [(vel.at[1, :, edge], yrecv0.at[t, 0]), (inv.at[:, edge], yrecv0.at[t, 1])]
            else:
                pairs = [(ysend.at[r - 1, s], yrecv.at[r - 1, t])]
        elif r == 0:
            pairs = [(zsend0, zrecv0.at[t])]
        else:
            pairs = [(zsend.at[r - 1], zrecv.at[r - 1, t])]
        return [
            remote(a, b, hs_sem.at[r, side, n], hr_sem.at[r, landing, n], neighbour(side))
            for n, (a, b) in enumerate(pairs)
        ]

    def halo_start(r, sides):
        pending.append(lambda: halo_sent(r, sides))
        for side in sides:
            @pl.when(has[side])
            def _():
                for c in halo(r, side, side ^ 1):
                    c.start()

    def halo_wait(r, sides):
        for side in sides:
            @pl.when(has[side])
            def _():
                for c in halo(r, side, side):
                    c.wait_recv()

    def halo_sent(r, sides):
        for side in sides:
            @pl.when(has[side])
            def _():
                for c in halo(r, side, side ^ 1):
                    c.wait_send()

    halo_start(0, range(6))

    for c in loads[2:]:
        c.wait()

    def accumulate(acc, parts):
        while len(parts) > 1:
            parts = [parts[n] + parts[n + 1] for n in range(0, len(parts), 2)]
        s, e = two_sum(acc[0], parts[0])
        return s, acc[1] + e

    def mul(a, b):
        return [x * y for x, y in zip(a, b)]

    def join(x):
        return jnp.concatenate(x, axis=0)

    def join_edges(ref):
        return jnp.stack([ref[1, pl.ds(TOP, NJ)], ref[NI, pl.ds(TOP, NJ)]])

    cx[0] = zero_plane

    def inner0(t, _):
        for g in range(GROUP):
            i = t * GROUP + g
            n = ip[i + 1, pl.ds(TOP, NJ)]
            xf = ip[i + 2, pl.ds(TOP, NJ)]
            yn = ip[i + 1, pl.ds(TOP + 1, NJ)]
            nt = tiles(n)
            zn = ahead(nt)
            cx[i + 1] = 0.5 * (n + xf)
            cy[i, pl.ds(TOP, NJ)] = 0.5 * (n + yn)
            cy[i, pl.ds(TOP - 1, 1)] = zero_row
            cz[i] = join([jnp.where(lane == NK - 1, 0.0, 0.5 * (a + b)) for a, b in zip(nt, zn)])
            around = (xf + ip[i, pl.ds(TOP, NJ)]) + (yn + ip[i + 1, pl.ds(TOP - 1, NJ)])
            around = around + (join(zn) + join(behind(nt)))
            dinv[i] = (SHIFT + 3.0 * n) + 0.5 * around
            at = tiles(vz[i])
            div = (vx[i + 2] - vx[i]) + (vy[i, pl.ds(TOP + 1, NJ)] - vy[i, pl.ds(TOP - 1, NJ)])
            part[i] = div + (join(ahead(at)) - join(behind(at)))
        return 0

    lax.fori_loop(0, NI // GROUP, inner0, 0)

    halo_wait(0, range(6))

    xcoef[...] = 0.5 * (xrecv0[:, 1] + join_edges(ip))
    ycoef[...] = 0.5 * (yrecv0[:, 1] + yown[...])
    hn = opposite_faces(zrecv0[1, 1], zrecv0[0, 1])
    hu = opposite_faces(zrecv0[1, 0], zrecv0[0, 0])
    hu = [jnp.where(odd_lane, -a, a) for a in hu]
    zcoef = [0.5 * (a + b) for a, b in zip(hn, fn)]
    yd[...] = 0.5 * yrecv0[:, 1]
    yf[0] = -yrecv0[0, 0]
    yf[1] = yrecv0[1, 0]
    hn = [0.5 * a for a in hn]
    dinv[0] = dinv[0] + 0.5 * xrecv0[0, 1]
    dinv[NI - 1] = dinv[NI - 1] + 0.5 * xrecv0[1, 1]
    part[0] = part[0] - xrecv0[0, 0]
    part[NI - 1] = part[NI - 1] + xrecv0[1, 0]

    def first(t, carry):
        faces, acc = carry
        terms = []
        for g in range(GROUP):
            i = t * GROUP + g
            row = pl.ds(i, 1)
            d = add_rows(tiles(dinv[i]), yd, i)
            d = [a + b for a, b in zip(d, at_ends(hn, i))]
            b = add_rows(tiles(part[i]), yf, i)
            b = [-0.5 * (x + y) for x, y in zip(b, at_ends(hu, i))]
            di = [1.0 / x for x in d]
            new = mul(b, di)
            dinv[i] = join(di)
            w0[i + 1, pl.ds(TOP, NJ)] = join(new)
            ysend[0, 0, row] = new[0][0:1]
            ysend[0, 1, row] = new[7][7:8]
            faces = pack(faces, new, i)
            terms += mul(b, new)
        return faces, accumulate(acc, terms)

    faces, acc = lax.fori_loop(0, NI // GROUP, first, (no_faces, (zero_acc, zero_acc)))
    moments = [acc]

    for k in range(ITERS):
        zsend[k] = join(faces)
        halo_start(k + 1, range(6))
        last = k == ITERS - 1
        here = w[k]

        def inner(t, odd):
            terms = []
            for g in range(GROUP):
                i = t * GROUP + g
                c = here[i + 1, pl.ds(TOP, NJ)]
                f = cz[i]
                bw = cx[i] * here[i, pl.ds(TOP, NJ)] + cx[i + 1] * here[i + 2, pl.ds(TOP, NJ)]
                bw = bw + cy[i, pl.ds(TOP - 1, NJ)] * here[i + 1, pl.ds(TOP - 1, NJ)]
                bw = bw + cy[i, pl.ds(TOP, NJ)] * here[i + 1, pl.ds(TOP + 1, NJ)]
                nxt = join([pltpu.roll(a, NK - 1, 1) for a in tiles(c)])
                prv = join([pltpu.roll(a, 1, 1) for a in tiles(f * c)])
                bw = bw + (f * nxt + prv)
                part[i] = bw
                terms += tiles(c * bw)
            return accumulate(odd, terms)

        odd = lax.fori_loop(0, NI // GROUP, inner, (zero_acc, zero_acc))

        halo_wait(k + 1, range(6))
        flux = mul(zcoef, opposite_faces(zrecv[k, 1], zrecv[k, 0]))
        terms = mul(flux, faces)
        for s in range(2):
            side = ycoef[s] * yrecv[k, s]
            yf[s] = side
            terms += tiles(side * ysend[k, s])
            side = xcoef[s] * xrecv[k, s]
            edge = (0, NI - 1)[s]
            terms += tiles(side * here[edge + 1, pl.ds(TOP, NJ)])
            if not last:
                part[edge] = part[edge] + side
        while len(terms) & (len(terms) - 1):
            terms.append(zero_acc)
        moments.append(accumulate(odd, terms))
        if last:
            break
        there = w[k + 1]

        def outer(t, carry):
            faces, even = carry
            terms = []
            for g in range(GROUP):
                i = t * GROUP + g
                row = pl.ds(i, 1)
                bw = add_rows(tiles(part[i]), yf, i)
                bw = [a + b for a, b in zip(bw, at_ends(flux, i))]
                new = mul(bw, tiles(dinv[i]))
                there[i + 1, pl.ds(TOP, NJ)] = join(new)
                ysend[k + 1, 0, row] = new[0][0:1]
                ysend[k + 1, 1, row] = new[7][7:8]
                faces = pack(faces, new, i)
                terms += mul(bw, new)
            return faces, accumulate(even, terms)

        faces, even = lax.fori_loop(0, NI // GROUP, outer, (no_faces, (zero_acc, zero_acc)))
        moments.append(even)

    def build_operands():
        twice = jnp.concatenate([fz[...], fz[...]], axis=0).T
        low_half = lanes((NK, 128)) < 64
        for n in range(4):
            turned = twice if n == 0 else pltpu.roll(twice, 16 * n, 1)
            top = jnp.where(low_half, turned, 0.0)
            hi, lo = split(jnp.concatenate([top, turned - top], axis=0))
            wz[n] = jnp.concatenate([hi, lo], axis=1)
        fyp = jnp.concatenate([fy[...], jnp.zeros((NJ, 64), F32)], axis=1)
        hi, lo = split(fyp.T[:64])
        fyt[...] = jnp.concatenate([hi, lo, hi], axis=1)
        fx_hi, fx_lo = split(fx[...])
        row = rows((512, NI))
        pair = ((row % 64) // 16 + 4 - me[2]) % 4
        plane = (row // 128) * 8 + pair * 2 + (row % 128) // 64
        rep = (plane == lanes((512, NI))).astype(F32).astype(BF16)
        same = (rows((512, 128)) % 16) == (lanes((512, 128)) % 16)

        def build_x(m, _):
            pick = (rows((64, 128)) == 8 * m + lanes((64, 128)) // 16).astype(F32).astype(BF16)
            for part_, dst in ((fx_hi, k_hi), (fx_lo, k_lo)):
                wide = dot(part_, pick).astype(BF16)
                dst[m] = jnp.where(same, dot(rep, wide), 0.0).astype(BF16)
            return 0

        lax.fori_loop(0, 8, build_x, 0)

    row8 = rows((8, NK))
    lane8 = lanes((8, NK))
    hi = zero_acc
    lo = zero_acc
    for m, acc in enumerate(moments):
        acc = exact_sum(acc)
        hi = jnp.where(row8 == m, acc[0], hi)
        lo = jnp.where(row8 == m, acc[1], lo)
    total = (hi, lo)

    plane_to = [{"gy": lax.rem(me[1] + dy, 4), "gz": lax.rem(me[2] + dz, 4)} for dy, dz in PLANE]
    line_to = [{"gx": lax.rem(me[0] + o, 8)} for o in range(1, 8)]
    for stage, (peers, landing) in enumerate(((plane_to, a_recv0), (line_to, a_recv1))):
        a_send[stage] = jnp.where(lane8 < 64, total[0], total[1])
        copies = [
            remote(a_send.at[stage], landing.at[n], as_sem.at[stage, n], ar_sem.at[stage, n], dev)
            for n, dev in enumerate(peers)
        ]
        for c in copies:
            c.start()
        if stage == 0:
            build_operands()
        for c in copies:
            c.wait_recv()
        terms = [total]
        for n in range(len(peers)):
            x = landing[n]
            y = pltpu.roll(x, 64, 1)
            terms.append((jnp.where(lane8 < 64, x, y), jnp.where(lane8 < 64, y, x)))
        while len(terms) > 1:
            terms = [
                df_add(terms[t], terms[t + 1]) if t + 1 < len(terms) else terms[t]
                for t in range(0, len(terms), 2)
            ]
        total = terms[0]
        pending.extend(c.wait_send for c in copies)

    nu = [(total[0][m : m + 1], total[1][m : m + 1]) for m in range(2 * ITERS)]
    coef = solve4(nu)

    def combine(parts):
        total = coef[0] * parts[0]
        for c, x in zip(coef[1:], parts[1:]):
            total = total + c * x
        return total

    pe = [opposite_faces(zrecv[k, 1], zrecv[k, 0]) for k in range(ITERS)]
    pe = [combine(list(parts)) for parts in zip(*pe)]
    pe = [jnp.where(odd_lane, -a, a) for a in pe]
    for s in range(2):
        pp[(0, NI + 1)[s], pl.ds(TOP, NJ)] = combine([xrecv[k, s] for k in range(ITERS)])
        yf[s] = combine([yrecv[k, s] for k in range(ITERS)])

    def keep(f, i, x, odd_plane):
        hi, lo = split(x)
        rr = pl.ds(pl.multiple_of((lax.rem(i // 2, 4) * 4 + i // 8) * NJ, NJ), NJ)
        cc = slice(NK * odd_plane, NK * odd_plane + NK)
        xh[f, rr, cc] = hi
        xl[f, rr, cc] = lo

    def press(t, _):
        for g in range(GROUP):
            i = t * GROUP + g
            pp[i + 1, pl.ds(TOP - 1, 1)] = yf[0, pl.ds(i, 1)]
            pp[i + 1, pl.ds(TOP + NJ, 1)] = yf[1, pl.ds(i, 1)]
            x = combine([ref[i + 1, pl.ds(TOP, NJ)] for ref in w])
            pp[i + 1, pl.ds(TOP, NJ)] = x
            pst[i] = x
            keep(3, i, x, g % 2)
        return 0

    lax.fori_loop(0, NI // GROUP, press, 0)

    def fix(f):
        def body(t, _):
            for g in range(GROUP):
                i = t * GROUP + g
                n = ip[i + 1, pl.ds(TOP, NJ)]
                if f == 0:
                    g_ = pp[i + 2, pl.ds(TOP, NJ)] - pp[i, pl.ds(TOP, NJ)]
                    x = vx[i + 1]
                elif f == 1:
                    g_ = pp[i + 1, pl.ds(TOP + 1, NJ)] - pp[i + 1, pl.ds(TOP - 1, NJ)]
                    x = vy[i, pl.ds(TOP, NJ)]
                else:
                    c = tiles(pp[i + 1, pl.ds(TOP, NJ)])
                    g_ = join(ahead(c)) - join(behind(c)) + join(at_ends(pe, i))
                    x = vz[i]
                x = x - n * (0.5 * g_)
                cst[f, i] = x
                keep(f, i, x, g % 2)
            return 0

        lax.fori_loop(0, NI // GROUP, body, 0)

    def ring(axis, way):
        a = AXES.index(axis)
        n = SIZES[a]
        to = lax.rem(me[a] + (n + way), n)
        back = lax.rem(me[a] + (n - way), n)
        opposite = lax.rem(me[a] + 2, n)
        return to, back, opposite

    def rows16(m):
        return pl.ds(pl.multiple_of(m * 16, 16), 16)

    def stage_refs(f, h, stage):
        axis, way = ROUTES[f]
        slot = 0 if way == 1 else 1
        part_ = pl.ds(2 * h, 2)
        if stage == 0:
            if axis == "gz":
                return axis, way, (lambda m: u.at[f, m, part_]), za_in.at[slot, h], za_acc.at[slot, h], za_dir.at[slot, h], za_out.at[slot, h]
            return axis, way, (lambda m: u.at[f, :, part_, rows16(m)]), ya_in.at[slot, h], ya_acc.at[slot, h], ya_dir.at[slot, h], ya_out.at[slot, h]
        other = "gy" if axis == "gz" else "gz"
        if axis == "gz":
            chunk = lambda m: b_src_z.at[slot, h, :, rows16(m)]
        else:
            chunk = lambda m: b_src_y.at[slot, h, m]
        return other, way, chunk, b_in.at[f, h], b_acc.at[f, h], b_dir.at[f, h], b_out.at[f, h]

    def stage_far(f, h, stage):
        axis, way, chunk, r_in, r_acc, r_dir, r_out = stage_refs(f, h, stage)
        to, back, opposite = ring(axis, way)
        return remote(chunk(opposite), r_in, rs_sem.at[f, h, stage, 0], rr_sem.at[f, h, stage, 0], {axis: to})

    def stage_near(f, h, stage):
        axis, way, chunk, r_in, r_acc, r_dir, r_out = stage_refs(f, h, stage)
        to, back, opposite = ring(axis, way)
        return remote(chunk(back), r_dir, rs_sem.at[f, h, stage, 1], rr_sem.at[f, h, stage, 1], {axis: back})

    def stage_next(f, h, stage):
        axis, way, chunk, r_in, r_acc, r_dir, r_out = stage_refs(f, h, stage)
        to, back, opposite = ring(axis, way)
        return remote(r_out, r_acc, rs_sem.at[f, h, stage, 2], rr_sem.at[f, h, stage, 2], {axis: to})

    def stage_open(f, h, stage):
        for c in (stage_far(f, h, stage), stage_near(f, h, stage)):
            c.start()
            pending.append(c.wait_send)

    def stage_relay(f, h, stage):
        axis, way, chunk, r_in, r_acc, r_dir, r_out = stage_refs(f, h, stage)
        stage_far(f, h, stage).wait_recv()
        r_out[...] = r_in[...] + chunk(ring(axis, way)[0])[...]
        relay = stage_next(f, h, stage)
        relay.start()
        pending.append(relay.wait_send)

    def stage_close(f, h, stage):
        axis, way, chunk, r_in, r_acc, r_dir, r_out = stage_refs(f, h, stage)
        stage_near(f, h, stage).wait_recv()
        stage_next(f, h, stage).wait_recv()
        return chunk(me[AXES.index(axis)])[...] + r_acc[...] + r_dir[...]

    block = (lane % 64) // 16

    def contract_z(f, h, slot):
        zs = []
        for n in range(4):
            operand = wz[n]
            cut = slice(256 * n + 128 * h, 256 * n + 128 * h + 128)
            both = dot(xh[f, cut], operand)
            zs.append((both[:, :128] + both[:, 128:]) + dot(xl[f, cut], operand[:, :128]))
        for g in range(2):
            for e in range(2):
                pair = [z[NJ * g : NJ * g + NJ] for z in zs[2 * e : 2 * e + 2]]
                hi, lo = split(jnp.concatenate(pair, axis=1))
                zb[slot, g, e] = jnp.concatenate([hi, lo], axis=0)

    def contract_y(f, h, slot):
        for g in range(2):
            done = []
            for e in range(2):
                both = zb[slot, g, e]
                y = dot(fyt[...], jnp.concatenate([both[:NJ], both], axis=0))
                done += [tiles(y[:, :128]), tiles(y[:, 128:])]
            for r in range(4):
                out = []
                for q in range(8):
                    acc = done[-r % 4][q]
                    for b in range(1, 4):
                        acc = jnp.where(block == b, done[(b - r) % 4][q], acc)
                    out.append(acc)
                u[f, r, 2 * h + g] = join(out)

    steps = [(f, h) for f in ORDER for h in range(2)]
    contract_z(*steps[0], 0)
    for n, (f, h) in enumerate(steps):
        if n + 1 < len(steps):
            if h == 1:
                fix(steps[n + 1][0])
            contract_z(*steps[n + 1], (n + 1) % 2)
        contract_y(f, h, n % 2)
        stage_open(f, h, 0)
    items = [(f, h) for f in ORDER for h in range(2)]
    for f, h in items:
        stage_relay(f, h, 0)
    for f, h in items:
        whole = stage_close(f, h, 0)
        slot = 0 if ROUTES[f][1] == 1 else 1
        if ROUTES[f][0] == "gz":
            b_src_z[slot, h] = whole
        else:
            b_src_y[slot, h] = whole
        stage_open(f, h, 1)
    for f, h in items:
        stage_relay(f, h, 1)
    for f, h in items:
        whole = stage_close(f, h, 1)
        for g in range(2):
            at = 128 * (2 * h + g)
            ysc[16 * f : 16 * f + 16, at : at + 128] = whole[g]

    hi, lo = split(ysc[...])
    copies = {}
    for o in (4, 3, 5, 2, 6, 1, 7, 0):
        m = lax.rem(me[0] + o, 8)
        v[m] = dot(hi, k_hi[m]) + dot(lo, k_hi[m]) + dot(hi, k_lo[m])
        if o:
            copies[o] = remote(
                v.at[m], v_recv.at[o - 1], xs_sem.at[o - 1], xr_sem.at[o - 1], line_to[o - 1]
            )
            copies[o].start()
            pending.append(copies[o].wait_send)
    total = v[me[0]]
    for o in (1, 7, 2, 6, 3, 5, 4):
        copies[o].wait_recv()
        total = total + v_recv[o - 1]
    for a in range(8):
        moved = total if a == 0 else pltpu.roll(total, 128 - 16 * a, 1)
        for f in range(4):
            out_core[a, f] = moved[16 * f : 16 * f + 16, :16]

    for wait in pending:
        wait()


def per_device(velocity, inv_density, factor_x, factor_y, factor_z):
    vmem = pl.BlockSpec(memory_space=pltpu.VMEM)
    hbm = pl.BlockSpec(memory_space=pl.ANY)
    tall = TOP + NJ + 8
    dma = pltpu.SemaphoreType.DMA
    scratch = [
        pltpu.VMEM((NI + 2, NJ, NK), F32),
        pltpu.VMEM((NI, tall, NK), F32),
        pltpu.VMEM((NI, NJ, NK), F32),
        pltpu.VMEM((NI + 2, tall, NK), F32),
        pltpu.VMEM((NI + 2, tall, NK), F32),
        pltpu.VMEM((NI + 2, tall, NK), F32),
        pltpu.VMEM((NI + 2, tall, NK), F32),
        pltpu.VMEM((NI + 2, tall, NK), F32),
        pltpu.VMEM((NI + 1, NJ, NK), F32),
        pltpu.VMEM((NI, tall, NK), F32),
        pltpu.VMEM((NI, NJ, NK), F32),
        pltpu.VMEM((NI, NJ, NK), F32),
        pltpu.VMEM((NI + 2, tall, NK), F32),
        pltpu.VMEM((NI, NJ, NK), F32),
        pltpu.VMEM((ITERS, 2, NJ, NK), F32),
        pltpu.VMEM((2, 2, NJ, NK), F32),
        pltpu.VMEM((2, NJ, NK), F32),
        pltpu.VMEM((ITERS, 2, NI, NK), F32),
        pltpu.VMEM((ITERS, 2, NI, NK), F32),
        pltpu.VMEM((2, 2, NI, NK), F32),
        pltpu.VMEM((2, NI, NK), F32),
        pltpu.VMEM((2, NI, NK), F32),
        pltpu.VMEM((2, NI, NK), F32),
        pltpu.VMEM((2, NI, NK), F32),
        pltpu.VMEM((ITERS, 32, NK), F32),
        pltpu.VMEM((ITERS, 2, 32, NK), F32),
        pltpu.VMEM((2, 32, NK), F32),
        pltpu.VMEM((2, 2, 32, NK), F32),
        pltpu.VMEM((2, 8, NK), F32),
        pltpu.VMEM((len(PLANE), 8, NK), F32),
        pltpu.VMEM((7, 8, NK), F32),
        pltpu.VMEM((4, 256, 256), BF16),
        pltpu.VMEM((2, 2, 2, 128, 256), BF16),
        pltpu.VMEM((64, 192), BF16),
        pltpu.VMEM((8, 512, 128), BF16),
        pltpu.VMEM((8, 512, 128), BF16),
        pltpu.VMEM((4, 1024, 256), BF16),
        pltpu.VMEM((4, 1024, 256), BF16),
        pltpu.VMEM((4, 4, 4, 64, 128), F32),
    ]
    scratch += [pltpu.VMEM((2, 2, 2, 64, 128), F32)] * 4
    scratch += [pltpu.VMEM((2, 2, 4, 2, 16, 128), F32)] * 4
    scratch += [pltpu.VMEM((2, 2, 2, 64, 128), F32), pltpu.VMEM((2, 2, 4, 2, 16, 128), F32)]
    scratch += [pltpu.VMEM((4, 2, 2, 16, 128), F32)] * 4
    scratch += [
        pltpu.VMEM((64, 512), F32),
        pltpu.VMEM((8, 64, 128), F32),
        pltpu.VMEM((7, 64, 128), F32),
        dma((6,)),
        dma((5, 6, 2)),
        dma((5, 6, 2)),
        dma((2, len(PLANE))),
        dma((2, len(PLANE))),
        dma((4, 2, 2, 3)),
        dma((4, 2, 2, 3)),
        dma((7,)),
        dma((7,)),
    ]
    pressure, corrected, core = pl.pallas_call(
        kernel,
        out_shape=(
            pltpu.VMEM(inv_density.shape, F32),
            pltpu.VMEM(velocity.shape, F32),
            pltpu.VMEM((8, 4, 16, 16), F32),
        ),
        in_specs=[hbm, hbm, vmem, vmem, vmem],
        out_specs=(vmem, vmem, vmem),
        scratch_shapes=scratch,
        compiler_params=pltpu.CompilerParams(
            collective_id=0, has_side_effects=True, vmem_limit_bytes=52 * 1024 * 1024
        ),
    )(velocity, inv_density, factor_x, factor_y, factor_z.T)
    return pressure, corrected, core


def solution(mesh):
    placed = (
        P(None, "gx", "gy", "gz"),
        P("gx", "gy", "gz"),
        P("gx", None),
        P("gy", None),
        P("gz", None),
    )
    return jax.shard_map(
        per_device,
        mesh=mesh,
        in_specs=placed,
        out_specs=(P("gx", "gy", "gz"), P(None, "gx", "gy", "gz"), P("gx", None, "gy", "gz")),
        check_vma=False,
    )
```

```python
import jax
import jax.numpy as jnp
from jax import lax
from jax.experimental import pallas as pl
from jax.experimental.pallas import tpu as pltpu
from jax.sharding import PartitionSpec as P

ITERS = 4
SHIFT = 0.1
MESH = pl.DeviceIdType.MESH
F32 = jnp.float32
BF16 = jnp.bfloat16
NI, NJ, NK = 32, 64, 128
TOP = 8
AXES = ("gx", "gy", "gz")
SIZES = (8, 4, 4)
PLANE = [(dy, dz) for dy in range(4) for dz in range(4) if dy or dz]
ROUTES = {3: ("gz", 1), 1: ("gy", 1), 0: ("gz", -1), 2: ("gy", -1)}
ORDER = (3, 1, 0, 2)
TINY = 1e-11


def two_sum(a, b):
    s = a + b
    t = s - a
    return s, (a - (s - t)) + (b - t)


def quick(a, b):
    s = a + b
    return s, b - (s - a)


def df_add(x, y):
    s, e = two_sum(x[0], y[0])
    return quick(s, e + (x[1] + y[1]))


def exact_sum(x):
    def total(a):
        return jnp.sum(jnp.sum(a, axis=0, keepdims=True), axis=1, keepdims=True)

    big = 4.0 * total(jnp.abs(x[0]))
    coarse = (x[0] + big) - big
    return quick(total(coarse), total((x[0] - coarse) + x[1]))


def df_neg(x):
    return -x[0], -x[1]


def halves(a):
    t = 4097.0 * a
    h = t - (t - a)
    return h, a - h


def df_mul(x, y):
    p = x[0] * y[0]
    ah, al = halves(x[0])
    bh, bl = halves(y[0])
    e = ((ah * bh - p) + ah * bl + al * bh) + al * bl
    return quick(p, e + (x[0] * y[1] + x[1] * y[0]))


def df_recip(x):
    r = 1.0 / x[0]
    one = (jnp.ones_like(r), jnp.zeros_like(r))
    two = (jnp.full_like(r, 2.0), jnp.zeros_like(r))
    y = (r, jnp.zeros_like(r))
    for _ in range(1):
        y = df_mul(y, df_add(two, df_neg(df_mul(x, y))))
    return y


def solve4(nu):
    n = ITERS
    g = [[None] * n for _ in range(n)]
    for i in range(n):
        for j in range(i + 1):
            g[i][j] = df_add(nu[i + j], df_neg(nu[i + j + 1]))
    y = list(nu[:n])
    low = [[None] * n for _ in range(n)]
    inv = []
    for k in range(n):
        pivot = g[k][k]
        start = nu[2 * k][0] - nu[2 * k + 1][0]
        ok = pivot[0] > TINY * start
        safe = (jnp.where(ok, pivot[0], 1.0), jnp.where(ok, pivot[1], 0.0))
        r = df_recip(safe)
        r = (jnp.where(ok, r[0], 0.0), jnp.where(ok, r[1], 0.0))
        inv.append(r)
        for i in range(k + 1, n):
            low[i][k] = df_mul(g[i][k], r)
        for i in range(k + 1, n):
            for j in range(k + 1, i + 1):
                g[i][j] = df_add(g[i][j], df_neg(df_mul(low[i][k], g[j][k])))
            y[i] = df_add(y[i], df_neg(df_mul(low[i][k], y[k])))
    c = [None] * n
    for i in reversed(range(n)):
        v = df_mul(y[i], inv[i])
        for j in range(i + 1, n):
            v = df_add(v, df_neg(df_mul(low[j][i], c[j])))
        c[i] = v
    return [v[0] for v in c]


def lanes(shape):
    return lax.broadcasted_iota(jnp.int32, shape, len(shape) - 1)


def rows(shape):
    return lax.broadcasted_iota(jnp.int32, shape, 0)


def split(x):
    hi = x.astype(BF16)
    return hi, (x - hi.astype(F32)).astype(BF16)


def dot(a, b):
    return lax.dot_general(a, b, (((1,), (0,)), ((), ())), preferred_element_type=F32)


def kernel(
    vel, inv, fx, fy, fz,
    pst, cst, out_core,
    vx, vy, vz, ip, w0, w1, w2, w3, cx, cy, cz, dinv, pp,
    part, xrecv, xrecv0, xcoef, ysend, yrecv, yrecv0, yown, ycoef, yf, yd,
    zsend, zrecv, zsend0, zrecv0,
    zc, zf, mom, a_send, a_recv0, a_recv1,
    wz, zb, fyt, k_hi, k_lo, xh, xl, u, uk,
    za_in, za_acc, za_dir, za_out, ya_in, ya_acc, ya_dir, ya_out,
    b_src_z, b_src_y, b_in, b_acc, b_dir, b_out, ysc, v, v_recv,
    in_sem, hs_sem, hr_sem, as_sem, ar_sem, rs_sem, rr_sem, xs_sem, xr_sem,
):
    w = (w0, w1, w2, w3)
    me = [lax.axis_index(a) for a in AXES]
    has = []
    for a in range(3):
        has += [me[a] > 0, me[a] < SIZES[a] - 1]

    def neighbour(side):
        a = side // 2
        step = 1 if side % 2 else SIZES[a] - 1
        return {AXES[a]: lax.rem(me[a] + step, SIZES[a])}

    def remote(src, dst, ss, rs, dev):
        return pltpu.make_async_remote_copy(
            src_ref=src, dst_ref=dst, send_sem=ss, recv_sem=rs, device_id=dev, device_id_type=MESH
        )

    lane = lanes((8, NK))
    pending = []

    loads = [
        pltpu.make_async_copy(inv, ip.at[pl.ds(1, NI), pl.ds(TOP, NJ)], in_sem.at[0]),
        pltpu.make_async_copy(vel.at[2], vz, in_sem.at[1]),
        pltpu.make_async_copy(vel.at[1], vy.at[:, pl.ds(TOP, NJ)], in_sem.at[2]),
        pltpu.make_async_copy(vel.at[0], vx.at[pl.ds(1, NI)], in_sem.at[3]),
        pltpu.make_async_copy(inv.at[:, 0], yown.at[0], in_sem.at[4]),
        pltpu.make_async_copy(inv.at[:, NJ - 1], yown.at[1], in_sem.at[5]),
    ]
    for c in loads:
        c.start()

    barrier = pltpu.get_barrier_semaphore()
    for side in range(6):
        pl.semaphore_signal(barrier, inc=1, device_id=neighbour(side), device_id_type=MESH)

    def tiles(x):
        return [x[8 * q : 8 * q + 8] for q in range(x.shape[0] // 8)]

    def pack(acc, x, i):
        out = list(acc)
        for q, part in enumerate(x):
            moved = pltpu.roll(part, 2 * i + 1 + 64 * (q // 4), 1)
            out[q % 4] = jnp.where(lane // 2 == i + 32 * (q // 4), moved, out[q % 4])
        return out

    def unpack(faces, i):
        return [pltpu.roll(faces[q % 4], lax.rem(255 - 2 * i - 64 * (q // 4), 128), 1) for q in range(8)]

    odd_lane = lane % 2 == 1
    end_lane = (lane == 0) | (lane == NK - 1)
    sub = rows((8, NK))

    def ahead(x):
        return [jnp.where(lane == NK - 1, 0.0, pltpu.roll(a, NK - 1, 1)) for a in x]

    def behind(x):
        return [jnp.where(lane == 0, 0.0, pltpu.roll(a, 1, 1)) for a in x]

    def opposite_faces(plus, minus):
        return [
            jnp.where(odd_lane, pltpu.roll(b, 1, 1), pltpu.roll(a, NK - 1, 1))
            for a, b in zip(tiles(plus), tiles(minus))
        ]

    def at_ends(faces, i):
        return [jnp.where(end_lane, e, 0.0) for e in unpack(faces, i)]

    def add_rows(x, ref, i):
        low = jnp.where(sub == 0, ref[0, pl.ds(i, 1)], 0.0)
        high = jnp.where(sub == 7, ref[1, pl.ds(i, 1)], 0.0)
        return [x[0] + low] + x[1:7] + [x[7] + high]

    GROUP = 4
    no_faces = [jnp.zeros((8, NK), F32)] * 4
    zero_acc = jnp.zeros((8, NK), F32)

    zero_plane = jnp.zeros((NJ, NK), F32)
    zero_row = jnp.zeros((1, NK), F32)
    for ref in (vx, ip) + w:
        top = 0 if ref is vx else TOP
        for far in (0, NI + 1):
            ref[far, pl.ds(top, NJ)] = zero_plane
    for ref in (vy, ip) + w:
        for i in range(NI):
            for far in (TOP - 1, TOP + NJ):
                ref[i if ref is vy else i + 1, pl.ds(far, 1)] = zero_row
    for s in range(2):
        @pl.when(jnp.logical_not(has[s]))
        def _():
            xrecv0[s] = jnp.zeros((2, NJ, NK), F32)
            for k in range(ITERS):
                xrecv[k, s] = zero_plane

        @pl.when(jnp.logical_not(has[2 + s]))
        def _():
            yrecv0[s] = jnp.zeros((2, NI, NK), F32)
            for k in range(ITERS):
                yrecv[k, s] = jnp.zeros((NI, NK), F32)

        @pl.when(jnp.logical_not(has[4 + s]))
        def _():
            zrecv0[s] = jnp.zeros((2, 32, NK), F32)
            for k in range(ITERS):
                zrecv[k, s] = jnp.zeros((32, NK), F32)

    for c in loads[:2]:
        c.wait()

    def face0(t, carry):
        a, b = carry
        for g in range(GROUP):
            i = t * GROUP + g
            a = pack(a, tiles(vz[i]), i)
            b = pack(b, tiles(ip[i + 1, pl.ds(TOP, NJ)]), i)
        return a, b

    fu, fn = lax.fori_loop(0, NI // GROUP, face0, (no_faces, no_faces))
    zsend0[0] = jnp.concatenate(fu, axis=0)
    zsend0[1] = jnp.concatenate(fn, axis=0)
    pl.semaphore_wait(barrier, 6)

    def halo(r, side, landing):
        s, t = side % 2, landing % 2
        ax = side // 2
        if ax == 0:
            if r == 0:
                edge = (0, NI - 1)[s]
                pairs = [(vel.at[0, edge], xrecv0.at[t, 0]), (inv.at[edge], xrecv0.at[t, 1])]
            else:
                pairs = [(w[r - 1].at[(1, NI)[s], pl.ds(TOP, NJ)], xrecv.at[r - 1, t])]
        elif ax == 1:
            if r == 0:
                edge = (0, NJ - 1)[s]
                pairs = [(vel.at[1, :, edge], yrecv0.at[t, 0]), (inv.at[:, edge], yrecv0.at[t, 1])]
            else:
                pairs = [(ysend.at[r - 1, s], yrecv.at[r - 1, t])]
        elif r == 0:
            pairs = [(zsend0, zrecv0.at[t])]
        else:
            pairs = [(zsend.at[r - 1], zrecv.at[r - 1, t])]
        return [
            remote(a, b, hs_sem.at[r, side, n], hr_sem.at[r, landing, n], neighbour(side))
            for n, (a, b) in enumerate(pairs)
        ]

    def halo_start(r, sides):
        pending.append(lambda: halo_sent(r, sides))
        for side in sides:
            @pl.when(has[side])
            def _():
                for c in halo(r, side, side ^ 1):
                    c.start()

    def halo_wait(r, sides):
        for side in sides:
            @pl.when(has[side])
            def _():
                for c in halo(r, side, side):
                    c.wait_recv()

    def halo_sent(r, sides):
        for side in sides:
            @pl.when(has[side])
            def _():
                for c in halo(r, side, side ^ 1):
                    c.wait_send()

    halo_start(0, range(6))

    for c in loads[2:]:
        c.wait()

    def accumulate(acc, parts):
        while len(parts) > 1:
            parts = [parts[n] + parts[n + 1] for n in range(0, len(parts), 2)]
        s, e = two_sum(acc[0], parts[0])
        return s, acc[1] + e

    def keep_moment(m, acc):
        mom[m, 0] = acc[0]
        mom[m, 1] = acc[1]

    def mul(a, b):
        return [x * y for x, y in zip(a, b)]

    def join(x):
        return jnp.concatenate(x, axis=0)

    def join_edges(ref):
        return jnp.stack([ref[1, pl.ds(TOP, NJ)], ref[NI, pl.ds(TOP, NJ)]])

    cx[0] = zero_plane

    def inner0(t, _):
        for g in range(GROUP):
            i = t * GROUP + g
            n = ip[i + 1, pl.ds(TOP, NJ)]
            xf = ip[i + 2, pl.ds(TOP, NJ)]
            yn = ip[i + 1, pl.ds(TOP + 1, NJ)]
            nt = tiles(n)
            zn = ahead(nt)
            cx[i + 1] = 0.5 * (n + xf)
            cy[i, pl.ds(TOP, NJ)] = 0.5 * (n + yn)
            cy[i, pl.ds(TOP - 1, 1)] = zero_row
            cz[i] = join([jnp.where(lane == NK - 1, 0.0, 0.5 * (a + b)) for a, b in zip(nt, zn)])
            around = (xf + ip[i, pl.ds(TOP, NJ)]) + (yn + ip[i + 1, pl.ds(TOP - 1, NJ)])
            around = around + (join(zn) + join(behind(nt)))
            dinv[i] = (SHIFT + 3.0 * n) + 0.5 * around
            at = tiles(vz[i])
            div = (vx[i + 2] - vx[i]) + (vy[i, pl.ds(TOP + 1, NJ)] - vy[i, pl.ds(TOP - 1, NJ)])
            part[i] = div + (join(ahead(at)) - join(behind(at)))
        return 0

    lax.fori_loop(0, NI // GROUP, inner0, 0)

    halo_wait(0, range(6))

    xcoef[...] = 0.5 * (xrecv0[:, 1] + join_edges(ip))
    ycoef[...] = 0.5 * (yrecv0[:, 1] + yown[...])
    hn = opposite_faces(zrecv0[1, 1], zrecv0[0, 1])
    hu = opposite_faces(zrecv0[1, 0], zrecv0[0, 0])
    hu = [jnp.where(odd_lane, -a, a) for a in hu]
    zc[...] = join([0.5 * (a + b) for a, b in zip(hn, fn)])
    yd[...] = 0.5 * yrecv0[:, 1]
    yf[0] = -yrecv0[0, 0]
    yf[1] = yrecv0[1, 0]
    hn = [0.5 * a for a in hn]
    dinv[0] = dinv[0] + 0.5 * xrecv0[0, 1]
    dinv[NI - 1] = dinv[NI - 1] + 0.5 * xrecv0[1, 1]
    part[0] = part[0] - xrecv0[0, 0]
    part[NI - 1] = part[NI - 1] + xrecv0[1, 0]

    def first(t, carry):
        faces, acc = carry
        terms = []
        for g in range(GROUP):
            i = t * GROUP + g
            row = pl.ds(i, 1)
            d = add_rows(tiles(dinv[i]), yd, i)
            d = [a + b for a, b in zip(d, at_ends(hn, i))]
            b = add_rows(tiles(part[i]), yf, i)
            b = [-0.5 * (x + y) for x, y in zip(b, at_ends(hu, i))]
            di = [1.0 / x for x in d]
            new = mul(b, di)
            dinv[i] = join(di)
            w0[i + 1, pl.ds(TOP, NJ)] = join(new)
            ysend[0, 0, row] = new[0][0:1]
            ysend[0, 1, row] = new[7][7:8]
            faces = pack(faces, new, i)
            terms += mul(b, new)
        return faces, accumulate(acc, terms)

    faces, acc = lax.fori_loop(0, NI // GROUP, first, (no_faces, (zero_acc, zero_acc)))
    keep_moment(0, acc)

    def build_operands():
        twice = jnp.concatenate([fz[...], fz[...]], axis=0).T
        low_half = lanes((NK, 128)) < 64
        for n in range(4):
            turned = twice if n == 0 else pltpu.roll(twice, 16 * n, 1)
            top = jnp.where(low_half, turned, 0.0)
            hi, lo = split(jnp.concatenate([top, turned - top], axis=0))
            wz[n] = jnp.concatenate([hi, lo], axis=1)
        fyp = jnp.concatenate([fy[...], jnp.zeros((NJ, 64), F32)], axis=1)
        hi, lo = split(fyp.T[:64])
        fyt[...] = jnp.concatenate([hi, lo, hi], axis=1)
        fx_hi, fx_lo = split(fx[...])
        row = rows((512, NI))
        pair = ((row % 64) // 16 + 4 - me[2]) % 4
        plane = (row // 128) * 8 + pair * 2 + (row % 128) // 64
        rep = (plane == lanes((512, NI))).astype(F32).astype(BF16)
        same = (rows((512, 128)) % 16) == (lanes((512, 128)) % 16)

        def build_x(m, _):
            pick = (rows((64, 128)) == 8 * m + lanes((64, 128)) // 16).astype(F32).astype(BF16)
            for part_, dst in ((fx_hi, k_hi), (fx_lo, k_lo)):
                wide = dot(part_, pick).astype(BF16)
                dst[m] = jnp.where(same, dot(rep, wide), 0.0).astype(BF16)
            return 0

        lax.fori_loop(0, 8, build_x, 0)

    def keep(f, i, x, odd_plane):
        hi, lo = split(x)
        rr = pl.ds(pl.multiple_of((lax.rem(i // 2, 4) * 4 + i // 8) * NJ, NJ), NJ)
        cc = slice(NK * odd_plane, NK * odd_plane + NK)
        xh[f, rr, cc] = hi
        xl[f, rr, cc] = lo

    block = (lane % 64) // 16

    def contract_z(f, h, slot):
        zs = []
        for n in range(4):
            operand = wz[n]
            cut = slice(256 * n + 128 * h, 256 * n + 128 * h + 128)
            both = dot(xh[f, cut], operand)
            zs.append((both[:, :128] + both[:, 128:]) + dot(xl[f, cut], operand[:, :128]))
        for g in range(2):
            for e in range(2):
                pair = [z[NJ * g : NJ * g + NJ] for z in zs[2 * e : 2 * e + 2]]
                hi, lo = split(jnp.concatenate(pair, axis=1))
                zb[slot, g, e] = jnp.concatenate([hi, lo], axis=0)

    def contract_y(h, slot, dst):
        for g in range(2):
            done = []
            for e in range(2):
                both = zb[slot, g, e]
                y = dot(fyt[...], jnp.concatenate([both[:NJ], both], axis=0))
                done += [tiles(y[:, :128]), tiles(y[:, 128:])]
            for r in range(4):
                out = []
                for q in range(8):
                    acc = done[-r % 4][q]
                    for b in range(1, 4):
                        acc = jnp.where(block == b, done[(b - r) % 4][q], acc)
                    out.append(acc)
                dst[r, 2 * h + g] = join(out)

    def contract_vector(k):
        def body(t, _):
            for g in range(GROUP):
                i = t * GROUP + g
                keep(3, i, w[k][i + 1, pl.ds(TOP, NJ)], g % 2)
            return 0

        lax.fori_loop(0, NI // GROUP, body, 0)
        for h in range(2):
            contract_z(3, h, h)
        for h in range(2):
            contract_y(h, h, uk.at[k])

    for k in range(ITERS):
        zsend[k] = join(faces)
        halo_start(k + 1, range(6))
        last = k == ITERS - 1
        here = w[k]

        def inner(t, odd):
            terms = []
            for g in range(GROUP):
                i = t * GROUP + g
                c = here[i + 1, pl.ds(TOP, NJ)]
                f = cz[i]
                bw = cx[i] * here[i, pl.ds(TOP, NJ)] + cx[i + 1] * here[i + 2, pl.ds(TOP, NJ)]
                bw = bw + cy[i, pl.ds(TOP - 1, NJ)] * here[i + 1, pl.ds(TOP - 1, NJ)]
                bw = bw + cy[i, pl.ds(TOP, NJ)] * here[i + 1, pl.ds(TOP + 1, NJ)]
                nxt = join([pltpu.roll(a, NK - 1, 1) for a in tiles(c)])
                prv = join([pltpu.roll(a, 1, 1) for a in tiles(f * c)])
                bw = bw + (f * nxt + prv)
                part[i] = bw
                terms += tiles(c * bw)
            return accumulate(odd, terms)

        keep_moment(2 * k + 1, lax.fori_loop(0, NI // GROUP, inner, (zero_acc, zero_acc)))

        if k == 0:
            build_operands()
        else:
            contract_vector(k - 1)

        halo_wait(k + 1, range(6))
        flux = mul(tiles(zc[...]), opposite_faces(zrecv[k, 1], zrecv[k, 0]))
        terms = mul(flux, tiles(zsend[k]))
        zf[...] = join(flux)
        for s in range(2):
            side = ycoef[s] * yrecv[k, s]
            yf[s] = side
            terms += tiles(side * ysend[k, s])
            side = xcoef[s] * xrecv[k, s]
            edge = (0, NI - 1)[s]
            terms += tiles(side * here[edge + 1, pl.ds(TOP, NJ)])
            if not last:
                part[edge] = part[edge] + side
        while len(terms) & (len(terms) - 1):
            terms.append(zero_acc)
        keep_moment(2 * k + 1, accumulate((mom[2 * k + 1, 0], mom[2 * k + 1, 1]), terms))
        if last:
            break
        there = w[k + 1]

        def outer(t, carry):
            faces, even = carry
            terms = []
            for g in range(GROUP):
                i = t * GROUP + g
                row = pl.ds(i, 1)
                bw = add_rows(tiles(part[i]), yf, i)
                bw = [a + b for a, b in zip(bw, at_ends(tiles(zf[...]), i))]
                new = mul(bw, tiles(dinv[i]))
                there[i + 1, pl.ds(TOP, NJ)] = join(new)
                ysend[k + 1, 0, row] = new[0][0:1]
                ysend[k + 1, 1, row] = new[7][7:8]
                faces = pack(faces, new, i)
                terms += mul(bw, new)
            return faces, accumulate(even, terms)

        faces, even = lax.fori_loop(0, NI // GROUP, outer, (no_faces, (zero_acc, zero_acc)))
        keep_moment(2 * k + 2, even)

    row8 = rows((8, NK))
    lane8 = lanes((8, NK))
    hi = zero_acc
    lo = zero_acc
    for m in range(2 * ITERS):
        acc = exact_sum((mom[m, 0], mom[m, 1]))
        hi = jnp.where(row8 == m, acc[0], hi)
        lo = jnp.where(row8 == m, acc[1], lo)
    total = (hi, lo)

    plane_to = [{"gy": lax.rem(me[1] + dy, 4), "gz": lax.rem(me[2] + dz, 4)} for dy, dz in PLANE]
    line_to = [{"gx": lax.rem(me[0] + o, 8)} for o in range(1, 8)]
    for stage, (peers, landing) in enumerate(((plane_to, a_recv0), (line_to, a_recv1))):
        a_send[stage] = jnp.where(lane8 < 64, total[0], total[1])
        copies = [
            remote(a_send.at[stage], landing.at[n], as_sem.at[stage, n], ar_sem.at[stage, n], dev)
            for n, dev in enumerate(peers)
        ]
        for c in copies:
            c.start()
        if stage == 0:
            contract_vector(ITERS - 1)
        for c in copies:
            c.wait_recv()
        terms = [total]
        for n in range(len(peers)):
            x = landing[n]
            y = pltpu.roll(x, 64, 1)
            terms.append((jnp.where(lane8 < 64, x, y), jnp.where(lane8 < 64, y, x)))
        while len(terms) > 1:
            terms = [
                df_add(terms[t], terms[t + 1]) if t + 1 < len(terms) else terms[t]
                for t in range(0, len(terms), 2)
            ]
        total = terms[0]
        pending.extend(c.wait_send for c in copies)

    nu = [(total[0][m : m + 1], total[1][m : m + 1]) for m in range(2 * ITERS)]
    coef = solve4(nu)

    def combine(parts):
        total = coef[0] * parts[0]
        for c, x in zip(coef[1:], parts[1:]):
            total = total + c * x
        return total

    def ring(axis, way):
        a = AXES.index(axis)
        n = SIZES[a]
        to = lax.rem(me[a] + (n + way), n)
        back = lax.rem(me[a] + (n - way), n)
        opposite = lax.rem(me[a] + 2, n)
        return to, back, opposite

    def rows16(m):
        return pl.ds(pl.multiple_of(m * 16, 16), 16)

    def stage_refs(f, h, stage):
        axis, way = ROUTES[f]
        slot = 0 if way == 1 else 1
        part_ = pl.ds(2 * h, 2)
        if stage == 0:
            if axis == "gz":
                return axis, way, (lambda m: u.at[f, m, part_]), za_in.at[slot, h], za_acc.at[slot, h], za_dir.at[slot, h], za_out.at[slot, h]
            return axis, way, (lambda m: u.at[f, :, part_, rows16(m)]), ya_in.at[slot, h], ya_acc.at[slot, h], ya_dir.at[slot, h], ya_out.at[slot, h]
        other = "gy" if axis == "gz" else "gz"
        if axis == "gz":
            chunk = lambda m: b_src_z.at[slot, h, :, rows16(m)]
        else:
            chunk = lambda m: b_src_y.at[slot, h, m]
        return other, way, chunk, b_in.at[f, h], b_acc.at[f, h], b_dir.at[f, h], b_out.at[f, h]

    def stage_far(f, h, stage):
        axis, way, chunk, r_in, r_acc, r_dir, r_out = stage_refs(f, h, stage)
        to, back, opposite = ring(axis, way)
        return remote(chunk(opposite), r_in, rs_sem.at[f, h, stage, 0], rr_sem.at[f, h, stage, 0], {axis: to})

    def stage_near(f, h, stage):
        axis, way, chunk, r_in, r_acc, r_dir, r_out = stage_refs(f, h, stage)
        to, back, opposite = ring(axis, way)
        return remote(chunk(back), r_dir, rs_sem.at[f, h, stage, 1], rr_sem.at[f, h, stage, 1], {axis: back})

    def stage_next(f, h, stage):
        axis, way, chunk, r_in, r_acc, r_dir, r_out = stage_refs(f, h, stage)
        to, back, opposite = ring(axis, way)
        return remote(r_out, r_acc, rs_sem.at[f, h, stage, 2], rr_sem.at[f, h, stage, 2], {axis: to})

    def stage_open(f, h, stage):
        for c in (stage_far(f, h, stage), stage_near(f, h, stage)):
            c.start()
            pending.append(c.wait_send)

    def stage_relay(f, h, stage):
        axis, way, chunk, r_in, r_acc, r_dir, r_out = stage_refs(f, h, stage)
        stage_far(f, h, stage).wait_recv()
        r_out[...] = r_in[...] + chunk(ring(axis, way)[0])[...]
        relay = stage_next(f, h, stage)
        relay.start()
        pending.append(relay.wait_send)

    def stage_close(f, h, stage):
        axis, way, chunk, r_in, r_acc, r_dir, r_out = stage_refs(f, h, stage)
        stage_near(f, h, stage).wait_recv()
        stage_next(f, h, stage).wait_recv()
        return chunk(me[AXES.index(axis)])[...] + r_acc[...] + r_dir[...]

    for h in range(2):
        for g in range(2 * h, 2 * h + 2):
            for r in range(4):
                u[3, r, g] = combine([uk[k, r, g] for k in range(ITERS)])
        stage_open(3, h, 0)

    pe = [opposite_faces(zrecv[k, 1], zrecv[k, 0]) for k in range(ITERS)]
    pe = [combine(list(parts)) for parts in zip(*pe)]
    pe = [jnp.where(odd_lane, -a, a) for a in pe]
    for s in range(2):
        pp[(0, NI + 1)[s], pl.ds(TOP, NJ)] = combine([xrecv[k, s] for k in range(ITERS)])
        yf[s] = combine([yrecv[k, s] for k in range(ITERS)])

    def press(t, _):
        for g in range(GROUP):
            i = t * GROUP + g
            pp[i + 1, pl.ds(TOP - 1, 1)] = yf[0, pl.ds(i, 1)]
            pp[i + 1, pl.ds(TOP + NJ, 1)] = yf[1, pl.ds(i, 1)]
            x = combine([ref[i + 1, pl.ds(TOP, NJ)] for ref in w])
            pp[i + 1, pl.ds(TOP, NJ)] = x
            pst[i] = x
        return 0

    lax.fori_loop(0, NI // GROUP, press, 0)

    def fix(f):
        def body(t, _):
            for g in range(GROUP):
                i = t * GROUP + g
                n = ip[i + 1, pl.ds(TOP, NJ)]
                if f == 0:
                    g_ = pp[i + 2, pl.ds(TOP, NJ)] - pp[i, pl.ds(TOP, NJ)]
                    x = vx[i + 1]
                elif f == 1:
                    g_ = pp[i + 1, pl.ds(TOP + 1, NJ)] - pp[i + 1, pl.ds(TOP - 1, NJ)]
                    x = vy[i, pl.ds(TOP, NJ)]
                else:
                    c = tiles(pp[i + 1, pl.ds(TOP, NJ)])
                    g_ = join(ahead(c)) - join(behind(c)) + join(at_ends(pe, i))
                    x = vz[i]
                x = x - n * (0.5 * g_)
                cst[f, i] = x
                keep(f, i, x, g % 2)
            return 0

        lax.fori_loop(0, NI // GROUP, body, 0)

    steps = [(f, h) for f in ORDER[1:] for h in range(2)]
    fix(ORDER[1])
    contract_z(*steps[0], 0)
    for n, (f, h) in enumerate(steps):
        if n + 1 < len(steps):
            if h == 1:
                fix(steps[n + 1][0])
            contract_z(*steps[n + 1], (n + 1) % 2)
        contract_y(h, n % 2, u.at[f])
        stage_open(f, h, 0)
    items = [(f, h) for f in ORDER for h in range(2)]
    for f, h in items:
        stage_relay(f, h, 0)
    for f, h in items:
        whole = stage_close(f, h, 0)
        slot = 0 if ROUTES[f][1] == 1 else 1
        if ROUTES[f][0] == "gz":
            b_src_z[slot, h] = whole
        else:
            b_src_y[slot, h] = whole
        stage_open(f, h, 1)
    for f, h in items:
        stage_relay(f, h, 1)
    for f, h in items:
        whole = stage_close(f, h, 1)
        for g in range(2):
            at = 128 * (2 * h + g)
            ysc[16 * f : 16 * f + 16, at : at + 128] = whole[g]

    hi, lo = split(ysc[...])
    copies = {}
    for o in (4, 3, 5, 2, 6, 1, 7, 0):
        m = lax.rem(me[0] + o, 8)
        v[m] = dot(hi, k_hi[m]) + dot(lo, k_hi[m]) + dot(hi, k_lo[m])
        if o:
            copies[o] = remote(
                v.at[m], v_recv.at[o - 1], xs_sem.at[o - 1], xr_sem.at[o - 1], line_to[o - 1]
            )
            copies[o].start()
            pending.append(copies[o].wait_send)
    total = v[me[0]]
    for o in (1, 7, 2, 6, 3, 5, 4):
        copies[o].wait_recv()
        total = total + v_recv[o - 1]
    for a in range(8):
        moved = total if a == 0 else pltpu.roll(total, 128 - 16 * a, 1)
        for f in range(4):
            out_core[a, f] = moved[16 * f : 16 * f + 16, :16]

    for wait in pending:
        wait()


def per_device(velocity, inv_density, factor_x, factor_y, factor_z):
    vmem = pl.BlockSpec(memory_space=pltpu.VMEM)
    hbm = pl.BlockSpec(memory_space=pl.ANY)
    tall = TOP + NJ + 8
    dma = pltpu.SemaphoreType.DMA
    scratch = [
        pltpu.VMEM((NI + 2, NJ, NK), F32),
        pltpu.VMEM((NI, tall, NK), F32),
        pltpu.VMEM((NI, NJ, NK), F32),
        pltpu.VMEM((NI + 2, tall, NK), F32),
        pltpu.VMEM((NI + 2, tall, NK), F32),
        pltpu.VMEM((NI + 2, tall, NK), F32),
        pltpu.VMEM((NI + 2, tall, NK), F32),
        pltpu.VMEM((NI + 2, tall, NK), F32),
        pltpu.VMEM((NI + 1, NJ, NK), F32),
        pltpu.VMEM((NI, tall, NK), F32),
        pltpu.VMEM((NI, NJ, NK), F32),
        pltpu.VMEM((NI, NJ, NK), F32),
        pltpu.VMEM((NI + 2, tall, NK), F32),
        pltpu.VMEM((NI, NJ, NK), F32),
        pltpu.VMEM((ITERS, 2, NJ, NK), F32),
        pltpu.VMEM((2, 2, NJ, NK), F32),
        pltpu.VMEM((2, NJ, NK), F32),
        pltpu.VMEM((ITERS, 2, NI, NK), F32),
        pltpu.VMEM((ITERS, 2, NI, NK), F32),
        pltpu.VMEM((2, 2, NI, NK), F32),
        pltpu.VMEM((2, NI, NK), F32),
        pltpu.VMEM((2, NI, NK), F32),
        pltpu.VMEM((2, NI, NK), F32),
        pltpu.VMEM((2, NI, NK), F32),
        pltpu.VMEM((ITERS, 32, NK), F32),
        pltpu.VMEM((ITERS, 2, 32, NK), F32),
        pltpu.VMEM((2, 32, NK), F32),
        pltpu.VMEM((2, 2, 32, NK), F32),
        pltpu.VMEM((32, NK), F32),
        pltpu.VMEM((32, NK), F32),
        pltpu.VMEM((8, 2, 8, NK), F32),
        pltpu.VMEM((2, 8, NK), F32),
        pltpu.VMEM((len(PLANE), 8, NK), F32),
        pltpu.VMEM((7, 8, NK), F32),
        pltpu.VMEM((4, 256, 256), BF16),
        pltpu.VMEM((2, 2, 2, 128, 256), BF16),
        pltpu.VMEM((64, 192), BF16),
        pltpu.VMEM((8, 512, 128), BF16),
        pltpu.VMEM((8, 512, 128), BF16),
        pltpu.VMEM((4, 1024, 256), BF16),
        pltpu.VMEM((4, 1024, 256), BF16),
        pltpu.VMEM((4, 4, 4, 64, 128), F32),
        pltpu.VMEM((ITERS, 4, 4, 64, 128), F32),
    ]
    scratch += [pltpu.VMEM((2, 2, 2, 64, 128), F32)] * 4
    scratch += [pltpu.VMEM((2, 2, 4, 2, 16, 128), F32)] * 4
    scratch += [pltpu.VMEM((2, 2, 2, 64, 128), F32), pltpu.VMEM((2, 2, 4, 2, 16, 128), F32)]
    scratch += [pltpu.VMEM((4, 2, 2, 16, 128), F32)] * 4
    scratch += [
        pltpu.VMEM((64, 512), F32),
        pltpu.VMEM((8, 64, 128), F32),
        pltpu.VMEM((7, 64, 128), F32),
        dma((6,)),
        dma((5, 6, 2)),
        dma((5, 6, 2)),
        dma((2, len(PLANE))),
        dma((2, len(PLANE))),
        dma((4, 2, 2, 3)),
        dma((4, 2, 2, 3)),
        dma((7,)),
        dma((7,)),
    ]
    pressure, corrected, core = pl.pallas_call(
        kernel,
        out_shape=(
            pltpu.VMEM(inv_density.shape, F32),
            pltpu.VMEM(velocity.shape, F32),
            pltpu.VMEM((8, 4, 16, 16), F32),
        ),
        in_specs=[hbm, hbm, vmem, vmem, vmem],
        out_specs=(vmem, vmem, vmem),
        scratch_shapes=scratch,
        compiler_params=pltpu.CompilerParams(
            collective_id=0, has_side_effects=True, vmem_limit_bytes=52 * 1024 * 1024
        ),
    )(velocity, inv_density, factor_x, factor_y, factor_z.T)
    return pressure, corrected, core


def solution(mesh):
    placed = (
        P(None, "gx", "gy", "gz"),
        P("gx", "gy", "gz"),
        P("gx", None),
        P("gy", None),
        P("gz", None),
    )
    return jax.shard_map(
        per_device,
        mesh=mesh,
        in_specs=placed,
        out_specs=(P("gx", "gy", "gz"), P(None, "gx", "gy", "gz"), P("gx", None, "gy", "gz")),
        check_vma=False,
    )
```

```python
import jax
import jax.numpy as jnp
from jax import lax
from jax.experimental import pallas as pl
from jax.experimental.pallas import tpu as pltpu
from jax.sharding import PartitionSpec as P

ITERS = 4
SHIFT = 0.1
MESH = pl.DeviceIdType.MESH
F32 = jnp.float32
BF16 = jnp.bfloat16
NI, NJ, NK = 32, 64, 128
TOP = 8
AXES = ("gx", "gy", "gz")
SIZES = (8, 4, 4)
PLANE = [(dy, dz) for dy in range(4) for dz in range(4) if dy or dz]
ROUTES = {3: ("gz", 1), 1: ("gy", 1), 0: ("gz", -1), 2: ("gy", -1)}
ORDER = (3, 1, 0, 2)
TINY = 1e-11


def two_sum(a, b):
    s = a + b
    t = s - a
    return s, (a - (s - t)) + (b - t)


def quick(a, b):
    s = a + b
    return s, b - (s - a)


def df_add(x, y):
    s, e = two_sum(x[0], y[0])
    return quick(s, e + (x[1] + y[1]))


def exact_sum(x):
    def total(a):
        return jnp.sum(jnp.sum(a, axis=0, keepdims=True), axis=1, keepdims=True)

    big = 4.0 * total(jnp.abs(x[0]))
    coarse = (x[0] + big) - big
    return quick(total(coarse), total((x[0] - coarse) + x[1]))


def df_neg(x):
    return -x[0], -x[1]


def halves(a):
    t = 4097.0 * a
    h = t - (t - a)
    return h, a - h


def df_mul(x, y):
    p = x[0] * y[0]
    ah, al = halves(x[0])
    bh, bl = halves(y[0])
    e = ((ah * bh - p) + ah * bl + al * bh) + al * bl
    return quick(p, e + (x[0] * y[1] + x[1] * y[0]))


def df_recip(x):
    r = 1.0 / x[0]
    one = (jnp.ones_like(r), jnp.zeros_like(r))
    two = (jnp.full_like(r, 2.0), jnp.zeros_like(r))
    y = (r, jnp.zeros_like(r))
    for _ in range(1):
        y = df_mul(y, df_add(two, df_neg(df_mul(x, y))))
    return y


def solve4(nu):
    n = ITERS
    g = [[None] * n for _ in range(n)]
    for i in range(n):
        for j in range(i + 1):
            g[i][j] = df_add(nu[i + j], df_neg(nu[i + j + 1]))
    y = list(nu[:n])
    low = [[None] * n for _ in range(n)]
    inv = []
    for k in range(n):
        pivot = g[k][k]
        start = nu[2 * k][0] - nu[2 * k + 1][0]
        ok = pivot[0] > TINY * start
        safe = (jnp.where(ok, pivot[0], 1.0), jnp.where(ok, pivot[1], 0.0))
        r = df_recip(safe)
        r = (jnp.where(ok, r[0], 0.0), jnp.where(ok, r[1], 0.0))
        inv.append(r)
        for i in range(k + 1, n):
            low[i][k] = df_mul(g[i][k], r)
        for i in range(k + 1, n):
            for j in range(k + 1, i + 1):
                g[i][j] = df_add(g[i][j], df_neg(df_mul(low[i][k], g[j][k])))
            y[i] = df_add(y[i], df_neg(df_mul(low[i][k], y[k])))
    c = [None] * n
    for i in reversed(range(n)):
        v = df_mul(y[i], inv[i])
        for j in range(i + 1, n):
            v = df_add(v, df_neg(df_mul(low[j][i], c[j])))
        c[i] = v
    return [v[0] for v in c]


def lanes(shape):
    return lax.broadcasted_iota(jnp.int32, shape, len(shape) - 1)


def rows(shape):
    return lax.broadcasted_iota(jnp.int32, shape, 0)


def split(x):
    hi = x.astype(BF16)
    return hi, (x - hi.astype(F32)).astype(BF16)


def dot(a, b):
    return lax.dot_general(a, b, (((1,), (0,)), ((), ())), preferred_element_type=F32)


def kernel(
    vel, inv, fx, fy, fz,
    pst, cst, out_core,
    vx, vy, vz, ip, w0, w1, w2, w3, cx, cy, cz, dinv, pp,
    part, xrecv, xrecv0, xcoef, ysend, yrecv, yrecv0, yown, ycoef, yf, yd,
    zsend, zrecv, zsend0, zrecv0,
    zc, zf, mom, a_send, a_recv0, a_recv1,
    wz, zb, fyt, k_hi, k_lo, xh, xl, u, uk,
    za_in, za_acc, za_dir, za_out, ya_in, ya_acc, ya_dir, ya_out,
    b_src_z, b_src_y, b_in, b_acc, b_dir, b_out, ysc, v, v_recv,
    in_sem, hs_sem, hr_sem, as_sem, ar_sem, rs_sem, rr_sem, xs_sem, xr_sem,
):
    w = (w0, w1, w2, w3)
    me = [lax.axis_index(a) for a in AXES]
    has = []
    for a in range(3):
        has += [me[a] > 0, me[a] < SIZES[a] - 1]

    def neighbour(side):
        a = side // 2
        step = 1 if side % 2 else SIZES[a] - 1
        return {AXES[a]: lax.rem(me[a] + step, SIZES[a])}

    def remote(src, dst, ss, rs, dev):
        return pltpu.make_async_remote_copy(
            src_ref=src, dst_ref=dst, send_sem=ss, recv_sem=rs, device_id=dev, device_id_type=MESH
        )

    lane = lanes((8, NK))
    pending = []

    loads = [
        pltpu.make_async_copy(inv, ip.at[pl.ds(1, NI), pl.ds(TOP, NJ)], in_sem.at[0]),
        pltpu.make_async_copy(vel.at[2], vz, in_sem.at[1]),
        pltpu.make_async_copy(vel.at[1], vy.at[:, pl.ds(TOP, NJ)], in_sem.at[2]),
        pltpu.make_async_copy(vel.at[0], vx.at[pl.ds(1, NI)], in_sem.at[3]),
        pltpu.make_async_copy(inv.at[:, 0], yown.at[0], in_sem.at[4]),
        pltpu.make_async_copy(inv.at[:, NJ - 1], yown.at[1], in_sem.at[5]),
    ]
    for c in loads:
        c.start()

    barrier = pltpu.get_barrier_semaphore()
    for side in range(6):
        pl.semaphore_signal(barrier, inc=1, device_id=neighbour(side), device_id_type=MESH)

    def tiles(x):
        return [x[8 * q : 8 * q + 8] for q in range(x.shape[0] // 8)]

    def pack(acc, x, i):
        out = list(acc)
        for q, part in enumerate(x):
            moved = pltpu.roll(part, 2 * i + 1 + 64 * (q // 4), 1)
            out[q % 4] = jnp.where(lane // 2 == i + 32 * (q // 4), moved, out[q % 4])
        return out

    def unpack(faces, i):
        return [pltpu.roll(faces[q % 4], lax.rem(255 - 2 * i - 64 * (q // 4), 128), 1) for q in range(8)]

    odd_lane = lane % 2 == 1
    end_lane = (lane == 0) | (lane == NK - 1)
    sub = rows((8, NK))

    def ahead(x):
        return [jnp.where(lane == NK - 1, 0.0, pltpu.roll(a, NK - 1, 1)) for a in x]

    def behind(x):
        return [jnp.where(lane == 0, 0.0, pltpu.roll(a, 1, 1)) for a in x]

    def opposite_faces(plus, minus):
        return [
            jnp.where(odd_lane, pltpu.roll(b, 1, 1), pltpu.roll(a, NK - 1, 1))
            for a, b in zip(tiles(plus), tiles(minus))
        ]

    def at_ends(faces, i):
        return [jnp.where(end_lane, e, 0.0) for e in unpack(faces, i)]

    def add_rows(x, ref, i):
        low = jnp.where(sub == 0, ref[0, pl.ds(i, 1)], 0.0)
        high = jnp.where(sub == 7, ref[1, pl.ds(i, 1)], 0.0)
        return [x[0] + low] + x[1:7] + [x[7] + high]

    GROUP = 4
    no_faces = [jnp.zeros((8, NK), F32)] * 4
    zero_acc = jnp.zeros((8, NK), F32)

    zero_plane = jnp.zeros((NJ, NK), F32)
    zero_row = jnp.zeros((1, NK), F32)
    for ref in (vx, ip) + w:
        top = 0 if ref is vx else TOP
        for far in (0, NI + 1):
            ref[far, pl.ds(top, NJ)] = zero_plane
    for ref in (vy, ip) + w:
        for i in range(NI):
            for far in (TOP - 1, TOP + NJ):
                ref[i if ref is vy else i + 1, pl.ds(far, 1)] = zero_row
    for s in range(2):
        @pl.when(jnp.logical_not(has[s]))
        def _():
            xrecv0[s] = jnp.zeros((2, NJ, NK), F32)
            for k in range(ITERS):
                xrecv[k, s] = zero_plane

        @pl.when(jnp.logical_not(has[2 + s]))
        def _():
            yrecv0[s] = jnp.zeros((2, NI, NK), F32)
            for k in range(ITERS):
                yrecv[k, s] = jnp.zeros((NI, NK), F32)

        @pl.when(jnp.logical_not(has[4 + s]))
        def _():
            zrecv0[s] = jnp.zeros((2, 32, NK), F32)
            for k in range(ITERS):
                zrecv[k, s] = jnp.zeros((32, NK), F32)

    for c in loads[:2]:
        c.wait()

    def face0(t, carry):
        a, b = carry
        for g in range(GROUP):
            i = t * GROUP + g
            a = pack(a, tiles(vz[i]), i)
            b = pack(b, tiles(ip[i + 1, pl.ds(TOP, NJ)]), i)
        return a, b

    fu, fn = lax.fori_loop(0, NI // GROUP, face0, (no_faces, no_faces))
    zsend0[0] = jnp.concatenate(fu, axis=0)
    zsend0[1] = jnp.concatenate(fn, axis=0)
    pl.semaphore_wait(barrier, 6)

    def halo(r, side, landing):
        s, t = side % 2, landing % 2
        ax = side // 2
        if ax == 0:
            if r == 0:
                edge = (0, NI - 1)[s]
                pairs = [(vel.at[0, edge], xrecv0.at[t, 0]), (inv.at[edge], xrecv0.at[t, 1])]
            else:
                pairs = [(w[r - 1].at[(1, NI)[s], pl.ds(TOP, NJ)], xrecv.at[r - 1, t])]
        elif ax == 1:
            if r == 0:
                edge = (0, NJ - 1)[s]
                pairs = [(vel.at[1, :, edge], yrecv0.at[t, 0]), (inv.at[:, edge], yrecv0.at[t, 1])]
            else:
                pairs = [(ysend.at[r - 1, s], yrecv.at[r - 1, t])]
        elif r == 0:
            pairs = [(zsend0, zrecv0.at[t])]
        else:
            pairs = [(zsend.at[r - 1], zrecv.at[r - 1, t])]
        return [
            remote(a, b, hs_sem.at[r, side, n], hr_sem.at[r, landing, n], neighbour(side))
            for n, (a, b) in enumerate(pairs)
        ]

    def halo_start(r, sides):
        pending.append(lambda: halo_sent(r, sides))
        for side in sides:
            @pl.when(has[side])
            def _():
                for c in halo(r, side, side ^ 1):
                    c.start()

    def halo_wait(r, sides):
        for side in sides:
            @pl.when(has[side])
            def _():
                for c in halo(r, side, side):
                    c.wait_recv()

    def halo_sent(r, sides):
        for side in sides:
            @pl.when(has[side])
            def _():
                for c in halo(r, side, side ^ 1):
                    c.wait_send()

    halo_start(0, range(6))

    for c in loads[2:]:
        c.wait()

    def accumulate(acc, parts):
        while len(parts) > 1:
            parts = [parts[n] + parts[n + 1] for n in range(0, len(parts), 2)]
        s, e = two_sum(acc[0], parts[0])
        return s, acc[1] + e

    def keep_moment(m, acc):
        mom[m, 0] = acc[0]
        mom[m, 1] = acc[1]

    def mul(a, b):
        return [x * y for x, y in zip(a, b)]

    def join(x):
        return jnp.concatenate(x, axis=0)

    def join_edges(ref):
        return jnp.stack([ref[1, pl.ds(TOP, NJ)], ref[NI, pl.ds(TOP, NJ)]])

    cx[0] = zero_plane

    def inner0(t, _):
        for g in range(GROUP):
            i = t * GROUP + g
            n = ip[i + 1, pl.ds(TOP, NJ)]
            xf = ip[i + 2, pl.ds(TOP, NJ)]
            yn = ip[i + 1, pl.ds(TOP + 1, NJ)]
            nt = tiles(n)
            zn = ahead(nt)
            cx[i + 1] = 0.5 * (n + xf)
            cy[i, pl.ds(TOP, NJ)] = 0.5 * (n + yn)
            cy[i, pl.ds(TOP - 1, 1)] = zero_row
            cz[i] = join([jnp.where(lane == NK - 1, 0.0, 0.5 * (a + b)) for a, b in zip(nt, zn)])
            around = (xf + ip[i, pl.ds(TOP, NJ)]) + (yn + ip[i + 1, pl.ds(TOP - 1, NJ)])
            around = around + (join(zn) + join(behind(nt)))
            dinv[i] = (SHIFT + 3.0 * n) + 0.5 * around
            at = tiles(vz[i])
            div = (vx[i + 2] - vx[i]) + (vy[i, pl.ds(TOP + 1, NJ)] - vy[i, pl.ds(TOP - 1, NJ)])
            part[i] = div + (join(ahead(at)) - join(behind(at)))
        return 0

    lax.fori_loop(0, NI // GROUP, inner0, 0)

    halo_wait(0, range(6))

    xcoef[...] = 0.5 * (xrecv0[:, 1] + join_edges(ip))
    ycoef[...] = 0.5 * (yrecv0[:, 1] + yown[...])
    hn = opposite_faces(zrecv0[1, 1], zrecv0[0, 1])
    hu = opposite_faces(zrecv0[1, 0], zrecv0[0, 0])
    hu = [jnp.where(odd_lane, -a, a) for a in hu]
    zc[...] = join([0.5 * (a + b) for a, b in zip(hn, fn)])
    yd[...] = 0.5 * yrecv0[:, 1]
    yf[0] = -yrecv0[0, 0]
    yf[1] = yrecv0[1, 0]
    hn = [0.5 * a for a in hn]
    dinv[0] = dinv[0] + 0.5 * xrecv0[0, 1]
    dinv[NI - 1] = dinv[NI - 1] + 0.5 * xrecv0[1, 1]
    part[0] = part[0] - xrecv0[0, 0]
    part[NI - 1] = part[NI - 1] + xrecv0[1, 0]

    def first(t, carry):
        faces, acc = carry
        terms = []
        for g in range(GROUP):
            i = t * GROUP + g
            row = pl.ds(i, 1)
            d = add_rows(tiles(dinv[i]), yd, i)
            d = [a + b for a, b in zip(d, at_ends(hn, i))]
            b = add_rows(tiles(part[i]), yf, i)
            b = [-0.5 * (x + y) for x, y in zip(b, at_ends(hu, i))]
            di = [1.0 / x for x in d]
            new = mul(b, di)
            dinv[i] = join(di)
            w0[i + 1, pl.ds(TOP, NJ)] = join(new)
            ysend[0, 0, row] = new[0][0:1]
            ysend[0, 1, row] = new[7][7:8]
            faces = pack(faces, new, i)
            terms += mul(b, new)
        return faces, accumulate(acc, terms)

    faces, acc = lax.fori_loop(0, NI // GROUP, first, (no_faces, (zero_acc, zero_acc)))
    keep_moment(0, acc)

    def build_operands():
        twice = jnp.concatenate([fz[...], fz[...]], axis=0).T
        low_half = lanes((NK, 128)) < 64
        for n in range(4):
            turned = twice if n == 0 else pltpu.roll(twice, 16 * n, 1)
            top = jnp.where(low_half, turned, 0.0)
            hi, lo = split(jnp.concatenate([top, turned - top], axis=0))
            wz[n] = jnp.concatenate([hi, lo], axis=1)
        fyp = jnp.concatenate([fy[...], jnp.zeros((NJ, 64), F32)], axis=1)
        hi, lo = split(fyp.T[:64])
        fyt[...] = jnp.concatenate([hi, lo, hi], axis=1)

    def build_x_operand():
        fx_hi, fx_lo = split(fx[...])
        row = rows((512, NI))
        pair = ((row % 64) // 16 + 4 - me[2]) % 4
        plane = (row // 128) * 8 + pair * 2 + (row % 128) // 64
        rep = (plane == lanes((512, NI))).astype(F32).astype(BF16)
        same = (rows((512, 128)) % 16) == (lanes((512, 128)) % 16)

        def build_x(m, _):
            pick = (rows((64, 128)) == 8 * m + lanes((64, 128)) // 16).astype(F32).astype(BF16)
            for part_, dst in ((fx_hi, k_hi), (fx_lo, k_lo)):
                wide = dot(part_, pick).astype(BF16)
                dst[m] = jnp.where(same, dot(rep, wide), 0.0).astype(BF16)
            return 0

        lax.fori_loop(0, 8, build_x, 0)

    def keep(f, i, x, odd_plane):
        hi, lo = split(x)
        rr = pl.ds(pl.multiple_of((lax.rem(i // 2, 4) * 4 + i // 8) * NJ, NJ), NJ)
        cc = slice(NK * odd_plane, NK * odd_plane + NK)
        xh[f, rr, cc] = hi
        xl[f, rr, cc] = lo

    block = (lane % 64) // 16

    def contract_z(f, h, slot):
        zs = []
        for n in range(4):
            operand = wz[n]
            cut = slice(256 * n + 128 * h, 256 * n + 128 * h + 128)
            both = dot(xh[f, cut], operand)
            zs.append((both[:, :128] + both[:, 128:]) + dot(xl[f, cut], operand[:, :128]))
        for g in range(2):
            for e in range(2):
                pair = [z[NJ * g : NJ * g + NJ] for z in zs[2 * e : 2 * e + 2]]
                hi, lo = split(jnp.concatenate(pair, axis=1))
                zb[slot, g, e] = jnp.concatenate([hi, lo], axis=0)

    def contract_y(h, slot, dst):
        for g in range(2):
            done = []
            for e in range(2):
                both = zb[slot, g, e]
                y = dot(fyt[...], jnp.concatenate([both[:NJ], both], axis=0))
                done += [tiles(y[:, :128]), tiles(y[:, 128:])]
            for r in range(4):
                out = []
                for q in range(8):
                    acc = done[-r % 4][q]
                    for b in range(1, 4):
                        acc = jnp.where(block == b, done[(b - r) % 4][q], acc)
                    out.append(acc)
                dst[r, 2 * h + g] = join(out)

    def contract_vector(k):
        def body(t, _):
            for g in range(GROUP):
                i = t * GROUP + g
                keep(3, i, w[k][i + 1, pl.ds(TOP, NJ)], g % 2)
            return 0

        lax.fori_loop(0, NI // GROUP, body, 0)
        for h in range(2):
            contract_z(3, h, h)
        for h in range(2):
            contract_y(h, h, uk.at[k])

    for k in range(ITERS):
        zsend[k] = join(faces)
        halo_start(k + 1, range(6))
        last = k == ITERS - 1
        here = w[k]

        if k == 0:
            build_operands()
        else:
            contract_vector(k - 1)

        def inner(t, odd):
            terms = []
            for g in range(GROUP):
                i = t * GROUP + g
                c = here[i + 1, pl.ds(TOP, NJ)]
                f = cz[i]
                bw = cx[i] * here[i, pl.ds(TOP, NJ)] + cx[i + 1] * here[i + 2, pl.ds(TOP, NJ)]
                bw = bw + cy[i, pl.ds(TOP - 1, NJ)] * here[i + 1, pl.ds(TOP - 1, NJ)]
                bw = bw + cy[i, pl.ds(TOP, NJ)] * here[i + 1, pl.ds(TOP + 1, NJ)]
                nxt = join([pltpu.roll(a, NK - 1, 1) for a in tiles(c)])
                prv = join([pltpu.roll(a, 1, 1) for a in tiles(f * c)])
                bw = bw + (f * nxt + prv)
                part[i] = bw
                terms += tiles(c * bw)
            return accumulate(odd, terms)

        keep_moment(2 * k + 1, lax.fori_loop(0, NI // GROUP, inner, (zero_acc, zero_acc)))

        halo_wait(k + 1, range(6))
        flux = mul(tiles(zc[...]), opposite_faces(zrecv[k, 1], zrecv[k, 0]))
        terms = mul(flux, tiles(zsend[k]))
        zf[...] = join(flux)
        for s in range(2):
            side = ycoef[s] * yrecv[k, s]
            yf[s] = side
            terms += tiles(side * ysend[k, s])
            side = xcoef[s] * xrecv[k, s]
            edge = (0, NI - 1)[s]
            terms += tiles(side * here[edge + 1, pl.ds(TOP, NJ)])
            if not last:
                part[edge] = part[edge] + side
        while len(terms) & (len(terms) - 1):
            terms.append(zero_acc)
        keep_moment(2 * k + 1, accumulate((mom[2 * k + 1, 0], mom[2 * k + 1, 1]), terms))
        if last:
            break
        there = w[k + 1]

        def outer(t, carry):
            faces, even = carry
            terms = []
            for g in range(GROUP):
                i = t * GROUP + g
                row = pl.ds(i, 1)
                bw = add_rows(tiles(part[i]), yf, i)
                bw = [a + b for a, b in zip(bw, at_ends(tiles(zf[...]), i))]
                new = mul(bw, tiles(dinv[i]))
                there[i + 1, pl.ds(TOP, NJ)] = join(new)
                ysend[k + 1, 0, row] = new[0][0:1]
                ysend[k + 1, 1, row] = new[7][7:8]
                faces = pack(faces, new, i)
                terms += mul(bw, new)
            return faces, accumulate(even, terms)

        faces, even = lax.fori_loop(0, NI // GROUP, outer, (no_faces, (zero_acc, zero_acc)))
        keep_moment(2 * k + 2, even)

    row8 = rows((8, NK))
    lane8 = lanes((8, NK))
    hi = zero_acc
    lo = zero_acc
    for m in range(2 * ITERS):
        acc = exact_sum((mom[m, 0], mom[m, 1]))
        hi = jnp.where(row8 == m, acc[0], hi)
        lo = jnp.where(row8 == m, acc[1], lo)
    total = (hi, lo)

    plane_to = [{"gy": lax.rem(me[1] + dy, 4), "gz": lax.rem(me[2] + dz, 4)} for dy, dz in PLANE]
    line_to = [{"gx": lax.rem(me[0] + o, 8)} for o in range(1, 8)]
    for stage, (peers, landing) in enumerate(((plane_to, a_recv0), (line_to, a_recv1))):
        a_send[stage] = jnp.where(lane8 < 64, total[0], total[1])
        copies = [
            remote(a_send.at[stage], landing.at[n], as_sem.at[stage, n], ar_sem.at[stage, n], dev)
            for n, dev in enumerate(peers)
        ]
        for c in copies:
            c.start()
        if stage == 0:
            contract_vector(ITERS - 1)
        else:
            build_x_operand()
        for c in copies:
            c.wait_recv()
        terms = [total]
        for n in range(len(peers)):
            x = landing[n]
            y = pltpu.roll(x, 64, 1)
            terms.append((jnp.where(lane8 < 64, x, y), jnp.where(lane8 < 64, y, x)))
        while len(terms) > 1:
            terms = [
                df_add(terms[t], terms[t + 1]) if t + 1 < len(terms) else terms[t]
                for t in range(0, len(terms), 2)
            ]
        total = terms[0]
        pending.extend(c.wait_send for c in copies)

    nu = [(total[0][m : m + 1], total[1][m : m + 1]) for m in range(2 * ITERS)]
    coef = solve4(nu)

    def combine(parts):
        total = coef[0] * parts[0]
        for c, x in zip(coef[1:], parts[1:]):
            total = total + c * x
        return total

    def ring(axis, way):
        a = AXES.index(axis)
        n = SIZES[a]
        to = lax.rem(me[a] + (n + way), n)
        back = lax.rem(me[a] + (n - way), n)
        opposite = lax.rem(me[a] + 2, n)
        return to, back, opposite

    def rows16(m):
        return pl.ds(pl.multiple_of(m * 16, 16), 16)

    def stage_refs(f, h, stage):
        axis, way = ROUTES[f]
        slot = 0 if way == 1 else 1
        part_ = pl.ds(2 * h, 2)
        if stage == 0:
            if axis == "gz":
                return axis, way, (lambda m: u.at[f, m, part_]), za_in.at[slot, h], za_acc.at[slot, h], za_dir.at[slot, h], za_out.at[slot, h]
            return axis, way, (lambda m: u.at[f, :, part_, rows16(m)]), ya_in.at[slot, h], ya_acc.at[slot, h], ya_dir.at[slot, h], ya_out.at[slot, h]
        other = "gy" if axis == "gz" else "gz"
        if axis == "gz":
            chunk = lambda m: b_src_z.at[slot, h, :, rows16(m)]
        else:
            chunk = lambda m: b_src_y.at[slot, h, m]
        return other, way, chunk, b_in.at[f, h], b_acc.at[f, h], b_dir.at[f, h], b_out.at[f, h]

    def stage_far(f, h, stage):
        axis, way, chunk, r_in, r_acc, r_dir, r_out = stage_refs(f, h, stage)
        to, back, opposite = ring(axis, way)
        return remote(chunk(opposite), r_in, rs_sem.at[f, h, stage, 0], rr_sem.at[f, h, stage, 0], {axis: to})

    def stage_near(f, h, stage):
        axis, way, chunk, r_in, r_acc, r_dir, r_out = stage_refs(f, h, stage)
        to, back, opposite = ring(axis, way)
        return remote(chunk(back), r_dir, rs_sem.at[f, h, stage, 1], rr_sem.at[f, h, stage, 1], {axis: back})

    def stage_next(f, h, stage):
        axis, way, chunk, r_in, r_acc, r_dir, r_out = stage_refs(f, h, stage)
        to, back, opposite = ring(axis, way)
        return remote(r_out, r_acc, rs_sem.at[f, h, stage, 2], rr_sem.at[f, h, stage, 2], {axis: to})

    def stage_open(f, h, stage):
        for c in (stage_far(f, h, stage), stage_near(f, h, stage)):
            c.start()
            pending.append(c.wait_send)

    def stage_relay(f, h, stage):
        axis, way, chunk, r_in, r_acc, r_dir, r_out = stage_refs(f, h, stage)
        stage_far(f, h, stage).wait_recv()
        r_out[...] = r_in[...] + chunk(ring(axis, way)[0])[...]
        relay = stage_next(f, h, stage)
        relay.start()
        pending.append(relay.wait_send)

    def stage_close(f, h, stage):
        axis, way, chunk, r_in, r_acc, r_dir, r_out = stage_refs(f, h, stage)
        stage_near(f, h, stage).wait_recv()
        stage_next(f, h, stage).wait_recv()
        return chunk(me[AXES.index(axis)])[...] + r_acc[...] + r_dir[...]

    for h in range(2):
        for g in range(2 * h, 2 * h + 2):
            for r in range(4):
                u[3, r, g] = combine([uk[k, r, g] for k in range(ITERS)])
        stage_open(3, h, 0)

    pe = [opposite_faces(zrecv[k, 1], zrecv[k, 0]) for k in range(ITERS)]
    pe = [combine(list(parts)) for parts in zip(*pe)]
    pe = [jnp.where(odd_lane, -a, a) for a in pe]
    for s in range(2):
        pp[(0, NI + 1)[s], pl.ds(TOP, NJ)] = combine([xrecv[k, s] for k in range(ITERS)])
        yf[s] = combine([yrecv[k, s] for k in range(ITERS)])

    def press(t, _):
        for g in range(GROUP):
            i = t * GROUP + g
            pp[i + 1, pl.ds(TOP - 1, 1)] = yf[0, pl.ds(i, 1)]
            pp[i + 1, pl.ds(TOP + NJ, 1)] = yf[1, pl.ds(i, 1)]
            x = combine([ref[i + 1, pl.ds(TOP, NJ)] for ref in w])
            pp[i + 1, pl.ds(TOP, NJ)] = x
            pst[i] = x
        return 0

    lax.fori_loop(0, NI // GROUP, press, 0)

    def fix(f):
        def body(t, _):
            for g in range(GROUP):
                i = t * GROUP + g
                n = ip[i + 1, pl.ds(TOP, NJ)]
                if f == 0:
                    g_ = pp[i + 2, pl.ds(TOP, NJ)] - pp[i, pl.ds(TOP, NJ)]
                    x = vx[i + 1]
                elif f == 1:
                    g_ = pp[i + 1, pl.ds(TOP + 1, NJ)] - pp[i + 1, pl.ds(TOP - 1, NJ)]
                    x = vy[i, pl.ds(TOP, NJ)]
                else:
                    c = tiles(pp[i + 1, pl.ds(TOP, NJ)])
                    g_ = join(ahead(c)) - join(behind(c)) + join(at_ends(pe, i))
                    x = vz[i]
                x = x - n * (0.5 * g_)
                cst[f, i] = x
                keep(f, i, x, g % 2)
            return 0

        lax.fori_loop(0, NI // GROUP, body, 0)

    steps = [(f, h) for f in ORDER[1:] for h in range(2)]
    fix(ORDER[1])
    contract_z(*steps[0], 0)
    for n, (f, h) in enumerate(steps):
        if n + 1 < len(steps):
            if h == 1:
                fix(steps[n + 1][0])
            contract_z(*steps[n + 1], (n + 1) % 2)
        contract_y(h, n % 2, u.at[f])
        stage_open(f, h, 0)
    items = [(f, h) for f in ORDER for h in range(2)]
    for f, h in items:
        stage_relay(f, h, 0)
    for f, h in items:
        whole = stage_close(f, h, 0)
        slot = 0 if ROUTES[f][1] == 1 else 1
        if ROUTES[f][0] == "gz":
            b_src_z[slot, h] = whole
        else:
            b_src_y[slot, h] = whole
        stage_open(f, h, 1)
    for f, h in items:
        stage_relay(f, h, 1)
    for f, h in items:
        whole = stage_close(f, h, 1)
        for g in range(2):
            at = 128 * (2 * h + g)
            ysc[16 * f : 16 * f + 16, at : at + 128] = whole[g]

    hi, lo = split(ysc[...])
    copies = {}
    for o in (4, 3, 5, 2, 6, 1, 7, 0):
        m = lax.rem(me[0] + o, 8)
        v[m] = dot(hi, k_hi[m]) + dot(lo, k_hi[m]) + dot(hi, k_lo[m])
        if o:
            copies[o] = remote(
                v.at[m], v_recv.at[o - 1], xs_sem.at[o - 1], xr_sem.at[o - 1], line_to[o - 1]
            )
            copies[o].start()
            pending.append(copies[o].wait_send)
    total = v[me[0]]
    for o in (1, 7, 2, 6, 3, 5, 4):
        copies[o].wait_recv()
        total = total + v_recv[o - 1]
    for a in range(8):
        moved = total if a == 0 else pltpu.roll(total, 128 - 16 * a, 1)
        for f in range(4):
            out_core[a, f] = moved[16 * f : 16 * f + 16, :16]

    for wait in pending:
        wait()


def per_device(velocity, inv_density, factor_x, factor_y, factor_z):
    vmem = pl.BlockSpec(memory_space=pltpu.VMEM)
    hbm = pl.BlockSpec(memory_space=pl.ANY)
    tall = TOP + NJ + 8
    dma = pltpu.SemaphoreType.DMA
    scratch = [
        pltpu.VMEM((NI + 2, NJ, NK), F32),
        pltpu.VMEM((NI, tall, NK), F32),
        pltpu.VMEM((NI, NJ, NK), F32),
        pltpu.VMEM((NI + 2, tall, NK), F32),
        pltpu.VMEM((NI + 2, tall, NK), F32),
        pltpu.VMEM((NI + 2, tall, NK), F32),
        pltpu.VMEM((NI + 2, tall, NK), F32),
        pltpu.VMEM((NI + 2, tall, NK), F32),
        pltpu.VMEM((NI + 1, NJ, NK), F32),
        pltpu.VMEM((NI, tall, NK), F32),
        pltpu.VMEM((NI, NJ, NK), F32),
        pltpu.VMEM((NI, NJ, NK), F32),
        pltpu.VMEM((NI + 2, tall, NK), F32),
        pltpu.VMEM((NI, NJ, NK), F32),
        pltpu.VMEM((ITERS, 2, NJ, NK), F32),
        pltpu.VMEM((2, 2, NJ, NK), F32),
        pltpu.VMEM((2, NJ, NK), F32),
        pltpu.VMEM((ITERS, 2, NI, NK), F32),
        pltpu.VMEM((ITERS, 2, NI, NK), F32),
        pltpu.VMEM((2, 2, NI, NK), F32),
        pltpu.VMEM((2, NI, NK), F32),
        pltpu.VMEM((2, NI, NK), F32),
        pltpu.VMEM((2, NI, NK), F32),
        pltpu.VMEM((2, NI, NK), F32),
        pltpu.VMEM((ITERS, 32, NK), F32),
        pltpu.VMEM((ITERS, 2, 32, NK), F32),
        pltpu.VMEM((2, 32, NK), F32),
        pltpu.VMEM((2, 2, 32, NK), F32),
        pltpu.VMEM((32, NK), F32),
        pltpu.VMEM((32, NK), F32),
        pltpu.VMEM((8, 2, 8, NK), F32),
        pltpu.VMEM((2, 8, NK), F32),
        pltpu.VMEM((len(PLANE), 8, NK), F32),
        pltpu.VMEM((7, 8, NK), F32),
        pltpu.VMEM((4, 256, 256), BF16),
        pltpu.VMEM((2, 2, 2, 128, 256), BF16),
        pltpu.VMEM((64, 192), BF16),
        pltpu.VMEM((8, 512, 128), BF16),
        pltpu.VMEM((8, 512, 128), BF16),
        pltpu.VMEM((4, 1024, 256), BF16),
        pltpu.VMEM((4, 1024, 256), BF16),
        pltpu.VMEM((4, 4, 4, 64, 128), F32),
        pltpu.VMEM((ITERS, 4, 4, 64, 128), F32),
    ]
    scratch += [pltpu.VMEM((2, 2, 2, 64, 128), F32)] * 4
    scratch += [pltpu.VMEM((2, 2, 4, 2, 16, 128), F32)] * 4
    scratch += [pltpu.VMEM((2, 2, 2, 64, 128), F32), pltpu.VMEM((2, 2, 4, 2, 16, 128), F32)]
    scratch += [pltpu.VMEM((4, 2, 2, 16, 128), F32)] * 4
    scratch += [
        pltpu.VMEM((64, 512), F32),
        pltpu.VMEM((8, 64, 128), F32),
        pltpu.VMEM((7, 64, 128), F32),
        dma((6,)),
        dma((5, 6, 2)),
        dma((5, 6, 2)),
        dma((2, len(PLANE))),
        dma((2, len(PLANE))),
        dma((4, 2, 2, 3)),
        dma((4, 2, 2, 3)),
        dma((7,)),
        dma((7,)),
    ]
    pressure, corrected, core = pl.pallas_call(
        kernel,
        out_shape=(
            pltpu.VMEM(inv_density.shape, F32),
            pltpu.VMEM(velocity.shape, F32),
            pltpu.VMEM((8, 4, 16, 16), F32),
        ),
        in_specs=[hbm, hbm, vmem, vmem, vmem],
        out_specs=(vmem, vmem, vmem),
        scratch_shapes=scratch,
        compiler_params=pltpu.CompilerParams(
            collective_id=0, has_side_effects=True, vmem_limit_bytes=52 * 1024 * 1024
        ),
    )(velocity, inv_density, factor_x, factor_y, factor_z.T)
    return pressure, corrected, core


def solution(mesh):
    placed = (
        P(None, "gx", "gy", "gz"),
        P("gx", "gy", "gz"),
        P("gx", None),
        P("gy", None),
        P("gz", None),
    )
    return jax.shard_map(
        per_device,
        mesh=mesh,
        in_specs=placed,
        out_specs=(P("gx", "gy", "gz"), P(None, "gx", "gy", "gz"), P("gx", None, "gy", "gz")),
        check_vma=False,
    )
```

```python
import jax
import jax.numpy as jnp
from jax import lax
from jax.experimental import pallas as pl
from jax.experimental.pallas import tpu as pltpu
from jax.sharding import PartitionSpec as P

ITERS = 4
SHIFT = 0.1
MESH = pl.DeviceIdType.MESH
F32 = jnp.float32
BF16 = jnp.bfloat16
NI, NJ, NK = 32, 64, 128
TOP = 8
AXES = ("gx", "gy", "gz")
SIZES = (8, 4, 4)
PLANE = [(dy, dz) for dy in range(4) for dz in range(4) if dy or dz]
ROUTES = {
    (f, h): (("gz", "gy")[h], way) for f, way in ((3, 1), (1, -1), (0, 1), (2, -1)) for h in range(2)
}
ORDER = (3, 1, 0, 2)
TINY = 1e-11


def two_sum(a, b):
    s = a + b
    t = s - a
    return s, (a - (s - t)) + (b - t)


def quick(a, b):
    s = a + b
    return s, b - (s - a)


def df_add(x, y):
    s, e = two_sum(x[0], y[0])
    return quick(s, e + (x[1] + y[1]))


def exact_sum(x):
    def total(a):
        return jnp.sum(jnp.sum(a, axis=0, keepdims=True), axis=1, keepdims=True)

    big = 4.0 * total(jnp.abs(x[0]))
    coarse = (x[0] + big) - big
    return quick(total(coarse), total((x[0] - coarse) + x[1]))


def df_neg(x):
    return -x[0], -x[1]


def halves(a):
    t = 4097.0 * a
    h = t - (t - a)
    return h, a - h


def df_mul(x, y):
    p = x[0] * y[0]
    ah, al = halves(x[0])
    bh, bl = halves(y[0])
    e = ((ah * bh - p) + ah * bl + al * bh) + al * bl
    return quick(p, e + (x[0] * y[1] + x[1] * y[0]))


def df_recip(x):
    r = 1.0 / x[0]
    one = (jnp.ones_like(r), jnp.zeros_like(r))
    two = (jnp.full_like(r, 2.0), jnp.zeros_like(r))
    y = (r, jnp.zeros_like(r))
    for _ in range(1):
        y = df_mul(y, df_add(two, df_neg(df_mul(x, y))))
    return y


def solve4(nu):
    n = ITERS
    g = [[None] * n for _ in range(n)]
    for i in range(n):
        for j in range(i + 1):
            g[i][j] = df_add(nu[i + j], df_neg(nu[i + j + 1]))
    y = list(nu[:n])
    low = [[None] * n for _ in range(n)]
    inv = []
    for k in range(n):
        pivot = g[k][k]
        start = nu[2 * k][0] - nu[2 * k + 1][0]
        ok = pivot[0] > TINY * start
        safe = (jnp.where(ok, pivot[0], 1.0), jnp.where(ok, pivot[1], 0.0))
        r = df_recip(safe)
        r = (jnp.where(ok, r[0], 0.0), jnp.where(ok, r[1], 0.0))
        inv.append(r)
        for i in range(k + 1, n):
            low[i][k] = df_mul(g[i][k], r)
        for i in range(k + 1, n):
            for j in range(k + 1, i + 1):
                g[i][j] = df_add(g[i][j], df_neg(df_mul(low[i][k], g[j][k])))
            y[i] = df_add(y[i], df_neg(df_mul(low[i][k], y[k])))
    c = [None] * n
    for i in reversed(range(n)):
        v = df_mul(y[i], inv[i])
        for j in range(i + 1, n):
            v = df_add(v, df_neg(df_mul(low[j][i], c[j])))
        c[i] = v
    return [v[0] for v in c]


def lanes(shape):
    return lax.broadcasted_iota(jnp.int32, shape, len(shape) - 1)


def rows(shape):
    return lax.broadcasted_iota(jnp.int32, shape, 0)


def split(x):
    hi = x.astype(BF16)
    return hi, (x - hi.astype(F32)).astype(BF16)


def dot(a, b):
    return lax.dot_general(a, b, (((1,), (0,)), ((), ())), preferred_element_type=F32)


def kernel(
    vel, inv, fx, fy, fz,
    pst, cst, out_core,
    vx, vy, vz, ip, w0, w1, w2, w3, cx, cy, cz, dinv, pp,
    part, xrecv, xrecv0, xcoef, ysend, yrecv, yrecv0, yown, ycoef, yf, yd,
    zsend, zrecv, zsend0, zrecv0,
    zc, zf, mom, a_send, a_recv0, a_recv1,
    wz, zb, fyt, k_hi, k_lo, xh, xl, u, uk,
    za_in, za_acc, za_dir, za_out, ya_in, ya_acc, ya_dir, ya_out,
    b_src_z, b_src_y, b_in, b_acc, b_dir, b_out, ysc, v, v_recv,
    in_sem, hs_sem, hr_sem, as_sem, ar_sem, rs_sem, rr_sem, xs_sem, xr_sem,
):
    w = (w0, w1, w2, w3)
    me = [lax.axis_index(a) for a in AXES]
    has = []
    for a in range(3):
        has += [me[a] > 0, me[a] < SIZES[a] - 1]

    def neighbour(side):
        a = side // 2
        step = 1 if side % 2 else SIZES[a] - 1
        return {AXES[a]: lax.rem(me[a] + step, SIZES[a])}

    def remote(src, dst, ss, rs, dev):
        return pltpu.make_async_remote_copy(
            src_ref=src, dst_ref=dst, send_sem=ss, recv_sem=rs, device_id=dev, device_id_type=MESH
        )

    lane = lanes((8, NK))
    pending = []

    loads = [
        pltpu.make_async_copy(inv, ip.at[pl.ds(1, NI), pl.ds(TOP, NJ)], in_sem.at[0]),
        pltpu.make_async_copy(vel.at[2], vz, in_sem.at[1]),
        pltpu.make_async_copy(vel.at[1], vy.at[:, pl.ds(TOP, NJ)], in_sem.at[2]),
        pltpu.make_async_copy(vel.at[0], vx.at[pl.ds(1, NI)], in_sem.at[3]),
        pltpu.make_async_copy(inv.at[:, 0], yown.at[0], in_sem.at[4]),
        pltpu.make_async_copy(inv.at[:, NJ - 1], yown.at[1], in_sem.at[5]),
    ]
    for c in loads:
        c.start()

    barrier = pltpu.get_barrier_semaphore()
    for side in range(6):
        pl.semaphore_signal(barrier, inc=1, device_id=neighbour(side), device_id_type=MESH)

    def tiles(x):
        return [x[8 * q : 8 * q + 8] for q in range(x.shape[0] // 8)]

    def pack(acc, x, i):
        out = list(acc)
        for q, part in enumerate(x):
            moved = pltpu.roll(part, 2 * i + 1 + 64 * (q // 4), 1)
            out[q % 4] = jnp.where(lane // 2 == i + 32 * (q // 4), moved, out[q % 4])
        return out

    def unpack(faces, i):
        return [pltpu.roll(faces[q % 4], lax.rem(255 - 2 * i - 64 * (q // 4), 128), 1) for q in range(8)]

    odd_lane = lane % 2 == 1
    end_lane = (lane == 0) | (lane == NK - 1)
    sub = rows((8, NK))

    def ahead(x):
        return [jnp.where(lane == NK - 1, 0.0, pltpu.roll(a, NK - 1, 1)) for a in x]

    def behind(x):
        return [jnp.where(lane == 0, 0.0, pltpu.roll(a, 1, 1)) for a in x]

    def opposite_faces(plus, minus):
        return [
            jnp.where(odd_lane, pltpu.roll(b, 1, 1), pltpu.roll(a, NK - 1, 1))
            for a, b in zip(tiles(plus), tiles(minus))
        ]

    def at_ends(faces, i):
        return [jnp.where(end_lane, e, 0.0) for e in unpack(faces, i)]

    def add_rows(x, ref, i):
        low = jnp.where(sub == 0, ref[0, pl.ds(i, 1)], 0.0)
        high = jnp.where(sub == 7, ref[1, pl.ds(i, 1)], 0.0)
        return [x[0] + low] + x[1:7] + [x[7] + high]

    GROUP = 4
    no_faces = [jnp.zeros((8, NK), F32)] * 4
    zero_acc = jnp.zeros((8, NK), F32)

    zero_plane = jnp.zeros((NJ, NK), F32)
    zero_row = jnp.zeros((1, NK), F32)
    for ref in (vx, ip) + w:
        top = 0 if ref is vx else TOP
        for far in (0, NI + 1):
            ref[far, pl.ds(top, NJ)] = zero_plane
    for ref in (vy, ip) + w:
        for i in range(NI):
            for far in (TOP - 1, TOP + NJ):
                ref[i if ref is vy else i + 1, pl.ds(far, 1)] = zero_row
    for s in range(2):
        @pl.when(jnp.logical_not(has[s]))
        def _():
            xrecv0[s] = jnp.zeros((2, NJ, NK), F32)
            for k in range(ITERS):
                xrecv[k, s] = zero_plane

        @pl.when(jnp.logical_not(has[2 + s]))
        def _():
            yrecv0[s] = jnp.zeros((2, NI, NK), F32)
            for k in range(ITERS):
                yrecv[k, s] = jnp.zeros((NI, NK), F32)

        @pl.when(jnp.logical_not(has[4 + s]))
        def _():
            zrecv0[s] = jnp.zeros((2, 32, NK), F32)
            for k in range(ITERS):
                zrecv[k, s] = jnp.zeros((32, NK), F32)

    for c in loads[:2]:
        c.wait()

    def face0(t, carry):
        a, b = carry
        for g in range(GROUP):
            i = t * GROUP + g
            a = pack(a, tiles(vz[i]), i)
            b = pack(b, tiles(ip[i + 1, pl.ds(TOP, NJ)]), i)
        return a, b

    fu, fn = lax.fori_loop(0, NI // GROUP, face0, (no_faces, no_faces))
    zsend0[0] = jnp.concatenate(fu, axis=0)
    zsend0[1] = jnp.concatenate(fn, axis=0)
    pl.semaphore_wait(barrier, 6)

    def halo(r, side, landing):
        s, t = side % 2, landing % 2
        ax = side // 2
        if ax == 0:
            if r == 0:
                edge = (0, NI - 1)[s]
                pairs = [(vel.at[0, edge], xrecv0.at[t, 0]), (inv.at[edge], xrecv0.at[t, 1])]
            else:
                pairs = [(w[r - 1].at[(1, NI)[s], pl.ds(TOP, NJ)], xrecv.at[r - 1, t])]
        elif ax == 1:
            if r == 0:
                edge = (0, NJ - 1)[s]
                pairs = [(vel.at[1, :, edge], yrecv0.at[t, 0]), (inv.at[:, edge], yrecv0.at[t, 1])]
            else:
                pairs = [(ysend.at[r - 1, s], yrecv.at[r - 1, t])]
        elif r == 0:
            pairs = [(zsend0, zrecv0.at[t])]
        else:
            pairs = [(zsend.at[r - 1], zrecv.at[r - 1, t])]
        return [
            remote(a, b, hs_sem.at[r, side, n], hr_sem.at[r, landing, n], neighbour(side))
            for n, (a, b) in enumerate(pairs)
        ]

    def halo_start(r, sides):
        pending.append(lambda: halo_sent(r, sides))
        for side in sides:
            @pl.when(has[side])
            def _():
                for c in halo(r, side, side ^ 1):
                    c.start()

    def halo_wait(r, sides):
        for side in sides:
            @pl.when(has[side])
            def _():
                for c in halo(r, side, side):
                    c.wait_recv()

    def halo_sent(r, sides):
        for side in sides:
            @pl.when(has[side])
            def _():
                for c in halo(r, side, side ^ 1):
                    c.wait_send()

    halo_start(0, range(6))

    for c in loads[2:]:
        c.wait()

    def accumulate(acc, parts):
        while len(parts) > 1:
            parts = [parts[n] + parts[n + 1] for n in range(0, len(parts), 2)]
        s, e = two_sum(acc[0], parts[0])
        return s, acc[1] + e

    def keep_moment(m, acc):
        mom[m, 0] = acc[0]
        mom[m, 1] = acc[1]

    def mul(a, b):
        return [x * y for x, y in zip(a, b)]

    def join(x):
        return jnp.concatenate(x, axis=0)

    def join_edges(ref):
        return jnp.stack([ref[1, pl.ds(TOP, NJ)], ref[NI, pl.ds(TOP, NJ)]])

    cx[0] = zero_plane

    def inner0(t, _):
        for g in range(GROUP):
            i = t * GROUP + g
            n = ip[i + 1, pl.ds(TOP, NJ)]
            xf = ip[i + 2, pl.ds(TOP, NJ)]
            yn = ip[i + 1, pl.ds(TOP + 1, NJ)]
            nt = tiles(n)
            zn = ahead(nt)
            cx[i + 1] = 0.5 * (n + xf)
            cy[i, pl.ds(TOP, NJ)] = 0.5 * (n + yn)
            cy[i, pl.ds(TOP - 1, 1)] = zero_row
            cz[i] = join([jnp.where(lane == NK - 1, 0.0, 0.5 * (a + b)) for a, b in zip(nt, zn)])
            around = (xf + ip[i, pl.ds(TOP, NJ)]) + (yn + ip[i + 1, pl.ds(TOP - 1, NJ)])
            around = around + (join(zn) + join(behind(nt)))
            dinv[i] = (SHIFT + 3.0 * n) + 0.5 * around
            at = tiles(vz[i])
            div = (vx[i + 2] - vx[i]) + (vy[i, pl.ds(TOP + 1, NJ)] - vy[i, pl.ds(TOP - 1, NJ)])
            part[i] = div + (join(ahead(at)) - join(behind(at)))
        return 0

    lax.fori_loop(0, NI // GROUP, inner0, 0)

    halo_wait(0, range(6))

    xcoef[...] = 0.5 * (xrecv0[:, 1] + join_edges(ip))
    ycoef[...] = 0.5 * (yrecv0[:, 1] + yown[...])
    hn = opposite_faces(zrecv0[1, 1], zrecv0[0, 1])
    hu = opposite_faces(zrecv0[1, 0], zrecv0[0, 0])
    hu = [jnp.where(odd_lane, -a, a) for a in hu]
    zc[...] = join([0.5 * (a + b) for a, b in zip(hn, fn)])
    yd[...] = 0.5 * yrecv0[:, 1]
    yf[0] = -yrecv0[0, 0]
    yf[1] = yrecv0[1, 0]
    hn = [0.5 * a for a in hn]
    dinv[0] = dinv[0] + 0.5 * xrecv0[0, 1]
    dinv[NI - 1] = dinv[NI - 1] + 0.5 * xrecv0[1, 1]
    part[0] = part[0] - xrecv0[0, 0]
    part[NI - 1] = part[NI - 1] + xrecv0[1, 0]

    def first(t, carry):
        faces, acc = carry
        terms = []
        for g in range(GROUP):
            i = t * GROUP + g
            row = pl.ds(i, 1)
            d = add_rows(tiles(dinv[i]), yd, i)
            d = [a + b for a, b in zip(d, at_ends(hn, i))]
            b = add_rows(tiles(part[i]), yf, i)
            b = [-0.5 * (x + y) for x, y in zip(b, at_ends(hu, i))]
            di = [1.0 / x for x in d]
            new = mul(b, di)
            dinv[i] = join(di)
            w0[i + 1, pl.ds(TOP, NJ)] = join(new)
            ysend[0, 0, row] = new[0][0:1]
            ysend[0, 1, row] = new[7][7:8]
            faces = pack(faces, new, i)
            terms += mul(b, new)
        return faces, accumulate(acc, terms)

    faces, acc = lax.fori_loop(0, NI // GROUP, first, (no_faces, (zero_acc, zero_acc)))
    keep_moment(0, acc)

    def build_operands():
        twice = jnp.concatenate([fz[...], fz[...]], axis=0).T
        low_half = lanes((NK, 128)) < 64
        for n in range(4):
            turned = twice if n == 0 else pltpu.roll(twice, 16 * n, 1)
            top = jnp.where(low_half, turned, 0.0)
            hi, lo = split(jnp.concatenate([top, turned - top], axis=0))
            wz[n] = jnp.concatenate([hi, lo], axis=1)
        fyp = jnp.concatenate([fy[...], jnp.zeros((NJ, 64), F32)], axis=1)
        hi, lo = split(fyp.T[:64])
        fyt[...] = jnp.concatenate([hi, lo, hi], axis=1)

    def build_x_operand():
        fx_hi, fx_lo = split(fx[...])
        row = rows((512, NI))
        pair = ((row % 64) // 16 + 4 - me[2]) % 4
        plane = (row // 128) * 8 + pair * 2 + (row % 128) // 64
        rep = (plane == lanes((512, NI))).astype(F32).astype(BF16)
        same = (rows((512, 128)) % 16) == (lanes((512, 128)) % 16)

        def build_x(m, _):
            pick = (rows((64, 128)) == 8 * m + lanes((64, 128)) // 16).astype(F32).astype(BF16)
            for part_, dst in ((fx_hi, k_hi), (fx_lo, k_lo)):
                wide = dot(part_, pick).astype(BF16)
                dst[m] = jnp.where(same, dot(rep, wide), 0.0).astype(BF16)
            return 0

        lax.fori_loop(0, 8, build_x, 0)

    def keep(f, i, x, odd_plane):
        hi, lo = split(x)
        rr = pl.ds(pl.multiple_of((lax.rem(i // 2, 4) * 4 + i // 8) * NJ, NJ), NJ)
        cc = slice(NK * odd_plane, NK * odd_plane + NK)
        xh[f, rr, cc] = hi
        xl[f, rr, cc] = lo

    block = (lane % 64) // 16

    def contract_z(f, h, slot):
        zs = []
        for n in range(4):
            operand = wz[n]
            cut = slice(256 * n + 128 * h, 256 * n + 128 * h + 128)
            both = dot(xh[f, cut], operand)
            zs.append((both[:, :128] + both[:, 128:]) + dot(xl[f, cut], operand[:, :128]))
        for g in range(2):
            for e in range(2):
                pair = [z[NJ * g : NJ * g + NJ] for z in zs[2 * e : 2 * e + 2]]
                hi, lo = split(jnp.concatenate(pair, axis=1))
                zb[slot, g, e] = jnp.concatenate([hi, lo], axis=0)

    def contract_y(h, slot, dst):
        for g in range(2):
            done = []
            for e in range(2):
                both = zb[slot, g, e]
                y = dot(fyt[...], jnp.concatenate([both[:NJ], both], axis=0))
                done += [tiles(y[:, :128]), tiles(y[:, 128:])]
            for r in range(4):
                out = []
                for q in range(8):
                    acc = done[-r % 4][q]
                    for b in range(1, 4):
                        acc = jnp.where(block == b, done[(b - r) % 4][q], acc)
                    out.append(acc)
                dst[r, 2 * h + g] = join(out)

    def contract_vector(k):
        def body(t, _):
            for g in range(GROUP):
                i = t * GROUP + g
                keep(3, i, w[k][i + 1, pl.ds(TOP, NJ)], g % 2)
            return 0

        lax.fori_loop(0, NI // GROUP, body, 0)
        for h in range(2):
            contract_z(3, h, h)
        for h in range(2):
            contract_y(h, h, uk.at[k])

    for k in range(ITERS):
        zsend[k] = join(faces)
        halo_start(k + 1, range(6))
        last = k == ITERS - 1
        here = w[k]

        if k == 0:
            build_operands()
        else:
            contract_vector(k - 1)

        def inner(t, odd):
            terms = []
            for g in range(GROUP):
                i = t * GROUP + g
                c = here[i + 1, pl.ds(TOP, NJ)]
                f = cz[i]
                bw = cx[i] * here[i, pl.ds(TOP, NJ)] + cx[i + 1] * here[i + 2, pl.ds(TOP, NJ)]
                bw = bw + cy[i, pl.ds(TOP - 1, NJ)] * here[i + 1, pl.ds(TOP - 1, NJ)]
                bw = bw + cy[i, pl.ds(TOP, NJ)] * here[i + 1, pl.ds(TOP + 1, NJ)]
                nxt = join([pltpu.roll(a, NK - 1, 1) for a in tiles(c)])
                prv = join([pltpu.roll(a, 1, 1) for a in tiles(f * c)])
                bw = bw + (f * nxt + prv)
                part[i] = bw
                terms += tiles(c * bw)
            return accumulate(odd, terms)

        keep_moment(2 * k + 1, lax.fori_loop(0, NI // GROUP, inner, (zero_acc, zero_acc)))

        halo_wait(k + 1, range(6))
        flux = mul(tiles(zc[...]), opposite_faces(zrecv[k, 1], zrecv[k, 0]))
        terms = mul(flux, tiles(zsend[k]))
        zf[...] = join(flux)
        for s in range(2):
            side = ycoef[s] * yrecv[k, s]
            yf[s] = side
            terms += tiles(side * ysend[k, s])
            side = xcoef[s] * xrecv[k, s]
            edge = (0, NI - 1)[s]
            terms += tiles(side * here[edge + 1, pl.ds(TOP, NJ)])
            if not last:
                part[edge] = part[edge] + side
        while len(terms) & (len(terms) - 1):
            terms.append(zero_acc)
        keep_moment(2 * k + 1, accumulate((mom[2 * k + 1, 0], mom[2 * k + 1, 1]), terms))
        if last:
            break
        there = w[k + 1]

        def outer(t, carry):
            faces, even = carry
            terms = []
            for g in range(GROUP):
                i = t * GROUP + g
                row = pl.ds(i, 1)
                bw = add_rows(tiles(part[i]), yf, i)
                bw = [a + b for a, b in zip(bw, at_ends(tiles(zf[...]), i))]
                new = mul(bw, tiles(dinv[i]))
                there[i + 1, pl.ds(TOP, NJ)] = join(new)
                ysend[k + 1, 0, row] = new[0][0:1]
                ysend[k + 1, 1, row] = new[7][7:8]
                faces = pack(faces, new, i)
                terms += mul(bw, new)
            return faces, accumulate(even, terms)

        faces, even = lax.fori_loop(0, NI // GROUP, outer, (no_faces, (zero_acc, zero_acc)))
        keep_moment(2 * k + 2, even)

    row8 = rows((8, NK))
    lane8 = lanes((8, NK))
    hi = zero_acc
    lo = zero_acc
    for m in range(2 * ITERS):
        acc = exact_sum((mom[m, 0], mom[m, 1]))
        hi = jnp.where(row8 == m, acc[0], hi)
        lo = jnp.where(row8 == m, acc[1], lo)
    total = (hi, lo)

    plane_to = [{"gy": lax.rem(me[1] + dy, 4), "gz": lax.rem(me[2] + dz, 4)} for dy, dz in PLANE]
    line_to = [{"gx": lax.rem(me[0] + o, 8)} for o in range(1, 8)]
    for stage, (peers, landing) in enumerate(((plane_to, a_recv0), (line_to, a_recv1))):
        a_send[stage] = jnp.where(lane8 < 64, total[0], total[1])
        copies = [
            remote(a_send.at[stage], landing.at[n], as_sem.at[stage, n], ar_sem.at[stage, n], dev)
            for n, dev in enumerate(peers)
        ]
        for c in copies:
            c.start()
        if stage == 0:
            contract_vector(ITERS - 1)
        else:
            build_x_operand()
        for c in copies:
            c.wait_recv()
        terms = [total]
        for n in range(len(peers)):
            x = landing[n]
            y = pltpu.roll(x, 64, 1)
            terms.append((jnp.where(lane8 < 64, x, y), jnp.where(lane8 < 64, y, x)))
        while len(terms) > 1:
            terms = [
                df_add(terms[t], terms[t + 1]) if t + 1 < len(terms) else terms[t]
                for t in range(0, len(terms), 2)
            ]
        total = terms[0]
        pending.extend(c.wait_send for c in copies)

    nu = [(total[0][m : m + 1], total[1][m : m + 1]) for m in range(2 * ITERS)]
    coef = solve4(nu)

    def combine(parts):
        total = coef[0] * parts[0]
        for c, x in zip(coef[1:], parts[1:]):
            total = total + c * x
        return total

    def ring(axis, way):
        a = AXES.index(axis)
        n = SIZES[a]
        to = lax.rem(me[a] + (n + way), n)
        back = lax.rem(me[a] + (n - way), n)
        opposite = lax.rem(me[a] + 2, n)
        return to, back, opposite

    def rows16(m):
        return pl.ds(pl.multiple_of(m * 16, 16), 16)

    def stage_refs(f, h, stage):
        axis, way = ROUTES[f, h]
        part_ = pl.ds(2 * h, 2)
        if stage == 0:
            if axis == "gz":
                return axis, way, (lambda m: u.at[f, m, part_]), za_in.at[f], za_acc.at[f], za_dir.at[f], za_out.at[f]
            return axis, way, (lambda m: u.at[f, :, part_, rows16(m)]), ya_in.at[f], ya_acc.at[f], ya_dir.at[f], ya_out.at[f]
        other = "gy" if axis == "gz" else "gz"
        if axis == "gz":
            chunk = lambda m: b_src_z.at[f, :, rows16(m)]
        else:
            chunk = lambda m: b_src_y.at[f, m]
        return other, way, chunk, b_in.at[f, h], b_acc.at[f, h], b_dir.at[f, h], b_out.at[f, h]

    def stage_far(f, h, stage):
        axis, way, chunk, r_in, r_acc, r_dir, r_out = stage_refs(f, h, stage)
        to, back, opposite = ring(axis, way)
        return remote(chunk(opposite), r_in, rs_sem.at[f, h, stage, 0], rr_sem.at[f, h, stage, 0], {axis: to})

    def stage_near(f, h, stage):
        axis, way, chunk, r_in, r_acc, r_dir, r_out = stage_refs(f, h, stage)
        to, back, opposite = ring(axis, way)
        return remote(chunk(back), r_dir, rs_sem.at[f, h, stage, 1], rr_sem.at[f, h, stage, 1], {axis: back})

    def stage_next(f, h, stage):
        axis, way, chunk, r_in, r_acc, r_dir, r_out = stage_refs(f, h, stage)
        to, back, opposite = ring(axis, way)
        return remote(r_out, r_acc, rs_sem.at[f, h, stage, 2], rr_sem.at[f, h, stage, 2], {axis: to})

    def stage_open(f, h, stage):
        for c in (stage_far(f, h, stage), stage_near(f, h, stage)):
            c.start()
            pending.append(c.wait_send)

    def stage_relay(f, h, stage):
        axis, way, chunk, r_in, r_acc, r_dir, r_out = stage_refs(f, h, stage)
        stage_far(f, h, stage).wait_recv()
        r_out[...] = r_in[...] + chunk(ring(axis, way)[0])[...]
        relay = stage_next(f, h, stage)
        relay.start()
        pending.append(relay.wait_send)

    def stage_close(f, h, stage):
        axis, way, chunk, r_in, r_acc, r_dir, r_out = stage_refs(f, h, stage)
        stage_near(f, h, stage).wait_recv()
        stage_next(f, h, stage).wait_recv()
        return chunk(me[AXES.index(axis)])[...] + r_acc[...] + r_dir[...]

    for h in range(2):
        for g in range(2 * h, 2 * h + 2):
            for r in range(4):
                u[3, r, g] = combine([uk[k, r, g] for k in range(ITERS)])
        stage_open(3, h, 0)

    pe = [opposite_faces(zrecv[k, 1], zrecv[k, 0]) for k in range(ITERS)]
    pe = [combine(list(parts)) for parts in zip(*pe)]
    pe = [jnp.where(odd_lane, -a, a) for a in pe]
    for s in range(2):
        pp[(0, NI + 1)[s], pl.ds(TOP, NJ)] = combine([xrecv[k, s] for k in range(ITERS)])
        yf[s] = combine([yrecv[k, s] for k in range(ITERS)])

    def press(t, _):
        for g in range(GROUP):
            i = t * GROUP + g
            pp[i + 1, pl.ds(TOP - 1, 1)] = yf[0, pl.ds(i, 1)]
            pp[i + 1, pl.ds(TOP + NJ, 1)] = yf[1, pl.ds(i, 1)]
            x = combine([ref[i + 1, pl.ds(TOP, NJ)] for ref in w])
            pp[i + 1, pl.ds(TOP, NJ)] = x
            pst[i] = x
        return 0

    lax.fori_loop(0, NI // GROUP, press, 0)

    def fix(f):
        def body(t, _):
            for g in range(GROUP):
                i = t * GROUP + g
                n = ip[i + 1, pl.ds(TOP, NJ)]
                if f == 0:
                    g_ = pp[i + 2, pl.ds(TOP, NJ)] - pp[i, pl.ds(TOP, NJ)]
                    x = vx[i + 1]
                elif f == 1:
                    g_ = pp[i + 1, pl.ds(TOP + 1, NJ)] - pp[i + 1, pl.ds(TOP - 1, NJ)]
                    x = vy[i, pl.ds(TOP, NJ)]
                else:
                    c = tiles(pp[i + 1, pl.ds(TOP, NJ)])
                    g_ = join(ahead(c)) - join(behind(c)) + join(at_ends(pe, i))
                    x = vz[i]
                x = x - n * (0.5 * g_)
                cst[f, i] = x
                keep(f, i, x, g % 2)
            return 0

        lax.fori_loop(0, NI // GROUP, body, 0)

    steps = [(f, h) for f in ORDER[1:] for h in range(2)]
    fix(ORDER[1])
    contract_z(*steps[0], 0)
    for n, (f, h) in enumerate(steps):
        if n + 1 < len(steps):
            if h == 1:
                fix(steps[n + 1][0])
            contract_z(*steps[n + 1], (n + 1) % 2)
        contract_y(h, n % 2, u.at[f])
        stage_open(f, h, 0)
    items = [(f, h) for f in ORDER for h in range(2)]
    for f, h in items:
        stage_relay(f, h, 0)
    for f, h in items:
        whole = stage_close(f, h, 0)
        if ROUTES[f, h][0] == "gz":
            b_src_z[f] = whole
        else:
            b_src_y[f] = whole
        stage_open(f, h, 1)
    for f, h in items:
        stage_relay(f, h, 1)
    for f, h in items:
        whole = stage_close(f, h, 1)
        for g in range(2):
            at = 128 * (2 * h + g)
            ysc[16 * f : 16 * f + 16, at : at + 128] = whole[g]

    hi, lo = split(ysc[...])
    copies = {}
    for o in (4, 3, 5, 2, 6, 1, 7, 0):
        m = lax.rem(me[0] + o, 8)
        v[m] = dot(hi, k_hi[m]) + dot(lo, k_hi[m]) + dot(hi, k_lo[m])
        if o:
            copies[o] = remote(
                v.at[m], v_recv.at[o - 1], xs_sem.at[o - 1], xr_sem.at[o - 1], line_to[o - 1]
            )
            copies[o].start()
            pending.append(copies[o].wait_send)
    total = v[me[0]]
    for o in (1, 7, 2, 6, 3, 5, 4):
        copies[o].wait_recv()
        total = total + v_recv[o - 1]
    for a in range(8):
        moved = total if a == 0 else pltpu.roll(total, 128 - 16 * a, 1)
        for f in range(4):
            out_core[a, f] = moved[16 * f : 16 * f + 16, :16]

    for wait in pending:
        wait()


def per_device(velocity, inv_density, factor_x, factor_y, factor_z):
    vmem = pl.BlockSpec(memory_space=pltpu.VMEM)
    hbm = pl.BlockSpec(memory_space=pl.ANY)
    tall = TOP + NJ + 8
    dma = pltpu.SemaphoreType.DMA
    scratch = [
        pltpu.VMEM((NI + 2, NJ, NK), F32),
        pltpu.VMEM((NI, tall, NK), F32),
        pltpu.VMEM((NI, NJ, NK), F32),
        pltpu.VMEM((NI + 2, tall, NK), F32),
        pltpu.VMEM((NI + 2, tall, NK), F32),
        pltpu.VMEM((NI + 2, tall, NK), F32),
        pltpu.VMEM((NI + 2, tall, NK), F32),
        pltpu.VMEM((NI + 2, tall, NK), F32),
        pltpu.VMEM((NI + 1, NJ, NK), F32),
        pltpu.VMEM((NI, tall, NK), F32),
        pltpu.VMEM((NI, NJ, NK), F32),
        pltpu.VMEM((NI, NJ, NK), F32),
        pltpu.VMEM((NI + 2, tall, NK), F32),
        pltpu.VMEM((NI, NJ, NK), F32),
        pltpu.VMEM((ITERS, 2, NJ, NK), F32),
        pltpu.VMEM((2, 2, NJ, NK), F32),
        pltpu.VMEM((2, NJ, NK), F32),
        pltpu.VMEM((ITERS, 2, NI, NK), F32),
        pltpu.VMEM((ITERS, 2, NI, NK), F32),
        pltpu.VMEM((2, 2, NI, NK), F32),
        pltpu.VMEM((2, NI, NK), F32),
        pltpu.VMEM((2, NI, NK), F32),
        pltpu.VMEM((2, NI, NK), F32),
        pltpu.VMEM((2, NI, NK), F32),
        pltpu.VMEM((ITERS, 32, NK), F32),
        pltpu.VMEM((ITERS, 2, 32, NK), F32),
        pltpu.VMEM((2, 32, NK), F32),
        pltpu.VMEM((2, 2, 32, NK), F32),
        pltpu.VMEM((32, NK), F32),
        pltpu.VMEM((32, NK), F32),
        pltpu.VMEM((8, 2, 8, NK), F32),
        pltpu.VMEM((2, 8, NK), F32),
        pltpu.VMEM((len(PLANE), 8, NK), F32),
        pltpu.VMEM((7, 8, NK), F32),
        pltpu.VMEM((4, 256, 256), BF16),
        pltpu.VMEM((2, 2, 2, 128, 256), BF16),
        pltpu.VMEM((64, 192), BF16),
        pltpu.VMEM((8, 512, 128), BF16),
        pltpu.VMEM((8, 512, 128), BF16),
        pltpu.VMEM((4, 1024, 256), BF16),
        pltpu.VMEM((4, 1024, 256), BF16),
        pltpu.VMEM((4, 4, 4, 64, 128), F32),
        pltpu.VMEM((ITERS, 4, 4, 64, 128), F32),
    ]
    scratch += [pltpu.VMEM((4, 2, 64, 128), F32)] * 4
    scratch += [pltpu.VMEM((4, 4, 2, 16, 128), F32)] * 4
    scratch += [pltpu.VMEM((4, 2, 64, 128), F32), pltpu.VMEM((4, 4, 2, 16, 128), F32)]
    scratch += [pltpu.VMEM((4, 2, 2, 16, 128), F32)] * 4
    scratch += [
        pltpu.VMEM((64, 512), F32),
        pltpu.VMEM((8, 64, 128), F32),
        pltpu.VMEM((7, 64, 128), F32),
        dma((6,)),
        dma((5, 6, 2)),
        dma((5, 6, 2)),
        dma((2, len(PLANE))),
        dma((2, len(PLANE))),
        dma((4, 2, 2, 3)),
        dma((4, 2, 2, 3)),
        dma((7,)),
        dma((7,)),
    ]
    pressure, corrected, core = pl.pallas_call(
        kernel,
        out_shape=(
            pltpu.VMEM(inv_density.shape, F32),
            pltpu.VMEM(velocity.shape, F32),
            pltpu.VMEM((8, 4, 16, 16), F32),
        ),
        in_specs=[hbm, hbm, vmem, vmem, vmem],
        out_specs=(vmem, vmem, vmem),
        scratch_shapes=scratch,
        compiler_params=pltpu.CompilerParams(
            collective_id=0, has_side_effects=True, vmem_limit_bytes=52 * 1024 * 1024
        ),
    )(velocity, inv_density, factor_x, factor_y, factor_z.T)
    return pressure, corrected, core


def solution(mesh):
    placed = (
        P(None, "gx", "gy", "gz"),
        P("gx", "gy", "gz"),
        P("gx", None),
        P("gy", None),
        P("gz", None),
    )
    return jax.shard_map(
        per_device,
        mesh=mesh,
        in_specs=placed,
        out_specs=(P("gx", "gy", "gz"), P(None, "gx", "gy", "gz"), P("gx", None, "gy", "gz")),
        check_vma=False,
    )
```

```python
import jax
import jax.numpy as jnp
from jax import lax
from jax.experimental import pallas as pl
from jax.experimental.pallas import tpu as pltpu
from jax.sharding import PartitionSpec as P

ITERS = 4
SHIFT = 0.1
MESH = pl.DeviceIdType.MESH
F32 = jnp.float32
BF16 = jnp.bfloat16
NI, NJ, NK = 32, 64, 128
TOP = 8
AXES = ("gx", "gy", "gz")
SIZES = (8, 4, 4)
PLANE = [(dy, dz) for dy in range(4) for dz in range(4) if dy or dz]
ROUTES = {
    (f, h): (("gz", "gy")[h], way) for f, way in ((3, 1), (1, -1), (0, 1), (2, -1)) for h in range(2)
}
ORDER = (3, 1, 0, 2)
TINY = 1e-11


def two_sum(a, b):
    s = a + b
    t = s - a
    return s, (a - (s - t)) + (b - t)


def quick(a, b):
    s = a + b
    return s, b - (s - a)


def df_add(x, y):
    s, e = two_sum(x[0], y[0])
    return quick(s, e + (x[1] + y[1]))


def exact_sum(x):
    def total(a):
        return jnp.sum(jnp.sum(a, axis=0, keepdims=True), axis=1, keepdims=True)

    big = 4.0 * total(jnp.abs(x[0]))
    coarse = (x[0] + big) - big
    return quick(total(coarse), total((x[0] - coarse) + x[1]))


def df_neg(x):
    return -x[0], -x[1]


def halves(a):
    t = 4097.0 * a
    h = t - (t - a)
    return h, a - h


def df_mul(x, y):
    p = x[0] * y[0]
    ah, al = halves(x[0])
    bh, bl = halves(y[0])
    e = ((ah * bh - p) + ah * bl + al * bh) + al * bl
    return quick(p, e + (x[0] * y[1] + x[1] * y[0]))


def df_recip(x):
    r = 1.0 / x[0]
    one = (jnp.ones_like(r), jnp.zeros_like(r))
    two = (jnp.full_like(r, 2.0), jnp.zeros_like(r))
    y = (r, jnp.zeros_like(r))
    for _ in range(1):
        y = df_mul(y, df_add(two, df_neg(df_mul(x, y))))
    return y


def solve4(nu):
    n = ITERS
    g = [[None] * n for _ in range(n)]
    for i in range(n):
        for j in range(i + 1):
            g[i][j] = df_add(nu[i + j], df_neg(nu[i + j + 1]))
    y = list(nu[:n])
    low = [[None] * n for _ in range(n)]
    inv = []
    for k in range(n):
        pivot = g[k][k]
        start = nu[2 * k][0] - nu[2 * k + 1][0]
        ok = pivot[0] > TINY * start
        safe = (jnp.where(ok, pivot[0], 1.0), jnp.where(ok, pivot[1], 0.0))
        r = df_recip(safe)
        r = (jnp.where(ok, r[0], 0.0), jnp.where(ok, r[1], 0.0))
        inv.append(r)
        for i in range(k + 1, n):
            low[i][k] = df_mul(g[i][k], r)
        for i in range(k + 1, n):
            for j in range(k + 1, i + 1):
                g[i][j] = df_add(g[i][j], df_neg(df_mul(low[i][k], g[j][k])))
            y[i] = df_add(y[i], df_neg(df_mul(low[i][k], y[k])))
    c = [None] * n
    for i in reversed(range(n)):
        v = df_mul(y[i], inv[i])
        for j in range(i + 1, n):
            v = df_add(v, df_neg(df_mul(low[j][i], c[j])))
        c[i] = v
    return [v[0] for v in c]


def lanes(shape):
    return lax.broadcasted_iota(jnp.int32, shape, len(shape) - 1)


def rows(shape):
    return lax.broadcasted_iota(jnp.int32, shape, 0)


def split(x):
    hi = x.astype(BF16)
    return hi, (x - hi.astype(F32)).astype(BF16)


def dot(a, b):
    return lax.dot_general(a, b, (((1,), (0,)), ((), ())), preferred_element_type=F32)


def kernel(
    vel, inv, fx, fy, fz,
    pst, cst, out_core,
    vx, vy, vz, ip, w0, w1, w2, w3, cx, cy, cz, dinv, pp,
    part, xrecv, xrecv0, xcoef, ysend, yrecv, yrecv0, yown, ycoef, yf, yd,
    zsend, zrecv, zsend0, zrecv0,
    zc, zf, mom, a_send, a_recv0, a_recv1,
    wz, zb, fyt, k_hi, k_lo, xh, xl, u, uk,
    za_in, za_acc, za_dir, za_out, ya_in, ya_acc, ya_dir, ya_out,
    b_src_z, b_src_y, b_in, b_acc, b_dir, b_out, ysc, v, v_recv,
    in_sem, hs_sem, hr_sem, as_sem, ar_sem, rs_sem, rr_sem, xs_sem, xr_sem,
):
    w = (w0, w1, w2, w3)
    me = [lax.axis_index(a) for a in AXES]
    has = []
    for a in range(3):
        has += [me[a] > 0, me[a] < SIZES[a] - 1]

    def neighbour(side):
        a = side // 2
        step = 1 if side % 2 else SIZES[a] - 1
        return {AXES[a]: lax.rem(me[a] + step, SIZES[a])}

    def remote(src, dst, ss, rs, dev):
        return pltpu.make_async_remote_copy(
            src_ref=src, dst_ref=dst, send_sem=ss, recv_sem=rs, device_id=dev, device_id_type=MESH
        )

    lane = lanes((8, NK))
    pending = []

    loads = [
        pltpu.make_async_copy(inv, ip.at[pl.ds(1, NI), pl.ds(TOP, NJ)], in_sem.at[0]),
        pltpu.make_async_copy(vel.at[2], vz, in_sem.at[1]),
        pltpu.make_async_copy(vel.at[1], vy.at[:, pl.ds(TOP, NJ)], in_sem.at[2]),
        pltpu.make_async_copy(vel.at[0], vx.at[pl.ds(1, NI)], in_sem.at[3]),
        pltpu.make_async_copy(inv.at[:, 0], yown.at[0], in_sem.at[4]),
        pltpu.make_async_copy(inv.at[:, NJ - 1], yown.at[1], in_sem.at[5]),
    ]
    for c in loads:
        c.start()

    barrier = pltpu.get_barrier_semaphore()
    for side in range(6):
        pl.semaphore_signal(barrier, inc=1, device_id=neighbour(side), device_id_type=MESH)

    def tiles(x):
        return [x[8 * q : 8 * q + 8] for q in range(x.shape[0] // 8)]

    def pack(acc, x, i):
        out = list(acc)
        for q, part in enumerate(x):
            moved = pltpu.roll(part, 2 * i + 1 + 64 * (q // 4), 1)
            out[q % 4] = jnp.where(lane // 2 == i + 32 * (q // 4), moved, out[q % 4])
        return out

    def unpack(faces, i):
        return [pltpu.roll(faces[q % 4], lax.rem(255 - 2 * i - 64 * (q // 4), 128), 1) for q in range(8)]

    odd_lane = lane % 2 == 1
    end_lane = (lane == 0) | (lane == NK - 1)
    sub = rows((8, NK))

    def ahead(x):
        return [jnp.where(lane == NK - 1, 0.0, pltpu.roll(a, NK - 1, 1)) for a in x]

    def behind(x):
        return [jnp.where(lane == 0, 0.0, pltpu.roll(a, 1, 1)) for a in x]

    def opposite_faces(plus, minus):
        return [
            jnp.where(odd_lane, pltpu.roll(b, 1, 1), pltpu.roll(a, NK - 1, 1))
            for a, b in zip(tiles(plus), tiles(minus))
        ]

    def at_ends(faces, i):
        return [jnp.where(end_lane, e, 0.0) for e in unpack(faces, i)]

    def add_rows(x, ref, i):
        low = jnp.where(sub == 0, ref[0, pl.ds(i, 1)], 0.0)
        high = jnp.where(sub == 7, ref[1, pl.ds(i, 1)], 0.0)
        return [x[0] + low] + x[1:7] + [x[7] + high]

    GROUP = 4
    no_faces = [jnp.zeros((8, NK), F32)] * 4
    zero_acc = jnp.zeros((8, NK), F32)

    zero_plane = jnp.zeros((NJ, NK), F32)
    zero_row = jnp.zeros((1, NK), F32)
    for ref in (vx, ip) + w:
        top = 0 if ref is vx else TOP
        for far in (0, NI + 1):
            ref[far, pl.ds(top, NJ)] = zero_plane
    for ref in (vy, ip) + w:
        for i in range(NI):
            for far in (TOP - 1, TOP + NJ):
                ref[i if ref is vy else i + 1, pl.ds(far, 1)] = zero_row
    for s in range(2):
        @pl.when(jnp.logical_not(has[s]))
        def _():
            xrecv0[s] = jnp.zeros((2, NJ, NK), F32)
            for k in range(ITERS):
                xrecv[k, s] = zero_plane

        @pl.when(jnp.logical_not(has[2 + s]))
        def _():
            yrecv0[s] = jnp.zeros((2, NI, NK), F32)
            for k in range(ITERS):
                yrecv[k, s] = jnp.zeros((NI, NK), F32)

        @pl.when(jnp.logical_not(has[4 + s]))
        def _():
            zrecv0[s] = jnp.zeros((2, 32, NK), F32)
            for k in range(ITERS):
                zrecv[k, s] = jnp.zeros((32, NK), F32)

    for c in loads[:2]:
        c.wait()

    def face0(t, carry):
        a, b = carry
        for g in range(GROUP):
            i = t * GROUP + g
            a = pack(a, tiles(vz[i]), i)
            b = pack(b, tiles(ip[i + 1, pl.ds(TOP, NJ)]), i)
        return a, b

    fu, fn = lax.fori_loop(0, NI // GROUP, face0, (no_faces, no_faces))
    zsend0[0] = jnp.concatenate(fu, axis=0)
    zsend0[1] = jnp.concatenate(fn, axis=0)
    pl.semaphore_wait(barrier, 6)

    def halo(r, side, landing):
        s, t = side % 2, landing % 2
        ax = side // 2
        if ax == 0:
            if r == 0:
                edge = (0, NI - 1)[s]
                pairs = [(vel.at[0, edge], xrecv0.at[t, 0]), (inv.at[edge], xrecv0.at[t, 1])]
            else:
                pairs = [(w[r - 1].at[(1, NI)[s], pl.ds(TOP, NJ)], xrecv.at[r - 1, t])]
        elif ax == 1:
            if r == 0:
                edge = (0, NJ - 1)[s]
                pairs = [(vel.at[1, :, edge], yrecv0.at[t, 0]), (inv.at[:, edge], yrecv0.at[t, 1])]
            else:
                pairs = [(ysend.at[r - 1, s], yrecv.at[r - 1, t])]
        elif r == 0:
            pairs = [(zsend0, zrecv0.at[t])]
        else:
            pairs = [(zsend.at[r - 1], zrecv.at[r - 1, t])]
        return [
            remote(a, b, hs_sem.at[r, side, n], hr_sem.at[r, landing, n], neighbour(side))
            for n, (a, b) in enumerate(pairs)
        ]

    def halo_start(r, sides):
        pending.append(lambda: halo_sent(r, sides))
        for side in sides:
            @pl.when(has[side])
            def _():
                for c in halo(r, side, side ^ 1):
                    c.start()

    def halo_wait(r, sides):
        for side in sides:
            @pl.when(has[side])
            def _():
                for c in halo(r, side, side):
                    c.wait_recv()

    def halo_sent(r, sides):
        for side in sides:
            @pl.when(has[side])
            def _():
                for c in halo(r, side, side ^ 1):
                    c.wait_send()

    halo_start(0, range(6))

    for c in loads[2:]:
        c.wait()

    def accumulate(acc, parts):
        while len(parts) > 1:
            parts = [parts[n] + parts[n + 1] for n in range(0, len(parts), 2)]
        s, e = two_sum(acc[0], parts[0])
        return s, acc[1] + e

    def keep_moment(m, acc):
        mom[m, 0] = acc[0]
        mom[m, 1] = acc[1]

    def mul(a, b):
        return [x * y for x, y in zip(a, b)]

    def join(x):
        return jnp.concatenate(x, axis=0)

    def join_edges(ref):
        return jnp.stack([ref[1, pl.ds(TOP, NJ)], ref[NI, pl.ds(TOP, NJ)]])

    cx[0] = zero_plane

    def inner0(t, _):
        for g in range(GROUP):
            i = t * GROUP + g
            n = ip[i + 1, pl.ds(TOP, NJ)]
            xf = ip[i + 2, pl.ds(TOP, NJ)]
            yn = ip[i + 1, pl.ds(TOP + 1, NJ)]
            nt = tiles(n)
            zn = ahead(nt)
            cx[i + 1] = 0.5 * (n + xf)
            cy[i, pl.ds(TOP, NJ)] = 0.5 * (n + yn)
            cy[i, pl.ds(TOP - 1, 1)] = zero_row
            cz[i] = join([jnp.where(lane == NK - 1, 0.0, 0.5 * (a + b)) for a, b in zip(nt, zn)])
            around = (xf + ip[i, pl.ds(TOP, NJ)]) + (yn + ip[i + 1, pl.ds(TOP - 1, NJ)])
            around = around + (join(zn) + join(behind(nt)))
            dinv[i] = (SHIFT + 3.0 * n) + 0.5 * around
            at = tiles(vz[i])
            div = (vx[i + 2] - vx[i]) + (vy[i, pl.ds(TOP + 1, NJ)] - vy[i, pl.ds(TOP - 1, NJ)])
            part[i] = div + (join(ahead(at)) - join(behind(at)))
        return 0

    lax.fori_loop(0, NI // GROUP, inner0, 0)

    halo_wait(0, range(6))

    xcoef[...] = 0.5 * (xrecv0[:, 1] + join_edges(ip))
    ycoef[...] = 0.5 * (yrecv0[:, 1] + yown[...])
    hn = opposite_faces(zrecv0[1, 1], zrecv0[0, 1])
    hu = opposite_faces(zrecv0[1, 0], zrecv0[0, 0])
    hu = [jnp.where(odd_lane, -a, a) for a in hu]
    zc[...] = join([0.5 * (a + b) for a, b in zip(hn, fn)])
    yd[...] = 0.5 * yrecv0[:, 1]
    yf[0] = -yrecv0[0, 0]
    yf[1] = yrecv0[1, 0]
    hn = [0.5 * a for a in hn]
    dinv[0] = dinv[0] + 0.5 * xrecv0[0, 1]
    dinv[NI - 1] = dinv[NI - 1] + 0.5 * xrecv0[1, 1]
    part[0] = part[0] - xrecv0[0, 0]
    part[NI - 1] = part[NI - 1] + xrecv0[1, 0]

    def first(t, carry):
        faces, acc = carry
        terms = []
        for g in range(GROUP):
            i = t * GROUP + g
            row = pl.ds(i, 1)
            d = add_rows(tiles(dinv[i]), yd, i)
            d = [a + b for a, b in zip(d, at_ends(hn, i))]
            b = add_rows(tiles(part[i]), yf, i)
            b = [-0.5 * (x + y) for x, y in zip(b, at_ends(hu, i))]
            di = [1.0 / x for x in d]
            new = mul(b, di)
            dinv[i] = join(di)
            w0[i + 1, pl.ds(TOP, NJ)] = join(new)
            ysend[0, 0, row] = new[0][0:1]
            ysend[0, 1, row] = new[7][7:8]
            faces = pack(faces, new, i)
            terms += mul(b, new)
        return faces, accumulate(acc, terms)

    faces, acc = lax.fori_loop(0, NI // GROUP, first, (no_faces, (zero_acc, zero_acc)))
    keep_moment(0, acc)

    def build_operands():
        twice = jnp.concatenate([fz[...], fz[...]], axis=0).T
        low_half = lanes((NK, 128)) < 64
        for n in range(4):
            turned = twice if n == 0 else pltpu.roll(twice, 16 * n, 1)
            top = jnp.where(low_half, turned, 0.0)
            hi, lo = split(jnp.concatenate([top, turned - top], axis=0))
            wz[n] = jnp.concatenate([hi, lo], axis=1)
        fyp = jnp.concatenate([fy[...], jnp.zeros((NJ, 64), F32)], axis=1)
        hi, lo = split(fyp.T[:64])
        fyt[...] = jnp.concatenate([hi, lo, hi], axis=1)

    def build_x_operand():
        fx_hi, fx_lo = split(fx[...])
        row = rows((512, NI))
        pair = ((row % 64) // 16 + 4 - me[2]) % 4
        plane = (row // 128) * 8 + pair * 2 + (row % 128) // 64
        rep = (plane == lanes((512, NI))).astype(F32).astype(BF16)
        same = (rows((512, 128)) % 16) == (lanes((512, 128)) % 16)

        def build_x(m, _):
            pick = (rows((64, 128)) == 8 * m + lanes((64, 128)) // 16).astype(F32).astype(BF16)
            for part_, dst in ((fx_hi, k_hi), (fx_lo, k_lo)):
                wide = dot(part_, pick).astype(BF16)
                dst[m] = jnp.where(same, dot(rep, wide), 0.0).astype(BF16)
            return 0

        lax.fori_loop(0, 8, build_x, 0)

    def keep(f, i, x, odd_plane):
        hi, lo = split(x)
        rr = pl.ds(pl.multiple_of((lax.rem(i // 2, 4) * 4 + i // 8) * NJ, NJ), NJ)
        cc = slice(NK * odd_plane, NK * odd_plane + NK)
        xh[f, rr, cc] = hi
        xl[f, rr, cc] = lo

    block = (lane % 64) // 16

    def contract_z(f, h, slot):
        zs = []
        for n in range(4):
            operand = wz[n]
            cut = slice(256 * n + 128 * h, 256 * n + 128 * h + 128)
            both = dot(xh[f, cut], operand)
            zs.append((both[:, :128] + both[:, 128:]) + dot(xl[f, cut], operand[:, :128]))
        for g in range(2):
            for e in range(2):
                pair = [z[NJ * g : NJ * g + NJ] for z in zs[2 * e : 2 * e + 2]]
                hi, lo = split(jnp.concatenate(pair, axis=1))
                zb[slot, g, e] = jnp.concatenate([hi, lo], axis=0)

    def contract_y(h, slot, dst):
        for g in range(2):
            done = []
            for e in range(2):
                both = zb[slot, g, e]
                y = dot(fyt[...], jnp.concatenate([both[:NJ], both], axis=0))
                done += [tiles(y[:, :128]), tiles(y[:, 128:])]
            for r in range(4):
                out = []
                for q in range(8):
                    acc = done[-r % 4][q]
                    for b in range(1, 4):
                        acc = jnp.where(block == b, done[(b - r) % 4][q], acc)
                    out.append(acc)
                dst[r, 2 * h + g] = join(out)

    def contract_vector(k):
        def body(t, _):
            for g in range(GROUP):
                i = t * GROUP + g
                keep(3, i, w[k][i + 1, pl.ds(TOP, NJ)], g % 2)
            return 0

        lax.fori_loop(0, NI // GROUP, body, 0)
        for h in range(2):
            contract_z(3, h, h)
        for h in range(2):
            contract_y(h, h, uk.at[k])

    for k in range(ITERS):
        zsend[k] = join(faces)
        halo_start(k + 1, range(6))
        last = k == ITERS - 1
        here = w[k]

        if k == 0:
            build_operands()
        else:
            contract_vector(k - 1)

        def inner(t, odd):
            terms = []
            for g in range(GROUP):
                i = t * GROUP + g
                c = here[i + 1, pl.ds(TOP, NJ)]
                f = cz[i]
                bw = cx[i] * here[i, pl.ds(TOP, NJ)] + cx[i + 1] * here[i + 2, pl.ds(TOP, NJ)]
                bw = bw + cy[i, pl.ds(TOP - 1, NJ)] * here[i + 1, pl.ds(TOP - 1, NJ)]
                bw = bw + cy[i, pl.ds(TOP, NJ)] * here[i + 1, pl.ds(TOP + 1, NJ)]
                nxt = join([pltpu.roll(a, NK - 1, 1) for a in tiles(c)])
                prv = join([pltpu.roll(a, 1, 1) for a in tiles(f * c)])
                bw = bw + (f * nxt + prv)
                part[i] = bw
                terms += tiles(c * bw)
            return accumulate(odd, terms)

        keep_moment(2 * k + 1, lax.fori_loop(0, NI // GROUP, inner, (zero_acc, zero_acc)))

        halo_wait(k + 1, range(6))
        flux = mul(tiles(zc[...]), opposite_faces(zrecv[k, 1], zrecv[k, 0]))
        terms = mul(flux, tiles(zsend[k]))
        zf[...] = join(flux)
        for s in range(2):
            side = ycoef[s] * yrecv[k, s]
            yf[s] = side
            terms += tiles(side * ysend[k, s])
            side = xcoef[s] * xrecv[k, s]
            edge = (0, NI - 1)[s]
            terms += tiles(side * here[edge + 1, pl.ds(TOP, NJ)])
            if not last:
                part[edge] = part[edge] + side
        while len(terms) & (len(terms) - 1):
            terms.append(zero_acc)
        keep_moment(2 * k + 1, accumulate((mom[2 * k + 1, 0], mom[2 * k + 1, 1]), terms))
        if last:
            break
        there = w[k + 1]

        def outer(t, carry):
            faces, even = carry
            terms = []
            for g in range(GROUP):
                i = t * GROUP + g
                row = pl.ds(i, 1)
                bw = add_rows(tiles(part[i]), yf, i)
                bw = [a + b for a, b in zip(bw, at_ends(tiles(zf[...]), i))]
                new = mul(bw, tiles(dinv[i]))
                there[i + 1, pl.ds(TOP, NJ)] = join(new)
                ysend[k + 1, 0, row] = new[0][0:1]
                ysend[k + 1, 1, row] = new[7][7:8]
                faces = pack(faces, new, i)
                terms += mul(bw, new)
            return faces, accumulate(even, terms)

        faces, even = lax.fori_loop(0, NI // GROUP, outer, (no_faces, (zero_acc, zero_acc)))
        keep_moment(2 * k + 2, even)

    row8 = rows((8, NK))
    lane8 = lanes((8, NK))
    hi = zero_acc
    lo = zero_acc
    for m in range(2 * ITERS):
        acc = exact_sum((mom[m, 0], mom[m, 1]))
        hi = jnp.where(row8 == m, acc[0], hi)
        lo = jnp.where(row8 == m, acc[1], lo)
    total = (hi, lo)

    plane_to = [{"gy": lax.rem(me[1] + dy, 4), "gz": lax.rem(me[2] + dz, 4)} for dy, dz in PLANE]
    line_to = [{"gx": lax.rem(me[0] + o, 8)} for o in range(1, 8)]
    for stage, (peers, landing) in enumerate(((plane_to, a_recv0), (line_to, a_recv1))):
        a_send[stage] = jnp.where(lane8 < 64, total[0], total[1])
        copies = [
            remote(a_send.at[stage], landing.at[n], as_sem.at[stage, n], ar_sem.at[stage, n], dev)
            for n, dev in enumerate(peers)
        ]
        for c in copies:
            c.start()
        if stage == 0:
            contract_vector(ITERS - 1)
        else:
            build_x_operand()
        for c in copies:
            c.wait_recv()
        terms = [total]
        for n in range(len(peers)):
            x = landing[n]
            y = pltpu.roll(x, 64, 1)
            terms.append((jnp.where(lane8 < 64, x, y), jnp.where(lane8 < 64, y, x)))
        while len(terms) > 1:
            terms = [
                df_add(terms[t], terms[t + 1]) if t + 1 < len(terms) else terms[t]
                for t in range(0, len(terms), 2)
            ]
        total = terms[0]
        pending.extend(c.wait_send for c in copies)

    nu = [(total[0][m : m + 1], total[1][m : m + 1]) for m in range(2 * ITERS)]
    coef = solve4(nu)

    def combine(parts):
        total = coef[0] * parts[0]
        for c, x in zip(coef[1:], parts[1:]):
            total = total + c * x
        return total

    def ring(axis, way):
        a = AXES.index(axis)
        n = SIZES[a]
        to = lax.rem(me[a] + (n + way), n)
        back = lax.rem(me[a] + (n - way), n)
        opposite = lax.rem(me[a] + 2, n)
        return to, back, opposite

    def rows16(m):
        return pl.ds(pl.multiple_of(m * 16, 16), 16)

    def stage_refs(f, h, stage):
        axis, way = ROUTES[f, h]
        part_ = pl.ds(2 * h, 2)
        if stage == 0:
            if axis == "gz":
                return axis, way, (lambda m: u.at[f, m, part_]), za_in.at[f], za_acc.at[f], za_dir.at[f], za_out.at[f]
            return axis, way, (lambda m: u.at[f, :, part_, rows16(m)]), ya_in.at[f], ya_acc.at[f], ya_dir.at[f], ya_out.at[f]
        other = "gy" if axis == "gz" else "gz"
        if axis == "gz":
            chunk = lambda m: b_src_z.at[f, :, rows16(m)]
        else:
            chunk = lambda m: b_src_y.at[f, m]
        return other, way, chunk, b_in.at[f, h], b_acc.at[f, h], b_dir.at[f, h], b_out.at[f, h]

    def stage_far(f, h, stage):
        axis, way, chunk, r_in, r_acc, r_dir, r_out = stage_refs(f, h, stage)
        to, back, opposite = ring(axis, way)
        return remote(chunk(opposite), r_in, rs_sem.at[f, h, stage, 0], rr_sem.at[f, h, stage, 0], {axis: to})

    def stage_near(f, h, stage):
        axis, way, chunk, r_in, r_acc, r_dir, r_out = stage_refs(f, h, stage)
        to, back, opposite = ring(axis, way)
        return remote(chunk(back), r_dir, rs_sem.at[f, h, stage, 1], rr_sem.at[f, h, stage, 1], {axis: back})

    def stage_next(f, h, stage):
        axis, way, chunk, r_in, r_acc, r_dir, r_out = stage_refs(f, h, stage)
        to, back, opposite = ring(axis, way)
        return remote(r_out, r_acc, rs_sem.at[f, h, stage, 2], rr_sem.at[f, h, stage, 2], {axis: to})

    def stage_open(f, h, stage):
        for c in (stage_far(f, h, stage), stage_near(f, h, stage)):
            c.start()
            pending.append(c.wait_send)

    def stage_relay(f, h, stage):
        axis, way, chunk, r_in, r_acc, r_dir, r_out = stage_refs(f, h, stage)
        stage_far(f, h, stage).wait_recv()
        r_out[...] = r_in[...] + chunk(ring(axis, way)[0])[...]
        relay = stage_next(f, h, stage)
        relay.start()
        pending.append(relay.wait_send)

    def stage_close(f, h, stage):
        axis, way, chunk, r_in, r_acc, r_dir, r_out = stage_refs(f, h, stage)
        stage_near(f, h, stage).wait_recv()
        stage_next(f, h, stage).wait_recv()
        return chunk(me[AXES.index(axis)])[...] + r_acc[...] + r_dir[...]

    for h in range(2):
        for g in range(2 * h, 2 * h + 2):
            for r in range(4):
                u[3, r, g] = combine([uk[k, r, g] for k in range(ITERS)])
        stage_open(3, h, 0)

    pe = [opposite_faces(zrecv[k, 1], zrecv[k, 0]) for k in range(ITERS)]
    pe = [combine(list(parts)) for parts in zip(*pe)]
    pe = [jnp.where(odd_lane, -a, a) for a in pe]
    for s in range(2):
        pp[(0, NI + 1)[s], pl.ds(TOP, NJ)] = combine([xrecv[k, s] for k in range(ITERS)])
        yf[s] = combine([yrecv[k, s] for k in range(ITERS)])

    def press(t, _):
        for g in range(GROUP):
            i = t * GROUP + g
            pp[i + 1, pl.ds(TOP - 1, 1)] = yf[0, pl.ds(i, 1)]
            pp[i + 1, pl.ds(TOP + NJ, 1)] = yf[1, pl.ds(i, 1)]
            x = combine([ref[i + 1, pl.ds(TOP, NJ)] for ref in w])
            pp[i + 1, pl.ds(TOP, NJ)] = x
            pst[i] = x
        return 0

    lax.fori_loop(0, NI // GROUP, press, 0)

    def fix(f):
        def body(t, _):
            for g in range(GROUP):
                i = t * GROUP + g
                n = ip[i + 1, pl.ds(TOP, NJ)]
                if f == 0:
                    g_ = pp[i + 2, pl.ds(TOP, NJ)] - pp[i, pl.ds(TOP, NJ)]
                    x = vx[i + 1]
                elif f == 1:
                    g_ = pp[i + 1, pl.ds(TOP + 1, NJ)] - pp[i + 1, pl.ds(TOP - 1, NJ)]
                    x = vy[i, pl.ds(TOP, NJ)]
                else:
                    c = tiles(pp[i + 1, pl.ds(TOP, NJ)])
                    g_ = join(ahead(c)) - join(behind(c)) + join(at_ends(pe, i))
                    x = vz[i]
                x = x - n * (0.5 * g_)
                cst[f, i] = x
                keep(f, i, x, g % 2)
            return 0

        lax.fori_loop(0, NI // GROUP, body, 0)

    steps = [(f, h) for f in ORDER[1:] for h in range(2)]
    fix(ORDER[1])
    contract_z(*steps[0], 0)
    for n, (f, h) in enumerate(steps):
        if n + 1 < len(steps):
            if h == 1:
                fix(steps[n + 1][0])
            contract_z(*steps[n + 1], (n + 1) % 2)
        contract_y(h, n % 2, u.at[f])
        stage_open(f, h, 0)
        if n == 4:
            for early in range(2):
                stage_relay(ORDER[0], early, 0)
    items = [(f, h) for f in ORDER for h in range(2)]
    for f, h in steps:
        stage_relay(f, h, 0)
    for f, h in items:
        whole = stage_close(f, h, 0)
        if ROUTES[f, h][0] == "gz":
            b_src_z[f] = whole
        else:
            b_src_y[f] = whole
        stage_open(f, h, 1)
    for f, h in items:
        stage_relay(f, h, 1)
    for f, h in items:
        whole = stage_close(f, h, 1)
        for g in range(2):
            at = 128 * (2 * h + g)
            ysc[16 * f : 16 * f + 16, at : at + 128] = whole[g]

    hi, lo = split(ysc[...])
    copies = {}
    for o in (4, 3, 5, 2, 6, 1, 7, 0):
        m = lax.rem(me[0] + o, 8)
        v[m] = dot(hi, k_hi[m]) + dot(lo, k_hi[m]) + dot(hi, k_lo[m])
        if o:
            copies[o] = remote(
                v.at[m], v_recv.at[o - 1], xs_sem.at[o - 1], xr_sem.at[o - 1], line_to[o - 1]
            )
            copies[o].start()
            pending.append(copies[o].wait_send)
    total = v[me[0]]
    for o in (1, 7, 2, 6, 3, 5, 4):
        copies[o].wait_recv()
        total = total + v_recv[o - 1]
    for a in range(8):
        moved = total if a == 0 else pltpu.roll(total, 128 - 16 * a, 1)
        for f in range(4):
            out_core[a, f] = moved[16 * f : 16 * f + 16, :16]

    for wait in pending:
        wait()


def per_device(velocity, inv_density, factor_x, factor_y, factor_z):
    vmem = pl.BlockSpec(memory_space=pltpu.VMEM)
    hbm = pl.BlockSpec(memory_space=pl.ANY)
    tall = TOP + NJ + 8
    dma = pltpu.SemaphoreType.DMA
    scratch = [
        pltpu.VMEM((NI + 2, NJ, NK), F32),
        pltpu.VMEM((NI, tall, NK), F32),
        pltpu.VMEM((NI, NJ, NK), F32),
        pltpu.VMEM((NI + 2, tall, NK), F32),
        pltpu.VMEM((NI + 2, tall, NK), F32),
        pltpu.VMEM((NI + 2, tall, NK), F32),
        pltpu.VMEM((NI + 2, tall, NK), F32),
        pltpu.VMEM((NI + 2, tall, NK), F32),
        pltpu.VMEM((NI + 1, NJ, NK), F32),
        pltpu.VMEM((NI, tall, NK), F32),
        pltpu.VMEM((NI, NJ, NK), F32),
        pltpu.VMEM((NI, NJ, NK), F32),
        pltpu.VMEM((NI + 2, tall, NK), F32),
        pltpu.VMEM((NI, NJ, NK), F32),
        pltpu.VMEM((ITERS, 2, NJ, NK), F32),
        pltpu.VMEM((2, 2, NJ, NK), F32),
        pltpu.VMEM((2, NJ, NK), F32),
        pltpu.VMEM((ITERS, 2, NI, NK), F32),
        pltpu.VMEM((ITERS, 2, NI, NK), F32),
        pltpu.VMEM((2, 2, NI, NK), F32),
        pltpu.VMEM((2, NI, NK), F32),
        pltpu.VMEM((2, NI, NK), F32),
        pltpu.VMEM((2, NI, NK), F32),
        pltpu.VMEM((2, NI, NK), F32),
        pltpu.VMEM((ITERS, 32, NK), F32),
        pltpu.VMEM((ITERS, 2, 32, NK), F32),
        pltpu.VMEM((2, 32, NK), F32),
        pltpu.VMEM((2, 2, 32, NK), F32),
        pltpu.VMEM((32, NK), F32),
        pltpu.VMEM((32, NK), F32),
        pltpu.VMEM((8, 2, 8, NK), F32),
        pltpu.VMEM((2, 8, NK), F32),
        pltpu.VMEM((len(PLANE), 8, NK), F32),
        pltpu.VMEM((7, 8, NK), F32),
        pltpu.VMEM((4, 256, 256), BF16),
        pltpu.VMEM((2, 2, 2, 128, 256), BF16),
        pltpu.VMEM((64, 192), BF16),
        pltpu.VMEM((8, 512, 128), BF16),
        pltpu.VMEM((8, 512, 128), BF16),
        pltpu.VMEM((4, 1024, 256), BF16),
        pltpu.VMEM((4, 1024, 256), BF16),
        pltpu.VMEM((4, 4, 4, 64, 128), F32),
        pltpu.VMEM((ITERS, 4, 4, 64, 128), F32),
    ]
    scratch += [pltpu.VMEM((4, 2, 64, 128), F32)] * 4
    scratch += [pltpu.VMEM((4, 4, 2, 16, 128), F32)] * 4
    scratch += [pltpu.VMEM((4, 2, 64, 128), F32), pltpu.VMEM((4, 4, 2, 16, 128), F32)]
    scratch += [pltpu.VMEM((4, 2, 2, 16, 128), F32)] * 4
    scratch += [
        pltpu.VMEM((64, 512), F32),
        pltpu.VMEM((8, 64, 128), F32),
        pltpu.VMEM((7, 64, 128), F32),
        dma((6,)),
        dma((5, 6, 2)),
        dma((5, 6, 2)),
        dma((2, len(PLANE))),
        dma((2, len(PLANE))),
        dma((4, 2, 2, 3)),
        dma((4, 2, 2, 3)),
        dma((7,)),
        dma((7,)),
    ]
    pressure, corrected, core = pl.pallas_call(
        kernel,
        out_shape=(
            pltpu.VMEM(inv_density.shape, F32),
            pltpu.VMEM(velocity.shape, F32),
            pltpu.VMEM((8, 4, 16, 16), F32),
        ),
        in_specs=[hbm, hbm, vmem, vmem, vmem],
        out_specs=(vmem, vmem, vmem),
        scratch_shapes=scratch,
        compiler_params=pltpu.CompilerParams(
            collective_id=0, has_side_effects=True, vmem_limit_bytes=52 * 1024 * 1024
        ),
    )(velocity, inv_density, factor_x, factor_y, factor_z.T)
    return pressure, corrected, core


def solution(mesh):
    placed = (
        P(None, "gx", "gy", "gz"),
        P("gx", "gy", "gz"),
        P("gx", None),
        P("gy", None),
        P("gz", None),
    )
    return jax.shard_map(
        per_device,
        mesh=mesh,
        in_specs=placed,
        out_specs=(P("gx", "gy", "gz"), P(None, "gx", "gy", "gz"), P("gx", None, "gy", "gz")),
        check_vma=False,
    )
```
